256 devices in a mesh: tp: 8 (over x, core), ad: 32 (over y, z).
Axes of the slice: x: 4, y: 4, z: 8, core: 2. Of those that a mesh axis runs over, the one named last changes fastest.
Arguments:
- hidden: bfloat16 [14336, 8192], P('ad'), may hold values from -6 to 6
- gain: bfloat16 [8192], replicated, may hold values from 0.25 to 1.75
- key_value_weight: bfloat16 [8192, 2, 1024], P(None, None, 'tp'), may hold values from -0.0625 to 0.0625
- adapter_down_weight: bfloat16 [64, 8192, 128], P('ad', 'tp'), may hold values from -0.0625 to 0.0625
- adapter_up_weight: bfloat16 [64, 2, 64, 1024], P('ad', None, None, 'tp'), may hold values from -0.75 to 0.75
- language_pair_index: int32 [14336], P('ad'), may hold values from 0 to 63, as said below
- adapter_row_index: int32 [64], replicated, may hold values from 0 to 63, as said below
Outputs:
- kv_out: bfloat16 [14336, 2, 1024], P('ad', None, 'tp')
The draws below stay inside these ranges and needn't reach their ends.
Inputs may be any that keep to these rules, and one draw needn't show every extreme that they name: A row's owner is adapter_row_index[language_pair_index] // 2. Among the rows of one device, one owner, the same for every device, has exactly 56 rows; every other owner has at most 28, and one other owner, the same for every device, exactly 28. `adapter_row_index`: each adapter's row in adapter_down_weight and adapter_up_weight; every row appears once.
All inputs are finite; a program needn't handle non-finite values.
Results may differ from the reference program's by a relative error of at most 0.0053.
Values may be sent and summed in bfloat16 or wider, within the bound.
No kernel may reach another device: no remote copies, remote signals or barrier semaphores. Data moves between devices by JAX's collectives and lax.ppermute only.
A program may use at most 128 MiB of HBM per device.

```python
import jax
import jax.numpy as jnp
from jax import lax

MODEL_DIM = 8192
KEY_VALUE_WIDTH = 1024
ADAPTER_RANK = 64
ADAPT_DEV = 2
TOK_DEV = 448
ADAPTER_COUNT = 64
ROWS = 14336
CAP_ALL = 56
CAP_REST = 28
N_AD = 32


def plan_tables(key):
    slot_of = jax.random.permutation(jax.random.fold_in(key, 11), ADAPTER_COUNT).astype(jnp.int32)
    adapter_at = jnp.argsort(slot_of, stable=True).astype(jnp.int32)
    hot_owner = jax.random.randint(jax.random.fold_in(key, 12), (), 0, N_AD, dtype=jnp.int32)
    step_up = jax.random.randint(jax.random.fold_in(key, 13), (), 1, N_AD, dtype=jnp.int32)
    second = (hot_owner + step_up) % N_AD
    rank_of = jax.random.permutation(jax.random.fold_in(key, 14), N_AD).astype(jnp.int32)
    weight_of = 1 + 7 * rank_of // (N_AD - 1)
    cand_count = N_AD * CAP_REST

    def one_block(block_index):
        block_key = jax.random.fold_in(key, 1000 + block_index)
        candidates = jnp.repeat(jnp.arange(N_AD, dtype=jnp.int32), CAP_REST)
        usable = (candidates != hot_owner) & (candidates != second)
        positions = jnp.arange(cand_count, dtype=jnp.int32)
        random_draw = jax.random.randint(jax.random.fold_in(block_key, 1), (cand_count,), 0, 4096, dtype=jnp.int32)
        scores = random_draw * weight_of[candidates] * cand_count + positions
        scores = jnp.where(usable, scores, -1 - positions)
        picked = lax.top_k(scores, TOK_DEV - CAP_ALL - CAP_REST)[1]
        owners = jnp.concatenate([jnp.full((CAP_ALL,), hot_owner, jnp.int32), jnp.full((CAP_REST,), second, jnp.int32), candidates[picked]])
        within = jax.random.randint(jax.random.fold_in(block_key, 2), (TOK_DEV,), 0, ADAPT_DEV, dtype=jnp.int32)
        block_pairs = adapter_at[owners * ADAPT_DEV + within]
        shuffle = jax.random.permutation(jax.random.fold_in(block_key, 3), TOK_DEV)
        return block_pairs[shuffle]
    all_pairs = jax.vmap(one_block)(jnp.arange(N_AD, dtype=jnp.int32)).reshape(ROWS).astype(jnp.int32)
    return (slot_of, all_pairs)


def draw_language_pair_index(key, part):
    return plan_tables(key)[1]


def draw_adapter_row_index(key, part):
    return plan_tables(key)[0]


def block_scale(key, extent, pieces, low, top_value):
    level = 1.0
    for position, shards_of in pieces:
        draws = jax.random.uniform(jax.random.fold_in(jax.random.fold_in(key, 6), position), (shards_of,), jnp.float32, low / len(pieces), top_value / len(pieces))
        level = level * jnp.repeat(jnp.exp(draws), extent[position] // shards_of).reshape((-1,) + (1,) * (len(extent) - 1 - position))
    return level


def gaussian(stream_key, shape, scale, most, pieces=(), kind=jnp.bfloat16):
    entries = jax.random.normal(stream_key, shape, jnp.float32) * scale
    if len(pieces) > 0:
        entries = block_scale(stream_key, shape, pieces, -0.22, 0.18) * entries
    return jnp.clip(entries, min=-most, max=most).astype(kind)


def setup_inputs(seed: int = 0) -> dict:
    key_of = jax.random.split(jax.random.key(seed), 8)
    return {
        "hidden": gaussian(key_of[0], (ROWS, MODEL_DIM), 1.0, 6.0, ((0, 32),)),
        "gain": jnp.clip(1.0 + 0.15 * jax.random.normal(key_of[1], (MODEL_DIM,), jnp.float32), 0.25, 1.75).astype(jnp.bfloat16),
        "key_value_weight": gaussian(key_of[2], (MODEL_DIM, 2, KEY_VALUE_WIDTH), MODEL_DIM ** -0.5, 0.0625, ((2, 8),)),
        "adapter_down_weight": gaussian(key_of[3], (ADAPTER_COUNT, MODEL_DIM, 2 * ADAPTER_RANK), MODEL_DIM ** -0.5, 0.0625, ((0, 32), (1, 8))),
        "adapter_up_weight": gaussian(key_of[4], (ADAPTER_COUNT, 2, ADAPTER_RANK, KEY_VALUE_WIDTH), ADAPTER_RANK ** -0.5, 0.75, ((0, 32), (3, 8))),
        "language_pair_index": draw_language_pair_index(jax.random.fold_in(key_of[7], 71), 0),
        "adapter_row_index": draw_adapter_row_index(jax.random.fold_in(key_of[7], 71), 0),
    }


epsilon = 1e-05
adapter_scale = 0.5

def reference(hidden, gain, key_value_weight, adapter_down_weight, adapter_up_weight, language_pair_index, adapter_row_index):
    wide_hidden = hidden.astype(jnp.float32)
    inv_rms = lax.rsqrt(lax.optimization_barrier(jnp.mean(wide_hidden * wide_hidden, axis=-1, keepdims=True)) + epsilon)
    normed = (wide_hidden * inv_rms * gain.astype(jnp.float32)).astype(jnp.bfloat16)
    base_projection = jnp.dot(normed, key_value_weight.reshape(MODEL_DIM, 2 * KEY_VALUE_WIDTH), preferred_element_type=jnp.float32).reshape(ROWS, 2, KEY_VALUE_WIDTH)
    slot_ids = adapter_row_index[language_pair_index].astype(jnp.int32)
    sorting_order = jnp.argsort(slot_ids, stable=True).astype(jnp.int32)
    sorted_slots = slot_ids[sorting_order]
    labels = jnp.arange(ADAPTER_COUNT, dtype=jnp.int32)
    counts = lax.optimization_barrier(jnp.sum((sorted_slots[None, :] == labels[:, None]).astype(jnp.int32), axis=1))
    starts = (jnp.cumsum(counts) - counts).astype(jnp.int32)
    longest = CAP_ALL * N_AD
    padded = jnp.concatenate([normed[sorting_order], jnp.zeros((longest, MODEL_DIM), jnp.bfloat16)], 0)
    padded_slots = jnp.concatenate([sorted_slots, jnp.full((longest,), -1, jnp.int32)], 0)

    def add_adapter(adapter_entry, totals):
        adapter_entry = jnp.asarray(adapter_entry).astype(jnp.int32)
        begin_row = starts[adapter_entry].astype(jnp.int32)
        block_row_count = lax.dynamic_slice_in_dim(padded, begin_row, longest, 0)
        block_slots = lax.dynamic_slice_in_dim(padded_slots, begin_row, longest, 0)
        reduced_rank_state = jnp.dot(block_row_count, adapter_down_weight[adapter_entry], preferred_element_type=jnp.float32).astype(jnp.bfloat16)
        key_portion = jnp.dot(reduced_rank_state[:, :ADAPTER_RANK], adapter_up_weight[adapter_entry, 0], preferred_element_type=jnp.float32)
        value_portion = jnp.dot(reduced_rank_state[:, ADAPTER_RANK:], adapter_up_weight[adapter_entry, 1], preferred_element_type=jnp.float32)
        narrow = jnp.stack([key_portion, value_portion], 1).astype(jnp.bfloat16)
        narrow = lax.optimization_barrier(narrow)
        delta_block = narrow.astype(jnp.float32)
        keep_mask = (block_slots == adapter_entry)[:, None, None]
        current = lax.dynamic_slice_in_dim(totals, begin_row, longest, 0)
        update = current + jnp.where(keep_mask, delta_block, jnp.float32(0.0))
        return lax.dynamic_update_slice_in_dim(totals, update, begin_row, 0)
    totals = lax.fori_loop(0, ADAPTER_COUNT, add_adapter, jnp.zeros((ROWS + longest, 2, KEY_VALUE_WIDTH), jnp.float32))
    delta_sorted = totals[:ROWS]
    delta_complete = jnp.zeros_like(delta_sorted).at[sorting_order].set(delta_sorted)
    return (base_projection + adapter_scale * delta_complete).astype(jnp.bfloat16)
```

```python
import functools

import jax
import jax.numpy as jnp
from jax import lax
from jax.experimental import pallas as pl
from jax.experimental.pallas import tpu as pltpu
from jax.sharding import Mesh, PartitionSpec as P


epsilon = 1e-05
adapter_scale = 0.5
F32 = jnp.float32
BF16 = jnp.bfloat16

TOK = 448
DIM = 8192
COLS = 1024
CAP = 28
BLOCK = 32
NZ = 8
NY = 4
BUCKETS = NZ + 1
SLOTS = BUCKETS * BLOCK
RANK2 = 128
CHUNK = COLS + RANK2
ROW_TILE = 64


def iota(shape, axis):
    return lax.broadcasted_iota(jnp.int32, shape, axis).astype(F32)


def to_column(row, count):
    same = iota((count, count), 0) == iota((count, count), 1)
    return jnp.sum(jnp.where(same, row, 0.0), axis=1, keepdims=True)


def dispatch_kernel(
    place_ref, hidden_ref, gain_ref, pair_ref, table_ref, inv_ref, send_ref, dst_ref, hot_ref, own_ref
):
    step = pl.program_id(0)
    col0 = pl.multiple_of(place_ref[0] * COLS, COLS)
    wide = hidden_ref[...].astype(F32)
    mean = jnp.sum(wide * wide, axis=1, keepdims=True) * (1.0 / DIM)
    inv = lax.rsqrt(mean + epsilon)
    inv_ref[...] = jnp.broadcast_to(inv, (ROW_TILE, 128))
    mine = hidden_ref[:, pl.ds(col0, COLS)].astype(F32)
    gain = gain_ref[:, pl.ds(col0, COLS)].astype(F32)
    row0 = pl.multiple_of(step * ROW_TILE, ROW_TILE)
    own_ref[pl.ds(row0, ROW_TILE), :] = (mine * inv * gain).astype(BF16)

    @pl.when(step == pl.num_programs(0) - 1)
    def _():
        y_me = place_ref[1].astype(F32)
        z_me = place_ref[2].astype(F32)
        count = table_ref.shape[1]
        pair = pair_ref[...].astype(F32)
        table = to_column(table_ref[...].astype(F32), count)
        slot = jnp.sum(jnp.where(iota((count, TOK), 0) == pair, table, 0.0), axis=0, keepdims=True)
        owner = jnp.floor(slot * 0.5)
        local = slot - 2.0 * owner
        owner_col = to_column(owner, TOK)
        same = owner_col == owner
        first = iota((TOK, TOK), 0)
        second = iota((TOK, TOK), 1)
        pos = jnp.sum(jnp.where(same & (first < second), 1.0, 0.0), axis=0, keepdims=True)
        y_to = jnp.floor(owner * (1.0 / NZ))
        dy = y_to - y_me
        dy = jnp.where(dy < 0, dy + NY, dy)
        dz = owner - NZ * y_to - z_me
        dz = jnp.where(dz < 0, dz + NZ, dz)
        over = pos >= CAP
        bucket = dy * BUCKETS + jnp.where(over, float(NZ), dz)
        place = jnp.where(over, pos - CAP, pos)
        dst = bucket * BLOCK + place
        dst_ref[...] = jnp.broadcast_to(to_column(dst, TOK), (TOK, 128))
        hot_ref[0] = jnp.max(jnp.where(over, dz, -1.0)).astype(jnp.int32)
        place_col = to_column(place, TOK)
        spot = jnp.where(iota((TOK, 128), 1) == place_col, 1.0, 0.0).astype(BF16)
        for part in range(NY):
            pick = jnp.where(iota((SLOTS, TOK), 0) + part * SLOTS == dst, 1.0, 0.0).astype(BF16)
            rows = jnp.dot(pick, own_ref[...], preferred_element_type=F32).astype(BF16)
            send_ref[part] = rows.reshape(BUCKETS, BLOCK, COLS)
            marks = jnp.where(iota((16, TOK), 0) + part * BUCKETS == bucket, local, 0.0).astype(BF16)
            ids = jnp.dot(marks, spot, preferred_element_type=F32)
            for b in range(BUCKETS):
                head = rows[b * BLOCK : (b + 1) * BLOCK, :128].astype(F32)
                head = jnp.where(iota((BLOCK, 128), 0) == CAP, ids[b : b + 1], head)
                send_ref[part, b, :, pl.ds(0, 128)] = head.astype(BF16)


def dispatch(place, hidden, gain, pair, table):
    steps = TOK // ROW_TILE
    return pl.pallas_call(
        dispatch_kernel,
        grid=(steps,),
        in_specs=[
            pl.BlockSpec(memory_space=pltpu.SMEM),
            pl.BlockSpec((ROW_TILE, DIM), lambda i: (i, 0)),
            pl.BlockSpec((1, DIM), lambda i: (0, 0)),
            pl.BlockSpec((1, TOK), lambda i: (0, 0)),
            pl.BlockSpec((1, table.shape[1]), lambda i: (0, 0)),
        ],
        out_specs=[
            pl.BlockSpec((ROW_TILE, 128), lambda i: (i, 0)),
            pl.BlockSpec((NY, BUCKETS, BLOCK, COLS), lambda i: (0, 0, 0, 0)),
            pl.BlockSpec((TOK, 128), lambda i: (0, 0)),
            pl.BlockSpec(memory_space=pltpu.SMEM),
        ],
        out_shape=[
            jax.ShapeDtypeStruct((TOK, 128), F32),
            jax.ShapeDtypeStruct((NY, BUCKETS, BLOCK, COLS), BF16),
            jax.ShapeDtypeStruct((TOK, 128), F32),
            jax.ShapeDtypeStruct((1,), jnp.int32),
        ],
        scratch_shapes=[pltpu.VMEM((TOK, COLS), BF16)],
        cost_estimate=pl.CostEstimate(
            flops=2 * NY * SLOTS * TOK * COLS, bytes_accessed=10_000_000, transcendentals=0
        ),
        name="dispatch",
    )(place, hidden, gain, pair, table)


def base_kernel(hidden_ref, inv_ref, gain_ref, weight_ref, out_ref):
    step = pl.program_id(0)
    wide = hidden_ref[...].astype(F32)
    inv = inv_ref[:, :1]
    normed = (wide * inv * gain_ref[...].astype(F32)).astype(BF16)
    weight = jnp.concatenate([weight_ref[0], weight_ref[1]], axis=1)
    term = jnp.dot(normed, weight, preferred_element_type=F32)

    @pl.when(step == 0)
    def _():
        out_ref[...] = term

    @pl.when(step > 0)
    def _():
        out_ref[...] += term


def base_projection(hidden, inv, gain, weight):
    tile = 1024
    return pl.pallas_call(
        base_kernel,
        grid=(DIM // tile,),
        in_specs=[
            pl.BlockSpec((TOK, tile), lambda k: (0, k)),
            pl.BlockSpec((TOK, 128), lambda k: (0, 0)),
            pl.BlockSpec((1, tile), lambda k: (0, k)),
            pl.BlockSpec((2, tile, 128), lambda k: (0, k, 0)),
        ],
        out_specs=pl.BlockSpec((TOK, 256), lambda k: (0, 0)),
        out_shape=jax.ShapeDtypeStruct((TOK, 256), F32),
        cost_estimate=pl.CostEstimate(
            flops=2 * TOK * DIM * 256, bytes_accessed=12_000_000, transcendentals=0
        ),
        name="base",
    )(hidden, inv, gain, weight)


def local_column(head):
    row = head[CAP : CAP + 1, :].astype(F32)
    same = iota((BLOCK, 128), 0) == iota((BLOCK, 128), 1)
    return jnp.sum(jnp.where(same, row, 0.0), axis=1, keepdims=True)


def down_kernel(offsets, parts, hot_ref, *refs):
    n = len(offsets)
    extra = jnp.concatenate([refs[s][0] for s in range(NY)], axis=0)
    extra_local = jnp.concatenate([local_column(refs[s][0, :, :128]) for s in range(NY)], axis=0)
    refs = refs[NY:]
    low_ref, more_ref = refs[-2:]
    more = jnp.zeros((NY * BLOCK, RANK2), F32)
    for k in range(n):
        rows_refs = refs[k * NY : (k + 1) * NY]
        rows = jnp.concatenate([r[0] for r in rows_refs], axis=0)
        local = jnp.concatenate([local_column(r[0, :, :128]) for r in rows_refs], axis=0)
        w = refs[n * NY + k * parts : n * NY + (k + 1) * parts]
        if parts == 1:
            weight = jnp.concatenate([w[0][0], w[0][1]], axis=1)
        else:
            weight = jnp.concatenate([w[0][0], w[1][0]], axis=1)
        both = jnp.dot(
            jnp.concatenate([rows, extra], axis=0), weight, preferred_element_type=F32
        )
        chosen = jnp.concatenate([local, extra_local], axis=0)
        part = jnp.where(chosen < 0.5, both[:, :RANK2], both[:, RANK2:])
        low_ref[k] = part[: NY * BLOCK].astype(BF16)
        here = hot_ref[0] == offsets[k]
        more = more + jnp.where(here, part[NY * BLOCK :], 0.0)
    more_ref[...] = more.astype(BF16)


def down(offsets, hot, received, chunks):
    n = len(offsets)
    parts = len(chunks[0])
    in_specs = [pl.BlockSpec(memory_space=pltpu.SMEM)]
    args = [hot]
    for s in range(NY):
        in_specs.append(pl.BlockSpec((1, BLOCK, COLS), lambda i: (NZ, 0, 0)))
        args.append(received[s])
    for dz in offsets:
        for s in range(NY):
            in_specs.append(pl.BlockSpec((1, BLOCK, COLS), lambda i, dz=dz: (dz, 0, 0)))
            args.append(received[s])
    for arrays in chunks:
        for a in arrays:
            in_specs.append(pl.BlockSpec((a.shape[0], COLS, 128), lambda i: (0, 0, 0)))
            args.append(a)
    return pl.pallas_call(
        functools.partial(down_kernel, offsets, parts),
        grid=(1,),
        in_specs=in_specs,
        out_specs=[
            pl.BlockSpec((n, NY * BLOCK, RANK2), lambda i: (0, 0, 0)),
            pl.BlockSpec((NY * BLOCK, RANK2), lambda i: (0, 0)),
        ],
        out_shape=[
            jax.ShapeDtypeStruct((n, NY * BLOCK, RANK2), BF16),
            jax.ShapeDtypeStruct((NY * BLOCK, RANK2), BF16),
        ],
        cost_estimate=pl.CostEstimate(
            flops=2 * n * 256 * 1024 * 256, bytes_accessed=n * 800_000, transcendentals=0
        ),
        name="down",
    )(*args)


def up_kernel(hot_ref, low_ref, *refs):
    heads = refs[:NY]
    out_ref = refs[-1]
    ups = refs[NY:-1]
    extra_low = low_ref[NZ].astype(F32)
    extra_local = jnp.concatenate([local_column(h[NZ]) for h in heads], axis=0)
    more = jnp.zeros((NY * BLOCK, 256), F32)
    at = 0
    for dz in range(NZ):
        if dz == 4:
            up = jnp.concatenate([ups[at][0], ups[at + 1][0]], axis=0)
            at += 2
        else:
            up = ups[at][...].reshape(2 * RANK2, 128)
            at += 1
        up = up.astype(F32)
        half = (lax.broadcasted_iota(jnp.int32, (2 * RANK2, 128), 0) % RANK2) < RANK2 // 2
        rhs = jnp.concatenate([jnp.where(half, up, 0.0), jnp.where(half, 0.0, up)], axis=1).astype(BF16)
        local = jnp.concatenate([local_column(h[dz]) for h in heads], axis=0)
        low = jnp.concatenate([low_ref[dz].astype(F32), extra_low], axis=0)
        chosen = jnp.concatenate([local, extra_local], axis=0)
        lhs = jnp.concatenate(
            [jnp.where(chosen < 0.5, low, 0.0), jnp.where(chosen < 0.5, 0.0, low)], axis=1
        ).astype(BF16)
        delta = jnp.dot(lhs, rhs, preferred_element_type=F32)
        out_ref[:, dz] = delta[: NY * BLOCK].astype(BF16).reshape(NY, BLOCK, 256)
        more = more + jnp.where(hot_ref[0] == dz, delta[NY * BLOCK :], 0.0)
    out_ref[:, NZ] = more.astype(BF16).reshape(NY, BLOCK, 256)


def upward(hot, low, received, chunks):
    in_specs = [
        pl.BlockSpec(memory_space=pltpu.SMEM),
        pl.BlockSpec((BUCKETS, NY * BLOCK, RANK2), lambda i: (0, 0, 0)),
    ]
    args = [hot, low]
    for s in range(NY):
        in_specs.append(pl.BlockSpec((BUCKETS, BLOCK, 128), lambda i: (0, 0, 0)))
        args.append(received[s])
    for arrays in chunks:
        for a in arrays:
            in_specs.append(pl.BlockSpec((a.shape[0], RANK2, 128), lambda i: (0, COLS // RANK2, 0)))
            args.append(a)
    return pl.pallas_call(
        up_kernel,
        grid=(1,),
        in_specs=in_specs,
        out_specs=pl.BlockSpec((NY, BUCKETS, BLOCK, 256), lambda i: (0, 0, 0, 0)),
        out_shape=jax.ShapeDtypeStruct((NY, BUCKETS, BLOCK, 256), BF16),
        cost_estimate=pl.CostEstimate(
            flops=2 * NZ * 256 * 256 * 256, bytes_accessed=1_500_000, transcendentals=0
        ),
        name="upward",
    )(*args)


def finish_kernel(base_ref, dst_ref, *refs):
    out_ref = refs[-1]
    dst = dst_ref[:, :1]
    total = jnp.zeros((TOK, 256), F32)
    for part in range(NY):
        pick = jnp.where(iota((TOK, SLOTS), 1) + part * SLOTS == dst, 1.0, 0.0).astype(BF16)
        total = total + jnp.dot(
            pick, refs[part][...].reshape(SLOTS, 256), preferred_element_type=F32
        )
    out_ref[...] = (base_ref[...] + adapter_scale * total).astype(BF16)


def finish(base, dst, back):
    return pl.pallas_call(
        finish_kernel,
        out_shape=jax.ShapeDtypeStruct((TOK, 256), BF16),
        cost_estimate=pl.CostEstimate(
            flops=2 * TOK * NY * SLOTS * 256, bytes_accessed=2_000_000, transcendentals=0
        ),
        name="finish",
    )(base, dst, *back)


def shift(x, axis, size, by):
    return lax.ppermute(x, axis, [(i, (i + by) % size) for i in range(size)])


def on_device(hidden, gain, kv_weight, down_weight, up_weight, pair_index, row_index):
    tp = lax.axis_index("x") * 2 + lax.axis_index("core")
    core = lax.axis_index("core")
    place = jnp.stack([tp, lax.axis_index("y"), lax.axis_index("z")]).astype(jnp.int32)

    own = jnp.concatenate([down_weight, up_weight.reshape(2, RANK2, 128)], axis=1)
    chunks = {0: [own]}
    plus = minus = own
    for k in range(1, 4):
        plus = shift(plus, "z", NZ, 1)
        minus = shift(minus, "z", NZ, -1)
        chunks[NZ - k] = [plus]
        chunks[k] = [minus]
    chunks[4] = [shift(plus[:1], "z", NZ, 1), shift(minus[1:], "z", NZ, -1)]

    gain_row = gain.reshape(1, DIM)
    inv, send, dst, hot = dispatch(
        place, hidden, gain_row, pair_index.reshape(1, TOK), row_index.reshape(1, -1)
    )
    received = [send[0]] + [shift(send[dy], "y", NY, dy) for dy in range(1, NY)]

    base = base_projection(hidden, inv, gain_row, kv_weight.transpose(1, 0, 2))

    low = [None] * NZ
    more = 0.0
    for offsets in ((0,), (7, 1), (6, 2), (5, 3), (4,)):
        out, extra = down(offsets, hot, received, [chunks[dz] for dz in offsets])
        for k, dz in enumerate(offsets):
            low[dz] = out[k]
        more = more + extra.astype(F32)
    partial = jnp.stack(low + [more.astype(BF16)])

    flat = partial.reshape(2, BUCKETS * NY * BLOCK // 2, RANK2)
    mine = lax.dynamic_index_in_dim(flat, core, 0, keepdims=False)
    other = lax.dynamic_index_in_dim(flat, 1 - core, 0, keepdims=False)
    chip = (mine.astype(F32) + shift(other, "core", 2, 1).astype(F32)).astype(BF16)
    total = chip.astype(F32)
    for k in range(1, 4):
        total = total + shift(chip, "x", 4, k).astype(F32)
    half = total.astype(BF16)
    theirs = shift(half, "core", 2, 1)
    full = jnp.concatenate(
        [jnp.where(core == 0, half, theirs), jnp.where(core == 0, theirs, half)], axis=0
    ).reshape(BUCKETS, NY * BLOCK, RANK2)

    delta = upward(hot, full, received, [chunks[dz] for dz in range(NZ)])
    back = [delta[0]] + [shift(delta[dy], "y", NY, -dy) for dy in range(1, NY)]
    return finish(base, dst, back).reshape(TOK, 2, 128)


def solution(mesh):
    split = Mesh(mesh.devices.reshape(4, 2, NY, NZ), ("x", "core", "y", "z"))
    tp = ("x", "core")
    ad = ("y", "z")
    return jax.shard_map(
        on_device,
        mesh=split,
        in_specs=(
            P(ad, None),
            P(),
            P(None, None, tp),
            P(ad, tp, None),
            P(ad, None, None, tp),
            P(ad),
            P(),
        ),
        out_specs=P(ad, None, tp),
        check_vma=False,
    )
```

```python
import jax
import jax.numpy as jnp
from jax import lax
from jax.experimental import pallas as pl
from jax.experimental.pallas import tpu as pltpu
from jax.sharding import Mesh, PartitionSpec as P


epsilon = 1e-05
adapter_scale = 0.5
F32 = jnp.float32
BF16 = jnp.bfloat16

TOK = 448
DIM = 8192
COLS = 1024
CAP = 28
BLOCK = 32
NZ = 8
NY = 4
BUCKETS = NZ + 1
SLOTS = BUCKETS * BLOCK
EARLY = 7
LATE = BUCKETS - EARLY
ORDER = (0, 7, 1, 6, 2, 5, 3, 4)
RANK2 = 128
VMEM_LIMIT = 24 * 1024 * 1024


def iota(shape, axis):
    return lax.broadcasted_iota(jnp.int32, shape, axis).astype(F32)


def to_column(row, count):
    same = iota((count, count), 0) == iota((count, count), 1)
    return jnp.sum(jnp.where(same, row, 0.0), axis=1, keepdims=True)


def params():
    return pltpu.CompilerParams(vmem_limit_bytes=VMEM_LIMIT)


def whole():
    return pl.BlockSpec(memory_space=pltpu.VMEM)


def scalars():
    return pl.BlockSpec(memory_space=pltpu.SMEM)


def gain_row(gain):
    wide = gain.astype(F32)
    return jnp.concatenate([wide[i : i + 1] for i in range(8)], axis=1)


def dispatch_kernel(place_ref, hidden_ref, gain_ref, pair_ref, table_ref, *outs):
    sends = outs[:NY]
    dst_ref, hot_ref = outs[NY:]
    own = (hidden_ref[...].astype(F32) * gain_row(gain_ref[...])).astype(BF16)
    y_me = place_ref[1].astype(F32)
    z_me = place_ref[2].astype(F32)
    count = table_ref.shape[1]
    pair = pair_ref[...].astype(F32)
    table = to_column(table_ref[...].astype(F32), count)
    slot = jnp.sum(jnp.where(iota((count, TOK), 0) == pair, table, 0.0), axis=0, keepdims=True)
    owner = jnp.floor(slot * 0.5)
    local = slot - 2.0 * owner
    same = to_column(owner, TOK) == owner
    before = iota((TOK, TOK), 0) < iota((TOK, TOK), 1)
    pos = jnp.sum(jnp.where(same & before, 1.0, 0.0), axis=0, keepdims=True)
    y_to = jnp.floor(owner * (1.0 / NZ))
    dy = y_to - y_me
    dy = jnp.where(dy < 0, dy + NY, dy)
    dz = owner - NZ * y_to - z_me
    dz = jnp.where(dz < 0, dz + NZ, dz)
    rank = jnp.where(dz == 4, 7.0, jnp.where(dz < 4, 2.0 * dz, 15.0 - 2.0 * dz))
    over = pos >= CAP
    bucket = dy * BUCKETS + jnp.where(over, float(NZ), rank)
    place = jnp.where(over, pos - CAP, pos)
    dst = bucket * BLOCK + place
    dst_ref[...] = jnp.broadcast_to(to_column(dst, TOK), (TOK, 128))
    hot_ref[0] = jnp.max(jnp.where(over, rank, -1.0)).astype(jnp.int32)
    spot = jnp.where(iota((TOK, 128), 1) == to_column(place, TOK), 1.0, 0.0).astype(BF16)
    for part in range(NY):
        pick = jnp.where(iota((SLOTS, TOK), 0) + part * SLOTS == dst, 1.0, 0.0).astype(BF16)
        rows = jnp.dot(pick, own, preferred_element_type=F32).astype(BF16)
        sends[part][...] = rows.reshape(BUCKETS, BLOCK, COLS)
        marks = jnp.where(iota((16, TOK), 0) + part * BUCKETS == bucket, local, 0.0).astype(BF16)
        ids = jnp.dot(marks, spot, preferred_element_type=F32)
        for b in range(BUCKETS):
            head = rows[b * BLOCK : (b + 1) * BLOCK, :128].astype(F32)
            head = jnp.where(iota((BLOCK, 128), 0) == CAP, ids[b : b + 1], head)
            sends[part][b, :, pl.ds(0, 128)] = head.astype(BF16)


def dispatch(place, hidden, gain, pair, table):
    message = jax.ShapeDtypeStruct((BUCKETS, BLOCK, COLS), BF16)
    out = pl.pallas_call(
        dispatch_kernel,
        grid_spec=pltpu.PrefetchScalarGridSpec(
            num_scalar_prefetch=1,
            grid=(1,),
            in_specs=[
                pl.BlockSpec((TOK, COLS), lambda i, p: (0, p[0])),
                pl.BlockSpec((8, 128), lambda i, p: (p[0], 0)),
                pl.BlockSpec((1, TOK), lambda i, p: (0, 0)),
                pl.BlockSpec((1, table.shape[1]), lambda i, p: (0, 0)),
            ],
            out_specs=[pl.BlockSpec((BUCKETS, BLOCK, COLS), lambda i, p: (0, 0, 0))] * NY
            + [pl.BlockSpec((TOK, 128), lambda i, p: (0, 0)), scalars()],
        ),
        out_shape=[message] * NY
        + [jax.ShapeDtypeStruct((TOK, 128), F32), jax.ShapeDtypeStruct((1,), jnp.int32)],
        cost_estimate=pl.CostEstimate(
            flops=2 * NY * SLOTS * TOK * COLS, bytes_accessed=4_000_000, transcendentals=0
        ),
        name="dispatch",
    )(place, hidden, gain, pair, table)
    return out[:NY], out[NY], out[NY + 1]


def base_kernel(hidden_ref, gain_ref, weight_ref, out_ref, inv_ref, square_ref):
    step = pl.program_id(0)
    wide = hidden_ref[...].astype(F32)
    scaled = (wide * gain_row(gain_ref[...])).astype(BF16)
    weight = jnp.concatenate([weight_ref[0], weight_ref[1]], axis=1)
    term = jnp.dot(scaled, weight, preferred_element_type=F32)
    lanes = sum(
        wide[:, c : c + 128] * wide[:, c : c + 128] for c in range(0, wide.shape[1], 128)
    )

    @pl.when(step == 0)
    def _():
        out_ref[...] = term
        square_ref[...] = lanes

    @pl.when(step > 0)
    def _():
        out_ref[...] += term
        square_ref[...] += lanes

    @pl.when(step == pl.num_programs(0) - 1)
    def _():
        mean = jnp.sum(square_ref[...], axis=1, keepdims=True) * (1.0 / DIM)
        inv = lax.rsqrt(mean + epsilon)
        out_ref[...] = out_ref[...] * inv
        inv_ref[...] = jnp.broadcast_to(inv, (TOK, 128))


def base_projection(hidden, gain, weight):
    tile = 1024
    return pl.pallas_call(
        base_kernel,
        grid=(DIM // tile,),
        in_specs=[
            pl.BlockSpec((TOK, tile), lambda k: (0, k)),
            pl.BlockSpec((8, 128), lambda k: (k, 0)),
            pl.BlockSpec((2, tile, 128), lambda k: (0, k, 0)),
        ],
        out_specs=[
            pl.BlockSpec((TOK, 256), lambda k: (0, 0)),
            pl.BlockSpec((TOK, 128), lambda k: (0, 0)),
        ],
        out_shape=[
            jax.ShapeDtypeStruct((TOK, 256), F32),
            jax.ShapeDtypeStruct((TOK, 128), F32),
        ],
        scratch_shapes=[pltpu.VMEM((TOK, 128), F32)],
        cost_estimate=pl.CostEstimate(
            flops=2 * TOK * DIM * 256, bytes_accessed=12_000_000, transcendentals=0
        ),
        name="base",
    )(hidden, gain, weight)


def local_column(head):
    row = head[CAP : CAP + 1, :].astype(F32)
    same = iota((BLOCK, 128), 0) == iota((BLOCK, 128), 1)
    return jnp.sum(jnp.where(same, row, 0.0), axis=1, keepdims=True)


def bucket_rows(received, b):
    rows = jnp.concatenate([r[b] for r in received], axis=0)
    local = jnp.concatenate([local_column(r[b, :, :128]) for r in received], axis=0)
    return rows, local


def project(rows, local, weight):
    both = jnp.dot(rows, weight, preferred_element_type=F32)
    return jnp.where(local < 0.5, both[:, :RANK2], both[:, RANK2:])


def down_early_kernel(place_ref, hot_ref, *refs):
    received = refs[:NY]
    chunks = refs[NY : NY + EARLY]
    mine_ref, other_ref, more_ref, low_ref = refs[NY + EARLY :]
    more_ref[...] = jnp.zeros_like(more_ref)
    for k in range(EARLY):
        c = chunks[k]
        weight = jnp.concatenate([c[0, :COLS], c[1, :COLS]], axis=1)
        rows, local = bucket_rows(received, k)
        low_ref[k * NY * BLOCK : (k + 1) * NY * BLOCK] = project(rows, local, weight).astype(BF16)

        @pl.when(hot_ref[0] == k)
        def _():
            rows, local = bucket_rows(received, NZ)
            more_ref[...] = project(rows, local, weight).astype(BF16)

    size = EARLY * NY * BLOCK // 2
    first = pl.multiple_of(place_ref[3] * size, size)
    second = pl.multiple_of(size - place_ref[3] * size, size)
    mine_ref[...] = low_ref[pl.ds(first, size), :]
    other_ref[...] = low_ref[pl.ds(second, size), :]


def down_early(place, hot, received, chunks):
    size = EARLY * NY * BLOCK // 2
    return pl.pallas_call(
        down_early_kernel,
        in_specs=[scalars(), scalars()] + [whole()] * (NY + EARLY),
        out_specs=[whole()] * 3,
        out_shape=[
            jax.ShapeDtypeStruct((size, RANK2), BF16),
            jax.ShapeDtypeStruct((size, RANK2), BF16),
            jax.ShapeDtypeStruct((NY * BLOCK, RANK2), BF16),
        ],
        scratch_shapes=[pltpu.VMEM((2 * size, RANK2), BF16)],
        compiler_params=params(),
        cost_estimate=pl.CostEstimate(
            flops=2 * EARLY * 128 * 1024 * 256, bytes_accessed=6_000_000, transcendentals=0
        ),
        name="down_early",
    )(place, hot, *received, *chunks)


def down_late_kernel(hot_ref, *refs):
    received = refs[:NY]
    zero, one, more_ref, low_ref = refs[NY:]
    weight = jnp.concatenate([zero[0, :COLS], one[0, :COLS]], axis=1)
    rows, local = bucket_rows(received, EARLY)
    low_ref[0] = project(rows, local, weight).astype(BF16)
    low_ref[1] = more_ref[...]

    @pl.when(hot_ref[0] == EARLY)
    def _():
        rows, local = bucket_rows(received, NZ)
        low_ref[1] = project(rows, local, weight).astype(BF16)


def down_late(hot, received, chunks, more):
    return pl.pallas_call(
        down_late_kernel,
        in_specs=[scalars()] + [whole()] * (NY + 3),
        out_specs=whole(),
        out_shape=jax.ShapeDtypeStruct((LATE, NY * BLOCK, RANK2), BF16),
        compiler_params=params(),
        cost_estimate=pl.CostEstimate(
            flops=2 * 256 * 1024 * 256, bytes_accessed=1_000_000, transcendentals=0
        ),
        name="down_late",
    )(hot, *received, *chunks, more)


def spread(low, local):
    zero = jnp.zeros_like(low)
    return jnp.concatenate(
        [jnp.where(local < 0.5, low, zero), jnp.where(local < 0.5, zero, low)], axis=1
    ).astype(BF16)


def up_matrix(up):
    key_row = (lax.broadcasted_iota(jnp.int32, (2 * RANK2, 128), 0) % RANK2) < RANK2 // 2
    up = up.astype(F32)
    return jnp.concatenate(
        [jnp.where(key_row, up, 0.0), jnp.where(key_row, 0.0, up)], axis=1
    ).astype(BF16)


def up_rows(chunk):
    return jnp.concatenate([chunk[0, COLS:], chunk[1, COLS:]], axis=0)


def up_early_kernel(place_ref, half_ref, theirs_ref, *refs):
    received = refs[:NY]
    chunks = refs[NY : NY + EARLY]
    outs = refs[NY + EARLY : -1]
    low_ref = refs[-1]
    size = EARLY * NY * BLOCK // 2
    first = pl.multiple_of(place_ref[3] * size, size)
    second = pl.multiple_of(size - place_ref[3] * size, size)
    low_ref[pl.ds(first, size), :] = half_ref[...]
    low_ref[pl.ds(second, size), :] = theirs_ref[...]
    for k in range(EARLY):
        local = jnp.concatenate([local_column(r[k, :, :128]) for r in received], axis=0)
        low = low_ref[k * NY * BLOCK : (k + 1) * NY * BLOCK, :].astype(F32)
        delta = jnp.dot(
            spread(low, local), up_matrix(up_rows(chunks[k])), preferred_element_type=F32
        ).astype(BF16)
        for s in range(NY):
            outs[s][k] = delta[s * BLOCK : (s + 1) * BLOCK]


def up_early(place, half, theirs, received, chunks):
    return pl.pallas_call(
        up_early_kernel,
        in_specs=[scalars()] + [whole()] * (2 + NY + EARLY),
        out_specs=[whole()] * NY,
        out_shape=[jax.ShapeDtypeStruct((EARLY, BLOCK, 256), BF16)] * NY,
        scratch_shapes=[pltpu.VMEM((EARLY * NY * BLOCK, RANK2), BF16)],
        compiler_params=params(),
        cost_estimate=pl.CostEstimate(
            flops=2 * EARLY * 128 * 256 * 256, bytes_accessed=1_500_000, transcendentals=0
        ),
        name="up_early",
    )(place, half, theirs, *received, *chunks)


def up_late_kernel(hot_ref, low_ref, *refs):
    received = refs[:NY]
    chunks = refs[NY : NY + EARLY]
    zero, one = refs[NY + EARLY : NY + EARLY + 2]
    outs = refs[NY + EARLY + 2 :]
    last = jnp.concatenate([zero[0, COLS:], one[0, COLS:]], axis=0)
    hot_up = last.astype(F32)
    for k in range(EARLY):
        hot_up = jnp.where(hot_ref[0] == k, up_rows(chunks[k]).astype(F32), hot_up)
    for at, up in ((0, last), (1, hot_up)):
        local = jnp.concatenate([local_column(r[EARLY + at, :, :128]) for r in received], axis=0)
        delta = jnp.dot(
            spread(low_ref[at].astype(F32), local), up_matrix(up), preferred_element_type=F32
        ).astype(BF16)
        for s in range(NY):
            outs[s][at] = delta[s * BLOCK : (s + 1) * BLOCK]


def up_late(hot, low, received, chunks, last):
    return pl.pallas_call(
        up_late_kernel,
        in_specs=[scalars()] + [whole()] * (1 + NY + EARLY + 2),
        out_specs=[whole()] * NY,
        out_shape=[jax.ShapeDtypeStruct((LATE, BLOCK, 256), BF16)] * NY,
        compiler_params=params(),
        cost_estimate=pl.CostEstimate(
            flops=2 * 2 * 128 * 256 * 256, bytes_accessed=1_000_000, transcendentals=0
        ),
        name="up_late",
    )(hot, low, *received, *chunks, *last)


def collect(dst, first, count, back):
    total = jnp.zeros((TOK, 256), F32)
    for part in range(NY):
        size = count * BLOCK
        at = iota((TOK, size), 1) + (part * SLOTS + first * BLOCK)
        pick = jnp.where(at == dst, 1.0, 0.0).astype(BF16)
        total = total + jnp.dot(
            pick, back[part][...].reshape(size, 256), preferred_element_type=F32
        )
    return total


def finish_early_kernel(base_ref, inv_ref, dst_ref, *refs):
    total = collect(dst_ref[:, :1], 0, EARLY, refs[:NY])
    refs[NY][...] = base_ref[...] + (adapter_scale * inv_ref[:, :1]) * total


def finish_late_kernel(sum_ref, inv_ref, dst_ref, *refs):
    total = collect(dst_ref[:, :1], EARLY, LATE, refs[:NY])
    refs[NY][...] = (sum_ref[...] + (adapter_scale * inv_ref[:, :1]) * total).astype(BF16)


def finish(kernel, start, inv, dst, back, kind):
    return pl.pallas_call(
        kernel,
        in_specs=[whole()] * (3 + NY),
        out_specs=whole(),
        out_shape=jax.ShapeDtypeStruct((TOK, 256), kind),
        compiler_params=params(),
        cost_estimate=pl.CostEstimate(
            flops=2 * TOK * 1024 * 256, bytes_accessed=1_500_000, transcendentals=0
        ),
    )(start, inv, dst, *back)


def shift(x, axis, size, by):
    return lax.ppermute(x, axis, [(i, (i + by) % size) for i in range(size)])


def on_device(hidden, gain, kv_weight, down_weight, up_weight, pair_index, row_index):
    tp = lax.axis_index("x") * 2 + lax.axis_index("core")
    places = [tp, lax.axis_index("y"), lax.axis_index("z"), lax.axis_index("core")]
    place = jnp.stack(places).astype(jnp.int32)

    own = jnp.concatenate([down_weight, up_weight.reshape(2, RANK2, 128)], axis=1)
    chunks = {0: own}
    plus = minus = own
    for k in range(1, 4):
        plus = shift(plus, "z", NZ, 1)
        minus = shift(minus, "z", NZ, -1)
        chunks[NZ - k] = plus
        chunks[k] = minus
    last = [shift(plus[:1], "z", NZ, 1), shift(minus[1:], "z", NZ, -1)]
    early = [chunks[dz] for dz in ORDER[:EARLY]]

    gains = gain.reshape(DIM // 128, 128)
    send, dst, hot = dispatch(
        place, hidden, gains, pair_index.reshape(1, TOK), row_index.reshape(1, -1)
    )
    received = [send[0]] + [shift(send[dy], "y", NY, dy) for dy in range(1, NY)]

    base, inv = base_projection(hidden, gains, kv_weight.transpose(1, 0, 2))

    mine, other, more = down_early(place, hot, received, early)
    got = shift(other, "core", 2, 1)
    chip = (mine.astype(F32) + got.astype(F32)).astype(BF16)
    total = chip.astype(F32)
    for k in range(1, 4):
        total = total + shift(chip, "x", 4, k).astype(F32)
    half = total.astype(BF16)
    theirs = shift(half, "core", 2, 1)
    delta = up_early(place, half, theirs, received, early)
    back = [delta[0]] + [shift(delta[dy], "y", NY, -dy) for dy in range(1, NY)]
    summed = finish(finish_early_kernel, base, inv, dst, back, F32)

    low = down_late(hot, received, last, more)
    chip = (low.astype(F32) + shift(low, "core", 2, 1).astype(F32)).astype(BF16)
    total = chip.astype(F32)
    for k in range(1, 4):
        total = total + shift(chip, "x", 4, k).astype(F32)
    delta = up_late(hot, total.astype(BF16), received, early, last)
    back = [delta[0]] + [shift(delta[dy], "y", NY, -dy) for dy in range(1, NY)]
    out = finish(finish_late_kernel, summed, inv, dst, back, BF16)
    return out.reshape(TOK, 2, 128)


def solution(mesh):
    split = Mesh(mesh.devices.reshape(4, 2, NY, NZ), ("x", "core", "y", "z"))
    tp = ("x", "core")
    ad = ("y", "z")
    return jax.shard_map(
        on_device,
        mesh=split,
        in_specs=(
            P(ad, None),
            P(),
            P(None, None, tp),
            P(ad, tp, None),
            P(ad, None, None, tp),
            P(ad),
            P(),
        ),
        out_specs=P(ad, None, tp),
        check_vma=False,
    )
```

```python
import jax
import jax.numpy as jnp
from jax import lax
from jax.experimental import pallas as pl
from jax.experimental.pallas import tpu as pltpu
from jax.sharding import Mesh, PartitionSpec as P


epsilon = 1e-05
adapter_scale = 0.5
F32 = jnp.float32
BF16 = jnp.bfloat16

TOK = 448
DIM = 8192
COLS = 1024
CAP = 28
BLOCK = 32
NZ = 8
NY = 4
BUCKETS = NZ + 1
SLOTS = BUCKETS * BLOCK
EARLY = 5
LATE = BUCKETS - EARLY
ORDER = (0, 7, 1, 6, 2, 5, 3, 4)
RANK2 = 128
VMEM_LIMIT = 24 * 1024 * 1024


def iota(shape, axis):
    return lax.broadcasted_iota(jnp.int32, shape, axis).astype(F32)


def to_column(row, count):
    same = iota((count, count), 0) == iota((count, count), 1)
    return jnp.sum(jnp.where(same, row, 0.0), axis=1, keepdims=True)


def params():
    return pltpu.CompilerParams(vmem_limit_bytes=VMEM_LIMIT)


def whole():
    return pl.BlockSpec(memory_space=pltpu.VMEM)


def scalars():
    return pl.BlockSpec(memory_space=pltpu.SMEM)


def gain_row(gain):
    wide = gain.astype(F32)
    return jnp.concatenate([wide[i : i + 1] for i in range(8)], axis=1)


def dispatch_kernel(place_ref, hidden_ref, gain_ref, pair_ref, table_ref, *outs):
    sends = outs[:NY]
    dst_ref, hot_ref = outs[NY:]
    own = (hidden_ref[...].astype(F32) * gain_row(gain_ref[...])).astype(BF16)
    y_me = place_ref[1].astype(F32)
    z_me = place_ref[2].astype(F32)
    count = table_ref.shape[1]
    pair = pair_ref[...].astype(F32)
    table = to_column(table_ref[...].astype(F32), count)
    slot = jnp.sum(jnp.where(iota((count, TOK), 0) == pair, table, 0.0), axis=0, keepdims=True)
    owner = jnp.floor(slot * 0.5)
    local = slot - 2.0 * owner
    same = to_column(owner, TOK) == owner
    before = iota((TOK, TOK), 0) < iota((TOK, TOK), 1)
    pos = jnp.sum(jnp.where(same & before, 1.0, 0.0), axis=0, keepdims=True)
    y_to = jnp.floor(owner * (1.0 / NZ))
    dy = y_to - y_me
    dy = jnp.where(dy < 0, dy + NY, dy)
    dz = owner - NZ * y_to - z_me
    dz = jnp.where(dz < 0, dz + NZ, dz)
    rank = jnp.where(dz == 4, 7.0, jnp.where(dz < 4, 2.0 * dz, 15.0 - 2.0 * dz))
    over = pos >= CAP
    bucket = dy * BUCKETS + jnp.where(over, float(NZ), rank)
    place = jnp.where(over, pos - CAP, pos)
    dst = bucket * BLOCK + place
    dst_ref[...] = dst
    hot_ref[0] = jnp.max(jnp.where(over, rank, -1.0)).astype(jnp.int32)
    spot = jnp.where(iota((TOK, 128), 1) == to_column(place, TOK), 1.0, 0.0).astype(BF16)
    for part in range(NY):
        pick = jnp.where(iota((SLOTS, TOK), 0) + part * SLOTS == dst, 1.0, 0.0).astype(BF16)
        rows = jnp.dot(pick, own, preferred_element_type=F32).astype(BF16)
        sends[part][...] = rows.reshape(BUCKETS, BLOCK, COLS)
        marks = jnp.where(iota((16, TOK), 0) + part * BUCKETS == bucket, local, 0.0).astype(BF16)
        ids = jnp.dot(marks, spot, preferred_element_type=F32)
        for b in range(BUCKETS):
            head = rows[b * BLOCK : (b + 1) * BLOCK, :128].astype(F32)
            head = jnp.where(iota((BLOCK, 128), 0) == CAP, ids[b : b + 1], head)
            sends[part][b, :, pl.ds(0, 128)] = head.astype(BF16)


def dispatch(place, hidden, gain, pair, table):
    message = jax.ShapeDtypeStruct((BUCKETS, BLOCK, COLS), BF16)
    out = pl.pallas_call(
        dispatch_kernel,
        grid_spec=pltpu.PrefetchScalarGridSpec(
            num_scalar_prefetch=1,
            grid=(1,),
            in_specs=[
                pl.BlockSpec((TOK, COLS), lambda i, p: (0, p[0])),
                pl.BlockSpec((8, 128), lambda i, p: (p[0], 0)),
                pl.BlockSpec((1, TOK), lambda i, p: (0, 0)),
                pl.BlockSpec((1, table.shape[1]), lambda i, p: (0, 0)),
            ],
            out_specs=[pl.BlockSpec((BUCKETS, BLOCK, COLS), lambda i, p: (0, 0, 0))] * NY
            + [pl.BlockSpec((1, TOK), lambda i, p: (0, 0)), scalars()],
        ),
        out_shape=[message] * NY
        + [jax.ShapeDtypeStruct((1, TOK), F32), jax.ShapeDtypeStruct((1,), jnp.int32)],
        cost_estimate=pl.CostEstimate(
            flops=2 * NY * SLOTS * TOK * COLS, bytes_accessed=4_000_000, transcendentals=0
        ),
        name="dispatch",
    )(place, hidden, gain, pair, table)
    return out[:NY], out[NY], out[NY + 1]


def columns_kernel(row_ref, column_ref):
    column_ref[...] = jnp.broadcast_to(to_column(row_ref[...], TOK), (TOK, 128))


def columns(row):
    return pl.pallas_call(
        columns_kernel,
        in_specs=[whole()],
        out_specs=whole(),
        out_shape=jax.ShapeDtypeStruct((TOK, 128), F32),
        compiler_params=params(),
        cost_estimate=pl.CostEstimate(flops=1_000_000, bytes_accessed=300_000, transcendentals=0),
        name="columns",
    )(row)


def base_kernel(
    hidden_ref, gain_ref, mixed_ref, out_ref, inv_ref, square_ref, scaled_ref, weight_ref
):
    step = pl.program_id(0)
    gain = gain_row(gain_ref[...]).astype(BF16)
    rows = 64

    @pl.when(step == 0)
    def _():
        square_ref[...] = jnp.zeros_like(square_ref)

    for r in range(0, TOK, rows):
        square = square_ref[r : r + rows, :]
        for c in range(0, hidden_ref.shape[1], 128):
            part = hidden_ref[r : r + rows, c : c + 128]
            scaled_ref[r : r + rows, c : c + 128] = part * gain[:, c : c + 128]
            wide = part.astype(F32)
            square = square + wide * wide
        square_ref[r : r + rows, :] = square
    row = lax.broadcasted_iota(jnp.int32, (256, 256), 0)
    source = 2 * (row % 128) + row // 128
    part_rows = jnp.where(
        lax.broadcasted_iota(jnp.int32, (256, 256), 1) == source, 1.0, 0.0
    ).astype(BF16)
    for b in range(0, mixed_ref.shape[0], 512):
        pair = jnp.concatenate([mixed_ref[b : b + 256], mixed_ref[b + 256 : b + 512]], axis=1)
        parted = jnp.dot(part_rows, pair, preferred_element_type=F32).astype(BF16)
        d = b // 2
        weight_ref[d : d + 128, :128] = parted[:128, :128]
        weight_ref[d : d + 128, 128:] = parted[128:, :128]
        weight_ref[d + 128 : d + 256, :128] = parted[:128, 128:]
        weight_ref[d + 128 : d + 256, 128:] = parted[128:, 128:]
    term = jnp.dot(scaled_ref[...], weight_ref[...], preferred_element_type=F32)

    @pl.when(step == 0)
    def _():
        out_ref[...] = term

    @pl.when(step > 0)
    def _():
        out_ref[...] += term

    @pl.when(step == pl.num_programs(0) - 1)
    def _():
        mean = jnp.sum(square_ref[...], axis=1, keepdims=True) * (1.0 / DIM)
        inv = lax.rsqrt(mean + epsilon)
        out_ref[...] = out_ref[...] * inv
        inv_ref[...] = jnp.broadcast_to(inv, (TOK, 128))


def base_projection(hidden, gain, weight):
    tile = 1024
    return pl.pallas_call(
        base_kernel,
        grid=(DIM // tile,),
        in_specs=[
            pl.BlockSpec((TOK, tile), lambda k: (0, k)),
            pl.BlockSpec((8, 128), lambda k: (k, 0)),
            pl.BlockSpec((2 * tile, 128), lambda k: (k, 0)),
        ],
        out_specs=[
            pl.BlockSpec((TOK, 256), lambda k: (0, 0)),
            pl.BlockSpec((TOK, 128), lambda k: (0, 0)),
        ],
        out_shape=[
            jax.ShapeDtypeStruct((TOK, 256), F32),
            jax.ShapeDtypeStruct((TOK, 128), F32),
        ],
        scratch_shapes=[pltpu.VMEM((TOK, 128), F32), pltpu.VMEM((TOK, tile), BF16), pltpu.VMEM((tile, 256), BF16)],
        cost_estimate=pl.CostEstimate(
            flops=2 * TOK * DIM * 256, bytes_accessed=12_000_000, transcendentals=0
        ),
        name="base",
    )(hidden, gain, weight)


def local_column(head):
    row = head[CAP : CAP + 1, :].astype(F32)
    same = iota((BLOCK, 128), 0) == iota((BLOCK, 128), 1)
    return jnp.sum(jnp.where(same, row, 0.0), axis=1, keepdims=True)


def bucket_rows(received, b):
    rows = jnp.concatenate([r[b] for r in received], axis=0)
    local = jnp.concatenate([local_column(r[b, :, :128]) for r in received], axis=0)
    return rows, local


def project(rows, local, weight):
    both = jnp.dot(rows, weight, preferred_element_type=F32)
    return jnp.where(local < 0.5, both[:, :RANK2], both[:, RANK2:])


def down_early_kernel(place_ref, hot_ref, *refs):
    received = refs[:NY]
    chunks = refs[NY : NY + EARLY]
    mine_ref, other_ref, more_ref, low_ref = refs[NY + EARLY :]
    more_ref[...] = jnp.zeros_like(more_ref)
    for k in range(EARLY):
        c = chunks[k]
        weight = jnp.concatenate([c[0, :COLS], c[1, :COLS]], axis=1)
        rows, local = bucket_rows(received, k)
        low_ref[k * NY * BLOCK : (k + 1) * NY * BLOCK] = project(rows, local, weight).astype(BF16)

        @pl.when(hot_ref[0] == k)
        def _():
            rows, local = bucket_rows(received, NZ)
            more_ref[...] = project(rows, local, weight).astype(BF16)

    size = EARLY * NY * BLOCK // 2
    first = pl.multiple_of(place_ref[3] * size, size)
    second = pl.multiple_of(size - place_ref[3] * size, size)
    mine_ref[...] = low_ref[pl.ds(first, size), :]
    other_ref[...] = low_ref[pl.ds(second, size), :]


def down_early(place, hot, received, chunks):
    size = EARLY * NY * BLOCK // 2
    return pl.pallas_call(
        down_early_kernel,
        in_specs=[scalars(), scalars()] + [whole()] * (NY + EARLY),
        out_specs=[whole()] * 3,
        out_shape=[
            jax.ShapeDtypeStruct((size, RANK2), BF16),
            jax.ShapeDtypeStruct((size, RANK2), BF16),
            jax.ShapeDtypeStruct((NY * BLOCK, RANK2), BF16),
        ],
        scratch_shapes=[pltpu.VMEM((2 * size, RANK2), BF16)],
        compiler_params=params(),
        cost_estimate=pl.CostEstimate(
            flops=2 * EARLY * 128 * 1024 * 256, bytes_accessed=6_000_000, transcendentals=0
        ),
        name="down_early",
    )(place, hot, *received, *chunks)


def down_late_kernel(hot_ref, *refs):
    received = refs[:NY]
    chunks = refs[NY:-2]
    more_ref, low_ref = refs[-2:]
    low_ref[LATE - 1] = more_ref[...]
    for at in range(LATE - 1):
        if at < LATE - 2:
            zero, one = chunks[at][0, :COLS], chunks[at][1, :COLS]
        else:
            zero, one = chunks[at][0, :COLS], chunks[at + 1][0, :COLS]
        weight = jnp.concatenate([zero, one], axis=1)
        rows, local = bucket_rows(received, EARLY + at)
        low_ref[at] = project(rows, local, weight).astype(BF16)

        @pl.when(hot_ref[0] == EARLY + at)
        def _():
            rows, local = bucket_rows(received, NZ)
            low_ref[LATE - 1] = project(rows, local, weight).astype(BF16)


def down_late(hot, received, chunks, more):
    return pl.pallas_call(
        down_late_kernel,
        in_specs=[scalars()] + [whole()] * (NY + len(chunks) + 1),
        out_specs=whole(),
        out_shape=jax.ShapeDtypeStruct((LATE, NY * BLOCK, RANK2), BF16),
        compiler_params=params(),
        cost_estimate=pl.CostEstimate(
            flops=2 * 512 * 1024 * 256, bytes_accessed=2_000_000, transcendentals=0
        ),
        name="down_late",
    )(hot, *received, *chunks, more)


def spread(low, local):
    zero = jnp.zeros_like(low)
    return jnp.concatenate(
        [jnp.where(local < 0.5, low, zero), jnp.where(local < 0.5, zero, low)], axis=1
    ).astype(BF16)


def up_matrix(up):
    key_row = (lax.broadcasted_iota(jnp.int32, (2 * RANK2, 128), 0) % RANK2) < RANK2 // 2
    up = up.astype(F32)
    return jnp.concatenate(
        [jnp.where(key_row, up, 0.0), jnp.where(key_row, 0.0, up)], axis=1
    ).astype(BF16)


def up_rows(chunk):
    return jnp.concatenate([chunk[0, COLS:], chunk[1, COLS:]], axis=0)


def up_early_kernel(place_ref, half_ref, theirs_ref, *refs):
    received = refs[:NY]
    chunks = refs[NY : NY + EARLY]
    outs = refs[NY + EARLY : -1]
    low_ref = refs[-1]
    size = EARLY * NY * BLOCK // 2
    first = pl.multiple_of(place_ref[3] * size, size)
    second = pl.multiple_of(size - place_ref[3] * size, size)
    low_ref[pl.ds(first, size), :] = half_ref[...]
    low_ref[pl.ds(second, size), :] = theirs_ref[...]
    for k in range(EARLY):
        local = jnp.concatenate([local_column(r[k, :, :128]) for r in received], axis=0)
        low = low_ref[k * NY * BLOCK : (k + 1) * NY * BLOCK, :].astype(F32)
        delta = jnp.dot(
            spread(low, local), up_matrix(up_rows(chunks[k])), preferred_element_type=F32
        ).astype(BF16)
        for s in range(NY):
            outs[s][k] = delta[s * BLOCK : (s + 1) * BLOCK]


def up_early(place, half, theirs, received, chunks):
    return pl.pallas_call(
        up_early_kernel,
        in_specs=[scalars()] + [whole()] * (2 + NY + EARLY),
        out_specs=[whole()] * NY,
        out_shape=[jax.ShapeDtypeStruct((EARLY, BLOCK, 256), BF16)] * NY,
        scratch_shapes=[pltpu.VMEM((EARLY * NY * BLOCK, RANK2), BF16)],
        compiler_params=params(),
        cost_estimate=pl.CostEstimate(
            flops=2 * EARLY * 128 * 256 * 256, bytes_accessed=1_500_000, transcendentals=0
        ),
        name="up_early",
    )(place, half, theirs, *received, *chunks)


def up_late_kernel(hot_ref, low_ref, *refs):
    received = refs[:NY]
    chunks = refs[NY:-NY]
    outs = refs[-NY:]
    ups = [up_rows(c) for c in chunks[:-2]]
    ups.append(jnp.concatenate([chunks[-2][0, COLS:], chunks[-1][0, COLS:]], axis=0))
    hot_up = ups[0].astype(F32)
    for k in range(1, NZ):
        hot_up = jnp.where(hot_ref[0] == k, ups[k].astype(F32), hot_up)
    for at in range(LATE):
        up = hot_up if at == LATE - 1 else ups[EARLY + at]
        local = jnp.concatenate([local_column(r[EARLY + at, :, :128]) for r in received], axis=0)
        delta = jnp.dot(
            spread(low_ref[at].astype(F32), local), up_matrix(up), preferred_element_type=F32
        ).astype(BF16)
        for s in range(NY):
            outs[s][at] = delta[s * BLOCK : (s + 1) * BLOCK]


def up_late(hot, low, received, chunks):
    return pl.pallas_call(
        up_late_kernel,
        in_specs=[scalars()] + [whole()] * (1 + NY + len(chunks)),
        out_specs=[whole()] * NY,
        out_shape=[jax.ShapeDtypeStruct((LATE, BLOCK, 256), BF16)] * NY,
        compiler_params=params(),
        cost_estimate=pl.CostEstimate(
            flops=2 * 512 * 256 * 256, bytes_accessed=1_500_000, transcendentals=0
        ),
        name="up_late",
    )(hot, low, *received, *chunks)


def collect(dst, first, count, back):
    total = jnp.zeros((TOK, 256), F32)
    for part in range(NY):
        size = count * BLOCK
        at = iota((TOK, size), 1) + (part * SLOTS + first * BLOCK)
        pick = jnp.where(at == dst, 1.0, 0.0).astype(BF16)
        total = total + jnp.dot(
            pick, back[part][...].reshape(size, 256), preferred_element_type=F32
        )
    return total


def finish_early_kernel(base_ref, inv_ref, dst_ref, *refs):
    total = collect(dst_ref[:, :1], 0, EARLY, refs[:NY])
    refs[NY][...] = base_ref[...] + (adapter_scale * inv_ref[:, :1]) * total


def finish_late_kernel(sum_ref, inv_ref, dst_ref, *refs):
    total = collect(dst_ref[:, :1], EARLY, LATE, refs[:NY])
    refs[NY][...] = (sum_ref[...] + (adapter_scale * inv_ref[:, :1]) * total).astype(BF16)


def finish(kernel, start, inv, dst, back, kind):
    return pl.pallas_call(
        kernel,
        in_specs=[whole()] * (3 + NY),
        out_specs=whole(),
        out_shape=jax.ShapeDtypeStruct((TOK, 256), kind),
        compiler_params=params(),
        cost_estimate=pl.CostEstimate(
            flops=2 * TOK * 1024 * 256, bytes_accessed=1_500_000, transcendentals=0
        ),
    )(start, inv, dst, *back)


def shift(x, axis, size, by):
    return lax.ppermute(x, axis, [(i, (i + by) % size) for i in range(size)])


def on_device(hidden, gain, kv_weight, down_weight, up_weight, pair_index, row_index):
    tp = lax.axis_index("x") * 2 + lax.axis_index("core")
    places = [tp, lax.axis_index("y"), lax.axis_index("z"), lax.axis_index("core")]
    place = jnp.stack(places).astype(jnp.int32)

    own = jnp.concatenate([down_weight, up_weight.reshape(2, RANK2, 128)], axis=1)
    chunks = {0: own}
    plus = minus = own
    for k in range(1, 4):
        plus = shift(plus, "z", NZ, 1)
        minus = shift(minus, "z", NZ, -1)
        chunks[NZ - k] = plus
        chunks[k] = minus
    last = [shift(plus[:1], "z", NZ, 1), shift(minus[1:], "z", NZ, -1)]
    early = [chunks[dz] for dz in ORDER[:EARLY]]
    late = [chunks[dz] for dz in ORDER[EARLY:-1]] + last

    gains = gain.reshape(DIM // 128, 128)
    send, dst, hot = dispatch(
        place, hidden, gains, pair_index.reshape(1, TOK), row_index.reshape(1, -1)
    )
    dst = columns(dst)
    received = [send[0]] + [shift(send[dy], "y", NY, dy) for dy in range(1, NY)]

    base, inv = base_projection(hidden, gains, kv_weight.reshape(2 * DIM, 128))

    mine, other, more = down_early(place, hot, received, early)
    got = shift(other, "core", 2, 1)
    chip = (mine.astype(F32) + got.astype(F32)).astype(BF16)
    total = chip.astype(F32)
    for k in range(1, 4):
        total = total + shift(chip, "x", 4, k).astype(F32)
    half = total.astype(BF16)
    theirs = shift(half, "core", 2, 1)
    delta = up_early(place, half, theirs, received, early)
    back = [delta[0]] + [shift(delta[dy], "y", NY, -dy) for dy in range(1, NY)]
    summed = finish(finish_early_kernel, base, inv, dst, back, F32)

    low = down_late(hot, received, late, more)
    chip = (low.astype(F32) + shift(low, "core", 2, 1).astype(F32)).astype(BF16)
    total = chip.astype(F32)
    for k in range(1, 4):
        total = total + shift(chip, "x", 4, k).astype(F32)
    delta = up_late(hot, total.astype(BF16), received, early + late)
    back = [delta[0]] + [shift(delta[dy], "y", NY, -dy) for dy in range(1, NY)]
    out = finish(finish_late_kernel, summed, inv, dst, back, BF16)
    return out.reshape(TOK, 2, 128)


def solution(mesh):
    split = Mesh(mesh.devices.reshape(4, 2, NY, NZ), ("x", "core", "y", "z"))
    tp = ("x", "core")
    ad = ("y", "z")
    return jax.shard_map(
        on_device,
        mesh=split,
        in_specs=(
            P(ad, None),
            P(),
            P(None, None, tp),
            P(ad, tp, None),
            P(ad, None, None, tp),
            P(ad),
            P(),
        ),
        out_specs=P(ad, None, tp),
        check_vma=False,
    )
```

```python
import jax
import jax.numpy as jnp
from jax import lax
from jax.experimental import pallas as pl
from jax.experimental.pallas import tpu as pltpu
from jax.sharding import Mesh, PartitionSpec as P


epsilon = 1e-05
adapter_scale = 0.5
F32 = jnp.float32
BF16 = jnp.bfloat16

TOK = 448
DIM = 8192
COLS = 1024
CAP = 28
BLOCK = 32
NZ = 8
NY = 4
BUCKETS = NZ + 1
SLOTS = BUCKETS * BLOCK
EARLY = 5
LATE = BUCKETS - EARLY
ORDER = (0, 7, 1, 6, 2, 5, 3, 4)
RANK2 = 128
VMEM_LIMIT = 24 * 1024 * 1024


def iota(shape, axis):
    return lax.broadcasted_iota(jnp.int32, shape, axis).astype(F32)


def to_column(row, count):
    same = iota((count, count), 0) == iota((count, count), 1)
    return jnp.sum(jnp.where(same, row, 0.0), axis=1, keepdims=True)


def params():
    return pltpu.CompilerParams(vmem_limit_bytes=VMEM_LIMIT)


def whole():
    return pl.BlockSpec(memory_space=pltpu.VMEM)


def scalars():
    return pl.BlockSpec(memory_space=pltpu.SMEM)


def gain_row(gain):
    wide = gain.astype(F32)
    return jnp.concatenate([wide[i : i + 1] for i in range(8)], axis=1)


def dispatch_kernel(place_ref, hidden_ref, gain_ref, pair_ref, table_ref, *outs):
    sends = outs[:NY]
    dst_ref, hot_ref = outs[NY:]
    own = (hidden_ref[...].astype(F32) * gain_row(gain_ref[...])).astype(BF16)
    y_me = place_ref[1].astype(F32)
    z_me = place_ref[2].astype(F32)
    count = table_ref.shape[1]
    pair = pair_ref[...].astype(F32)
    table = to_column(table_ref[...].astype(F32), count)
    slot = jnp.sum(jnp.where(iota((count, TOK), 0) == pair, table, 0.0), axis=0, keepdims=True)
    owner = jnp.floor(slot * 0.5)
    local = slot - 2.0 * owner
    same = to_column(owner, TOK) == owner
    before = iota((TOK, TOK), 0) < iota((TOK, TOK), 1)
    pos = jnp.sum(jnp.where(same & before, 1.0, 0.0), axis=0, keepdims=True)
    y_to = jnp.floor(owner * (1.0 / NZ))
    dy = y_to - y_me
    dy = jnp.where(dy < 0, dy + NY, dy)
    dz = owner - NZ * y_to - z_me
    dz = jnp.where(dz < 0, dz + NZ, dz)
    rank = jnp.where(dz == 4, 7.0, jnp.where(dz < 4, 2.0 * dz, 15.0 - 2.0 * dz))
    over = pos >= CAP
    bucket = dy * BUCKETS + jnp.where(over, float(NZ), rank)
    place = jnp.where(over, pos - CAP, pos)
    dst = bucket * BLOCK + place
    dst_ref[...] = dst
    hot_ref[0] = jnp.max(jnp.where(over, rank, -1.0)).astype(jnp.int32)
    spot = jnp.where(iota((TOK, 128), 1) == to_column(place, TOK), 1.0, 0.0).astype(BF16)
    for part in range(NY):
        pick = jnp.where(iota((SLOTS, TOK), 0) + part * SLOTS == dst, 1.0, 0.0).astype(BF16)
        rows = jnp.dot(pick, own, preferred_element_type=F32).astype(BF16)
        sends[part][...] = rows.reshape(BUCKETS, BLOCK, COLS)
        marks = jnp.where(iota((16, TOK), 0) + part * BUCKETS == bucket, local, 0.0).astype(BF16)
        ids = jnp.dot(marks, spot, preferred_element_type=F32)
        for b in range(BUCKETS):
            head = rows[b * BLOCK : (b + 1) * BLOCK, :128].astype(F32)
            head = jnp.where(iota((BLOCK, 128), 0) == CAP, ids[b : b + 1], head)
            sends[part][b, :, pl.ds(0, 128)] = head.astype(BF16)


def dispatch(place, hidden, gain, pair, table):
    message = jax.ShapeDtypeStruct((BUCKETS, BLOCK, COLS), BF16)
    out = pl.pallas_call(
        dispatch_kernel,
        grid_spec=pltpu.PrefetchScalarGridSpec(
            num_scalar_prefetch=1,
            grid=(1,),
            in_specs=[
                pl.BlockSpec((TOK, COLS), lambda i, p: (0, p[0])),
                pl.BlockSpec((8, 128), lambda i, p: (p[0], 0)),
                pl.BlockSpec((1, TOK), lambda i, p: (0, 0)),
                pl.BlockSpec((1, table.shape[1]), lambda i, p: (0, 0)),
            ],
            out_specs=[pl.BlockSpec((BUCKETS, BLOCK, COLS), lambda i, p: (0, 0, 0))] * NY
            + [pl.BlockSpec((1, TOK), lambda i, p: (0, 0)), scalars()],
        ),
        out_shape=[message] * NY
        + [jax.ShapeDtypeStruct((1, TOK), F32), jax.ShapeDtypeStruct((1,), jnp.int32)],
        cost_estimate=pl.CostEstimate(
            flops=2 * NY * SLOTS * TOK * COLS, bytes_accessed=4_000_000, transcendentals=0
        ),
        name="dispatch",
    )(place, hidden, gain, pair, table)
    return out[:NY], out[NY], out[NY + 1]


def columns_kernel(row_ref, column_ref):
    column_ref[...] = jnp.broadcast_to(to_column(row_ref[...], TOK), (TOK, 128))


def columns(row):
    return pl.pallas_call(
        columns_kernel,
        in_specs=[whole()],
        out_specs=whole(),
        out_shape=jax.ShapeDtypeStruct((TOK, 128), F32),
        compiler_params=params(),
        cost_estimate=pl.CostEstimate(flops=1_000_000, bytes_accessed=300_000, transcendentals=0),
        name="columns",
    )(row)


def base_kernel(
    hidden_ref, gain_ref, mixed_ref, out_ref, inv_ref, square_ref, scaled_ref, weight_ref
):
    step = pl.program_id(0)
    gain = gain_row(gain_ref[...]).astype(BF16)
    rows = 64

    @pl.when(step == 0)
    def _():
        square_ref[...] = jnp.zeros_like(square_ref)

    for r in range(0, TOK, rows):
        square = square_ref[r : r + rows, :]
        for c in range(0, hidden_ref.shape[1], 128):
            part = hidden_ref[r : r + rows, c : c + 128]
            scaled_ref[r : r + rows, c : c + 128] = part * gain[:, c : c + 128]
            wide = part.astype(F32)
            square = square + wide * wide
        square_ref[r : r + rows, :] = square
    row = lax.broadcasted_iota(jnp.int32, (256, 256), 0)
    source = 2 * (row % 128) + row // 128
    part_rows = jnp.where(
        lax.broadcasted_iota(jnp.int32, (256, 256), 1) == source, 1.0, 0.0
    ).astype(BF16)
    for b in range(0, mixed_ref.shape[0], 512):
        pair = jnp.concatenate([mixed_ref[b : b + 256], mixed_ref[b + 256 : b + 512]], axis=1)
        parted = jnp.dot(part_rows, pair, preferred_element_type=F32).astype(BF16)
        d = b // 2
        weight_ref[d : d + 128, :128] = parted[:128, :128]
        weight_ref[d : d + 128, 128:] = parted[128:, :128]
        weight_ref[d + 128 : d + 256, :128] = parted[:128, 128:]
        weight_ref[d + 128 : d + 256, 128:] = parted[128:, 128:]
    term = jnp.dot(scaled_ref[...], weight_ref[...], preferred_element_type=F32)

    @pl.when(step == 0)
    def _():
        out_ref[...] = term

    @pl.when(step > 0)
    def _():
        out_ref[...] += term

    @pl.when(step == pl.num_programs(0) - 1)
    def _():
        mean = jnp.sum(square_ref[...], axis=1, keepdims=True) * (1.0 / DIM)
        inv = lax.rsqrt(mean + epsilon)
        out_ref[...] = out_ref[...] * inv
        inv_ref[...] = jnp.broadcast_to(inv, (TOK, 128))


def base_projection(hidden, gain, weight):
    tile = 1024
    return pl.pallas_call(
        base_kernel,
        grid=(DIM // tile,),
        in_specs=[
            pl.BlockSpec((TOK, tile), lambda k: (0, k)),
            pl.BlockSpec((8, 128), lambda k: (k, 0)),
            pl.BlockSpec((2 * tile, 128), lambda k: (k, 0)),
        ],
        out_specs=[
            pl.BlockSpec((TOK, 256), lambda k: (0, 0)),
            pl.BlockSpec((TOK, 128), lambda k: (0, 0)),
        ],
        out_shape=[
            jax.ShapeDtypeStruct((TOK, 256), F32),
            jax.ShapeDtypeStruct((TOK, 128), F32),
        ],
        scratch_shapes=[pltpu.VMEM((TOK, 128), F32), pltpu.VMEM((TOK, tile), BF16), pltpu.VMEM((tile, 256), BF16)],
        cost_estimate=pl.CostEstimate(
            flops=2 * TOK * DIM * 256, bytes_accessed=12_000_000, transcendentals=0
        ),
        name="base",
    )(hidden, gain, weight)


def local_column(head):
    row = head[CAP : CAP + 1, :].astype(F32)
    same = iota((BLOCK, 128), 0) == iota((BLOCK, 128), 1)
    return jnp.sum(jnp.where(same, row, 0.0), axis=1, keepdims=True)


def bucket_rows(received, b):
    rows = jnp.concatenate([r[b] for r in received], axis=0)
    local = jnp.concatenate([local_column(r[b, :, :128]) for r in received], axis=0)
    return rows, local


def project(rows, local, weight):
    both = jnp.dot(rows, weight, preferred_element_type=F32)
    return jnp.where(local < 0.5, both[:, :RANK2], both[:, RANK2:])


def down_early_kernel(hot_ref, *refs):
    received = refs[:NY]
    chunks = refs[NY : NY + EARLY]
    low_ref, more_ref = refs[NY + EARLY :]
    more_ref[...] = jnp.zeros_like(more_ref)
    for k in range(EARLY):
        c = chunks[k]
        weight = jnp.concatenate([c[0, :COLS], c[1, :COLS]], axis=1)
        rows, local = bucket_rows(received, k)
        low_ref[k] = project(rows, local, weight).astype(BF16)

        @pl.when(hot_ref[0] == k)
        def _():
            rows, local = bucket_rows(received, NZ)
            more_ref[...] = project(rows, local, weight).astype(BF16)


def down_early(hot, received, chunks):
    return pl.pallas_call(
        down_early_kernel,
        in_specs=[scalars()] + [whole()] * (NY + EARLY),
        out_specs=[whole()] * 2,
        out_shape=[
            jax.ShapeDtypeStruct((EARLY, NY * BLOCK, RANK2), BF16),
            jax.ShapeDtypeStruct((NY * BLOCK, RANK2), BF16),
        ],
        compiler_params=params(),
        cost_estimate=pl.CostEstimate(
            flops=2 * EARLY * 128 * 1024 * 256, bytes_accessed=6_000_000, transcendentals=0
        ),
        name="down_early",
    )(hot, *received, *chunks)


def down_late_kernel(hot_ref, *refs):
    received = refs[:NY]
    chunks = refs[NY:-2]
    more_ref, low_ref = refs[-2:]
    low_ref[LATE - 1] = more_ref[...]
    for at in range(LATE - 1):
        if at < LATE - 2:
            zero, one = chunks[at][0, :COLS], chunks[at][1, :COLS]
        else:
            zero, one = chunks[at][0, :COLS], chunks[at + 1][0, :COLS]
        weight = jnp.concatenate([zero, one], axis=1)
        rows, local = bucket_rows(received, EARLY + at)
        low_ref[at] = project(rows, local, weight).astype(BF16)

        @pl.when(hot_ref[0] == EARLY + at)
        def _():
            rows, local = bucket_rows(received, NZ)
            low_ref[LATE - 1] = project(rows, local, weight).astype(BF16)


def down_late(hot, received, chunks, more):
    return pl.pallas_call(
        down_late_kernel,
        in_specs=[scalars()] + [whole()] * (NY + len(chunks) + 1),
        out_specs=whole(),
        out_shape=jax.ShapeDtypeStruct((LATE, NY * BLOCK, RANK2), BF16),
        compiler_params=params(),
        cost_estimate=pl.CostEstimate(
            flops=2 * 512 * 1024 * 256, bytes_accessed=2_000_000, transcendentals=0
        ),
        name="down_late",
    )(hot, *received, *chunks, more)


def spread(low, local):
    zero = jnp.zeros_like(low)
    return jnp.concatenate(
        [jnp.where(local < 0.5, low, zero), jnp.where(local < 0.5, zero, low)], axis=1
    ).astype(BF16)


def up_matrix(up):
    key_row = (lax.broadcasted_iota(jnp.int32, (2 * RANK2, 128), 0) % RANK2) < RANK2 // 2
    up = up.astype(F32)
    return jnp.concatenate(
        [jnp.where(key_row, up, 0.0), jnp.where(key_row, 0.0, up)], axis=1
    ).astype(BF16)


def up_rows(chunk):
    return jnp.concatenate([chunk[0, COLS:], chunk[1, COLS:]], axis=0)


def up_early_kernel(low_ref, *refs):
    received = refs[:NY]
    chunks = refs[NY : NY + EARLY]
    outs = refs[NY + EARLY :]
    for k in range(EARLY):
        local = jnp.concatenate([local_column(r[k, :, :128]) for r in received], axis=0)
        low = low_ref[k].astype(F32)
        delta = jnp.dot(
            spread(low, local), up_matrix(up_rows(chunks[k])), preferred_element_type=F32
        ).astype(BF16)
        for s in range(NY):
            outs[s][k] = delta[s * BLOCK : (s + 1) * BLOCK]


def up_early(low, received, chunks):
    return pl.pallas_call(
        up_early_kernel,
        in_specs=[whole()] * (1 + NY + EARLY),
        out_specs=[whole()] * NY,
        out_shape=[jax.ShapeDtypeStruct((EARLY, BLOCK, 256), BF16)] * NY,
        compiler_params=params(),
        cost_estimate=pl.CostEstimate(
            flops=2 * EARLY * 128 * 256 * 256, bytes_accessed=1_500_000, transcendentals=0
        ),
        name="up_early",
    )(low, *received, *chunks)


def up_prepare_kernel(hot_ref, *refs):
    received = refs[:NY]
    chunks = refs[NY:-2]
    matrix_ref, mask_ref = refs[-2:]
    ups = [up_rows(c) for c in chunks[:-2]]
    ups.append(jnp.concatenate([chunks[-2][0, COLS:], chunks[-1][0, COLS:]], axis=0))
    hot_up = ups[0].astype(F32)
    for k in range(1, NZ):
        hot_up = jnp.where(hot_ref[0] == k, ups[k].astype(F32), hot_up)
    ones = jnp.ones((NY * BLOCK, RANK2), F32)
    for at in range(LATE):
        matrix_ref[at] = up_matrix(hot_up if at == LATE - 1 else ups[EARLY + at])
        local = jnp.concatenate([local_column(r[EARLY + at, :, :128]) for r in received], axis=0)
        mask_ref[at] = spread(ones, local)


def up_prepare(hot, received, chunks):
    return pl.pallas_call(
        up_prepare_kernel,
        in_specs=[scalars()] + [whole()] * (NY + len(chunks)),
        out_specs=[whole()] * 2,
        out_shape=[
            jax.ShapeDtypeStruct((LATE, 256, 256), BF16),
            jax.ShapeDtypeStruct((LATE, NY * BLOCK, 256), BF16),
        ],
        compiler_params=params(),
        cost_estimate=pl.CostEstimate(
            flops=4_000_000, bytes_accessed=1_500_000, transcendentals=0
        ),
        name="up_prepare",
    )(hot, *received, *chunks)


def up_late_kernel(low_ref, matrix_ref, mask_ref, *outs):
    for at in range(LATE):
        low = low_ref[at]
        both = jnp.concatenate([low, low], axis=1) * mask_ref[at]
        delta = jnp.dot(both, matrix_ref[at], preferred_element_type=F32).astype(BF16)
        for s in range(NY):
            outs[s][at] = delta[s * BLOCK : (s + 1) * BLOCK]


def up_late(low, matrix, mask):
    return pl.pallas_call(
        up_late_kernel,
        in_specs=[whole()] * 3,
        out_specs=[whole()] * NY,
        out_shape=[jax.ShapeDtypeStruct((LATE, BLOCK, 256), BF16)] * NY,
        compiler_params=params(),
        cost_estimate=pl.CostEstimate(
            flops=2 * 512 * 256 * 256, bytes_accessed=1_000_000, transcendentals=0
        ),
        name="up_late",
    )(low, matrix, mask)


def collect(dst, first, count, back):
    total = jnp.zeros((TOK, 256), F32)
    for part in range(NY):
        size = count * BLOCK
        at = iota((TOK, size), 1) + (part * SLOTS + first * BLOCK)
        pick = jnp.where(at == dst, 1.0, 0.0).astype(BF16)
        total = total + jnp.dot(
            pick, back[part][...].reshape(size, 256), preferred_element_type=F32
        )
    return total


def finish_early_kernel(base_ref, inv_ref, dst_ref, *refs):
    total = collect(dst_ref[:, :1], 0, EARLY, refs[:NY])
    refs[NY][...] = base_ref[...] + (adapter_scale * inv_ref[:, :1]) * total


def finish_late_kernel(sum_ref, inv_ref, dst_ref, *refs):
    total = collect(dst_ref[:, :1], EARLY, LATE, refs[:NY])
    refs[NY][...] = (sum_ref[...] + (adapter_scale * inv_ref[:, :1]) * total).astype(BF16)


def finish(kernel, start, inv, dst, back, kind):
    return pl.pallas_call(
        kernel,
        in_specs=[whole()] * (3 + NY),
        out_specs=whole(),
        out_shape=jax.ShapeDtypeStruct((TOK, 256), kind),
        compiler_params=params(),
        cost_estimate=pl.CostEstimate(
            flops=2 * TOK * 1024 * 256, bytes_accessed=1_500_000, transcendentals=0
        ),
    )(start, inv, dst, *back)


def shift(x, axis, size, by):
    return lax.ppermute(x, axis, [(i, (i + by) % size) for i in range(size)])


def pair_sum(x, axis, size, flip):
    other = lax.ppermute(x, axis, [(i, i ^ flip) for i in range(size)])
    return (x.astype(F32) + other.astype(F32)).astype(BF16)


def sum_over_tp(x):
    x = pair_sum(x, "core", 2, 1)
    x = pair_sum(x, "x", 4, 1)
    return pair_sum(x, "x", 4, 3)


def on_device(hidden, gain, kv_weight, down_weight, up_weight, pair_index, row_index):
    tp = lax.axis_index("x") * 2 + lax.axis_index("core")
    places = [tp, lax.axis_index("y"), lax.axis_index("z")]
    place = jnp.stack(places).astype(jnp.int32)

    own = jnp.concatenate([down_weight, up_weight.reshape(2, RANK2, 128)], axis=1)
    chunks = {0: own}
    plus = minus = own
    for k in range(1, 4):
        plus = shift(plus, "z", NZ, 1)
        minus = shift(minus, "z", NZ, -1)
        chunks[NZ - k] = plus
        chunks[k] = minus
    last = [shift(plus[:1], "z", NZ, 1), shift(minus[1:], "z", NZ, -1)]
    early = [chunks[dz] for dz in ORDER[:EARLY]]
    late = [chunks[dz] for dz in ORDER[EARLY:-1]] + last

    gains = gain.reshape(DIM // 128, 128)
    send, dst, hot = dispatch(
        place, hidden, gains, pair_index.reshape(1, TOK), row_index.reshape(1, -1)
    )
    dst = columns(dst)
    received = [send[0]] + [shift(send[dy], "y", NY, dy) for dy in range(1, NY)]

    base, inv = base_projection(hidden, gains, kv_weight.reshape(2 * DIM, 128))

    low, more = down_early(hot, received, early)
    low = sum_over_tp(low)
    delta = up_early(low, received, early)
    back = [delta[0]] + [shift(delta[dy], "y", NY, -dy) for dy in range(1, NY)]
    summed = finish(finish_early_kernel, base, inv, dst, back, F32)

    low = down_late(hot, received, late, more)
    matrix, mask = up_prepare(hot, received, early + late)
    low = sum_over_tp(low)
    delta = up_late(low, matrix, mask)
    back = [delta[0]] + [shift(delta[dy], "y", NY, -dy) for dy in range(1, NY)]
    out = finish(finish_late_kernel, summed, inv, dst, back, BF16)
    return out.reshape(TOK, 2, 128)


def solution(mesh):
    split = Mesh(mesh.devices.reshape(4, 2, NY, NZ), ("x", "core", "y", "z"))
    tp = ("x", "core")
    ad = ("y", "z")
    return jax.shard_map(
        on_device,
        mesh=split,
        in_specs=(
            P(ad, None),
            P(),
            P(None, None, tp),
            P(ad, tp, None),
            P(ad, None, None, tp),
            P(ad),
            P(),
        ),
        out_specs=P(ad, None, tp),
        check_vma=False,
    )
```

```python
import functools

import jax
import jax.numpy as jnp
from jax import lax
from jax.experimental import pallas as pl
from jax.experimental.pallas import tpu as pltpu
from jax.sharding import Mesh, PartitionSpec as P


epsilon = 1e-05
adapter_scale = 0.5
F32 = jnp.float32
BF16 = jnp.bfloat16

TOK = 448
DIM = 8192
COLS = 1024
CAP = 28
BLOCK = 32
NZ = 8
NY = 4
BUCKETS = NZ + 1
SLOTS = BUCKETS * BLOCK
EARLY = 5
LATE = BUCKETS - EARLY
ORDER = (0, 7, 1, 6, 2, 5, 3, 4)
RANK2 = 128
CHUNK = COLS + RANK2
VMEM_LIMIT = 24 * 1024 * 1024


def iota(shape, axis):
    return lax.broadcasted_iota(jnp.int32, shape, axis).astype(F32)


def to_column(row, count):
    same = iota((count, count), 0) == iota((count, count), 1)
    return jnp.sum(jnp.where(same, row, 0.0), axis=1, keepdims=True)


def params():
    return pltpu.CompilerParams(vmem_limit_bytes=VMEM_LIMIT)


def whole():
    return pl.BlockSpec(memory_space=pltpu.VMEM)


def scalars():
    return pl.BlockSpec(memory_space=pltpu.SMEM)


def pack_kernel(down_ref, up_ref, zero_ref, one_ref):
    for a, out_ref in enumerate((zero_ref, one_ref)):
        out_ref[:COLS] = down_ref[a]
        out_ref[COLS:] = up_ref[a]


def pack(down_weight, up_planes):
    return pl.pallas_call(
        pack_kernel,
        grid=(1,),
        in_specs=[
            pl.BlockSpec((2, COLS, 128), lambda i: (0, 0, 0)),
            pl.BlockSpec((2, RANK2, 128), lambda i: (0, 0, 0)),
        ],
        out_specs=[pl.BlockSpec((CHUNK, 128), lambda i: (0, 0))] * 2,
        out_shape=[jax.ShapeDtypeStruct((CHUNK, 128), BF16)] * 2,
        compiler_params=params(),
        cost_estimate=pl.CostEstimate(flops=0, bytes_accessed=1_200_000, transcendentals=0),
        name="pack",
    )(down_weight, up_planes)


def gain_row(gain):
    wide = gain.astype(F32)
    return jnp.concatenate([wide[i : i + 1] for i in range(8)], axis=1)


def dispatch_kernel(place_ref, hidden_ref, gain_ref, pair_ref, table_ref, *outs):
    sends = outs[:NY]
    dst_ref, hot_ref = outs[NY:]
    own = (hidden_ref[...].astype(F32) * gain_row(gain_ref[...])).astype(BF16)
    y_me = place_ref[1].astype(F32)
    z_me = place_ref[2].astype(F32)
    count = table_ref.shape[1]
    pair = pair_ref[...].astype(F32)
    table = to_column(table_ref[...].astype(F32), count)
    slot = jnp.sum(jnp.where(iota((count, TOK), 0) == pair, table, 0.0), axis=0, keepdims=True)
    owner = jnp.floor(slot * 0.5)
    local = slot - 2.0 * owner
    same = to_column(owner, TOK) == owner
    before = iota((TOK, TOK), 0) < iota((TOK, TOK), 1)
    pos = jnp.sum(jnp.where(same & before, 1.0, 0.0), axis=0, keepdims=True)
    y_to = jnp.floor(owner * (1.0 / NZ))
    dy = y_to - y_me
    dy = jnp.where(dy < 0, dy + NY, dy)
    dz = owner - NZ * y_to - z_me
    dz = jnp.where(dz < 0, dz + NZ, dz)
    rank = jnp.where(dz == 4, 7.0, jnp.where(dz < 4, 2.0 * dz, 15.0 - 2.0 * dz))
    over = pos >= CAP
    bucket = dy * BUCKETS + jnp.where(over, float(NZ), rank)
    place = jnp.where(over, pos - CAP, pos)
    dst = bucket * BLOCK + place
    dst_ref[...] = dst
    hot_ref[0] = jnp.max(jnp.where(over, rank, -1.0)).astype(jnp.int32)
    spot = jnp.where(iota((TOK, 128), 1) == to_column(place, TOK), 1.0, 0.0).astype(BF16)
    for part in range(NY):
        pick = jnp.where(iota((SLOTS, TOK), 0) + part * SLOTS == dst, 1.0, 0.0).astype(BF16)
        rows = jnp.dot(pick, own, preferred_element_type=F32).astype(BF16)
        sends[part][...] = rows.reshape(BUCKETS, BLOCK, COLS)
        marks = jnp.where(iota((16, TOK), 0) + part * BUCKETS == bucket, local, 0.0).astype(BF16)
        ids = jnp.dot(marks, spot, preferred_element_type=F32)
        for b in range(BUCKETS):
            head = rows[b * BLOCK : (b + 1) * BLOCK, :128].astype(F32)
            head = jnp.where(iota((BLOCK, 128), 0) == CAP, ids[b : b + 1], head)
            sends[part][b, :, pl.ds(0, 128)] = head.astype(BF16)


def dispatch(place, hidden, gain, pair, table):
    message = jax.ShapeDtypeStruct((BUCKETS, BLOCK, COLS), BF16)
    out = pl.pallas_call(
        dispatch_kernel,
        grid_spec=pltpu.PrefetchScalarGridSpec(
            num_scalar_prefetch=1,
            grid=(1,),
            in_specs=[
                pl.BlockSpec((TOK, COLS), lambda i, p: (0, p[0])),
                pl.BlockSpec((8, 128), lambda i, p: (p[0], 0)),
                pl.BlockSpec((1, TOK), lambda i, p: (0, 0)),
                pl.BlockSpec((1, table.shape[1]), lambda i, p: (0, 0)),
            ],
            out_specs=[pl.BlockSpec((BUCKETS, BLOCK, COLS), lambda i, p: (0, 0, 0))] * NY
            + [pl.BlockSpec((1, TOK), lambda i, p: (0, 0)), scalars()],
        ),
        out_shape=[message] * NY
        + [jax.ShapeDtypeStruct((1, TOK), F32), jax.ShapeDtypeStruct((1,), jnp.int32)],
        cost_estimate=pl.CostEstimate(
            flops=2 * NY * SLOTS * TOK * COLS, bytes_accessed=4_000_000, transcendentals=0
        ),
        name="dispatch",
    )(place, hidden, gain, pair, table)
    return out[:NY], out[NY], out[NY + 1]


def columns_kernel(row_ref, column_ref):
    column_ref[...] = jnp.broadcast_to(to_column(row_ref[...], TOK), (TOK, 128))


def columns(row):
    return pl.pallas_call(
        columns_kernel,
        in_specs=[whole()],
        out_specs=whole(),
        out_shape=jax.ShapeDtypeStruct((TOK, 128), F32),
        compiler_params=params(),
        cost_estimate=pl.CostEstimate(flops=1_000_000, bytes_accessed=300_000, transcendentals=0),
        name="columns",
    )(row)


def base_kernel(last, hidden_ref, gain_ref, mixed_ref, *refs):
    out_ref, square_ref, scaled_ref, weight_ref = refs[-4:]
    step = pl.program_id(0)
    gain = gain_row(gain_ref[...]).astype(BF16)
    rows = 64

    @pl.when(step == 0)
    def _():
        out_ref[...] = refs[0][...] if last else jnp.zeros_like(out_ref)
        square_ref[...] = refs[1][...] if last else jnp.zeros_like(square_ref)

    for r in range(0, TOK, rows):
        square = square_ref[r : r + rows, :]
        for c in range(0, hidden_ref.shape[1], 128):
            part = hidden_ref[r : r + rows, c : c + 128]
            scaled_ref[r : r + rows, c : c + 128] = part * gain[:, c : c + 128]
            wide = part.astype(F32)
            square = square + wide * wide
        square_ref[r : r + rows, :] = square
    row = lax.broadcasted_iota(jnp.int32, (256, 256), 0)
    source = 2 * (row % 128) + row // 128
    part_rows = jnp.where(
        lax.broadcasted_iota(jnp.int32, (256, 256), 1) == source, 1.0, 0.0
    ).astype(BF16)
    for b in range(0, mixed_ref.shape[0], 512):
        pair = jnp.concatenate([mixed_ref[b : b + 256], mixed_ref[b + 256 : b + 512]], axis=1)
        parted = jnp.dot(part_rows, pair, preferred_element_type=F32).astype(BF16)
        d = b // 2
        weight_ref[d : d + 128, :128] = parted[:128, :128]
        weight_ref[d : d + 128, 128:] = parted[128:, :128]
        weight_ref[d + 128 : d + 256, :128] = parted[:128, 128:]
        weight_ref[d + 128 : d + 256, 128:] = parted[128:, 128:]
    out_ref[...] += jnp.dot(scaled_ref[...], weight_ref[...], preferred_element_type=F32)

    if last:

        @pl.when(step == pl.num_programs(0) - 1)
        def _():
            mean = jnp.sum(square_ref[...], axis=1, keepdims=True) * (1.0 / DIM)
            inv = lax.rsqrt(mean + epsilon)
            out_ref[...] = out_ref[...] * inv
            square_ref[...] = jnp.broadcast_to(inv, (TOK, 128))


def base_projection(part, hidden, gain, weight, *begun):
    tile = 1024
    steps = DIM // tile // 2
    first = part * steps
    return pl.pallas_call(
        functools.partial(base_kernel, part == 1),
        grid=(steps,),
        in_specs=[
            pl.BlockSpec((TOK, tile), lambda k: (0, first + k)),
            pl.BlockSpec((8, 128), lambda k: (first + k, 0)),
            pl.BlockSpec((2 * tile, 128), lambda k: (first + k, 0)),
        ]
        + [
            pl.BlockSpec((TOK, 256), lambda k: (0, 0)),
            pl.BlockSpec((TOK, 128), lambda k: (0, 0)),
        ][: len(begun)],
        out_specs=[
            pl.BlockSpec((TOK, 256), lambda k: (0, 0)),
            pl.BlockSpec((TOK, 128), lambda k: (0, 0)),
        ],
        out_shape=[
            jax.ShapeDtypeStruct((TOK, 256), F32),
            jax.ShapeDtypeStruct((TOK, 128), F32),
        ],
        scratch_shapes=[pltpu.VMEM((TOK, tile), BF16), pltpu.VMEM((tile, 256), BF16)],
        cost_estimate=pl.CostEstimate(
            flops=TOK * DIM * 256, bytes_accessed=6_000_000, transcendentals=0
        ),
        name="base",
    )(hidden, gain, weight, *begun)


def local_column(head):
    row = head[CAP : CAP + 1, :].astype(F32)
    same = iota((BLOCK, 128), 0) == iota((BLOCK, 128), 1)
    return jnp.sum(jnp.where(same, row, 0.0), axis=1, keepdims=True)


def bucket_rows(received, b):
    rows = jnp.concatenate([r[b] for r in received], axis=0)
    local = jnp.concatenate([local_column(r[b, :, :128]) for r in received], axis=0)
    return rows, local


def project(rows, local, weight):
    both = jnp.dot(rows, weight, preferred_element_type=F32)
    return jnp.where(local < 0.5, both[:, :RANK2], both[:, RANK2:])


def down_early_kernel(hot_ref, *refs):
    received = refs[:NY]
    chunks = refs[NY:-2]
    low_ref, more_ref = refs[-2:]
    more_ref[...] = jnp.zeros_like(more_ref)
    for k in range(EARLY):
        weight = jnp.concatenate([chunks[2 * k][:COLS], chunks[2 * k + 1][:COLS]], axis=1)
        rows, local = bucket_rows(received, k)
        low_ref[k] = project(rows, local, weight).astype(BF16)

        @pl.when(hot_ref[0] == k)
        def _():
            rows, local = bucket_rows(received, NZ)
            more_ref[...] = project(rows, local, weight).astype(BF16)


def down_early(hot, received, chunks):
    return pl.pallas_call(
        down_early_kernel,
        in_specs=[scalars()] + [whole()] * (NY + len(chunks)),
        out_specs=[whole()] * 2,
        out_shape=[
            jax.ShapeDtypeStruct((EARLY, NY * BLOCK, RANK2), BF16),
            jax.ShapeDtypeStruct((NY * BLOCK, RANK2), BF16),
        ],
        compiler_params=params(),
        cost_estimate=pl.CostEstimate(
            flops=2 * EARLY * 128 * 1024 * 256, bytes_accessed=6_000_000, transcendentals=0
        ),
        name="down_early",
    )(hot, *received, *chunks)


def down_late_kernel(hot_ref, *refs):
    received = refs[:NY]
    chunks = refs[NY:-2]
    more_ref, low_ref = refs[-2:]
    low_ref[LATE - 1] = more_ref[...]
    for at in range(LATE - 1):
        weight = jnp.concatenate([chunks[2 * at][:COLS], chunks[2 * at + 1][:COLS]], axis=1)
        rows, local = bucket_rows(received, EARLY + at)
        low_ref[at] = project(rows, local, weight).astype(BF16)

        @pl.when(hot_ref[0] == EARLY + at)
        def _():
            rows, local = bucket_rows(received, NZ)
            low_ref[LATE - 1] = project(rows, local, weight).astype(BF16)


def down_late(hot, received, chunks, more):
    return pl.pallas_call(
        down_late_kernel,
        in_specs=[scalars()] + [whole()] * (NY + len(chunks) + 1),
        out_specs=whole(),
        out_shape=jax.ShapeDtypeStruct((LATE, NY * BLOCK, RANK2), BF16),
        compiler_params=params(),
        cost_estimate=pl.CostEstimate(
            flops=2 * 512 * 1024 * 256, bytes_accessed=2_000_000, transcendentals=0
        ),
        name="down_late",
    )(hot, *received, *chunks, more)


def spread(low, local):
    zero = jnp.zeros_like(low)
    return jnp.concatenate(
        [jnp.where(local < 0.5, low, zero), jnp.where(local < 0.5, zero, low)], axis=1
    ).astype(BF16)


def up_matrix(up):
    key_row = (lax.broadcasted_iota(jnp.int32, (2 * RANK2, 128), 0) % RANK2) < RANK2 // 2
    up = up.astype(F32)
    return jnp.concatenate(
        [jnp.where(key_row, up, 0.0), jnp.where(key_row, 0.0, up)], axis=1
    ).astype(BF16)


def up_rows(zero, one):
    return jnp.concatenate([zero[COLS:], one[COLS:]], axis=0)


def up_early_kernel(low_ref, *refs):
    received = refs[:NY]
    chunks = refs[NY:-NY]
    outs = refs[-NY:]
    for k in range(EARLY):
        local = jnp.concatenate([local_column(r[k, :, :128]) for r in received], axis=0)
        low = low_ref[k].astype(F32)
        delta = jnp.dot(
            spread(low, local), up_matrix(up_rows(chunks[2 * k], chunks[2 * k + 1])), preferred_element_type=F32
        ).astype(BF16)
        for s in range(NY):
            outs[s][k] = delta[s * BLOCK : (s + 1) * BLOCK]


def up_early(low, received, chunks):
    return pl.pallas_call(
        up_early_kernel,
        in_specs=[whole()] * (1 + NY + len(chunks)),
        out_specs=[whole()] * NY,
        out_shape=[jax.ShapeDtypeStruct((EARLY, BLOCK, 256), BF16)] * NY,
        compiler_params=params(),
        cost_estimate=pl.CostEstimate(
            flops=2 * EARLY * 128 * 256 * 256, bytes_accessed=1_500_000, transcendentals=0
        ),
        name="up_early",
    )(low, *received, *chunks)


def up_prepare_kernel(hot_ref, *refs):
    received = refs[:NY]
    chunks = refs[NY:-2]
    matrix_ref, mask_ref = refs[-2:]
    ups = [up_rows(chunks[2 * k], chunks[2 * k + 1]) for k in range(NZ - 1)]
    hot_up = ups[0].astype(F32)
    for k in range(1, NZ - 1):
        hot_up = jnp.where(hot_ref[0] == k, ups[k].astype(F32), hot_up)
    ones = jnp.ones((NY * BLOCK, RANK2), F32)
    for at in range(LATE - 2):
        matrix_ref[at] = up_matrix(ups[EARLY + at])
    matrix_ref[LATE - 2] = up_matrix(hot_up)
    for at in range(LATE):
        local = jnp.concatenate([local_column(r[EARLY + at, :, :128]) for r in received], axis=0)
        mask_ref[at] = spread(ones, local)


def up_prepare(hot, received, chunks):
    return pl.pallas_call(
        up_prepare_kernel,
        in_specs=[scalars()] + [whole()] * (NY + len(chunks)),
        out_specs=[whole()] * 2,
        out_shape=[
            jax.ShapeDtypeStruct((LATE - 1, 256, 256), BF16),
            jax.ShapeDtypeStruct((LATE, NY * BLOCK, 256), BF16),
        ],
        compiler_params=params(),
        cost_estimate=pl.CostEstimate(
            flops=4_000_000, bytes_accessed=1_500_000, transcendentals=0
        ),
        name="up_prepare",
    )(hot, *received, *chunks)


def up_late_kernel(hot_ref, low_ref, matrix_ref, mask_ref, zero_ref, one_ref, *outs):
    last = up_matrix(up_rows(zero_ref, one_ref))
    hot = jnp.where(
        hot_ref[0] == NZ - 1, last.astype(F32), matrix_ref[LATE - 2].astype(F32)
    ).astype(BF16)
    for at in range(LATE):
        low = low_ref[at]
        both = jnp.concatenate([low, low], axis=1) * mask_ref[at]
        matrix = matrix_ref[at] if at < LATE - 2 else (last if at == LATE - 2 else hot)
        delta = jnp.dot(both, matrix, preferred_element_type=F32).astype(BF16)
        for s in range(NY):
            outs[s][at] = delta[s * BLOCK : (s + 1) * BLOCK]


def up_late(hot, low, matrix, mask, last):
    return pl.pallas_call(
        up_late_kernel,
        in_specs=[scalars()] + [whole()] * 5,
        out_specs=[whole()] * NY,
        out_shape=[jax.ShapeDtypeStruct((LATE, BLOCK, 256), BF16)] * NY,
        compiler_params=params(),
        cost_estimate=pl.CostEstimate(
            flops=2 * 512 * 256 * 256, bytes_accessed=1_000_000, transcendentals=0
        ),
        name="up_late",
    )(hot, low, matrix, mask, *last)


def collect(dst, first, count, back):
    total = jnp.zeros((TOK, 256), F32)
    for part in range(NY):
        size = count * BLOCK
        at = iota((TOK, size), 1) + (part * SLOTS + first * BLOCK)
        pick = jnp.where(at == dst, 1.0, 0.0).astype(BF16)
        total = total + jnp.dot(
            pick, back[part][...].reshape(size, 256), preferred_element_type=F32
        )
    return total


def finish_early_kernel(base_ref, inv_ref, dst_ref, *refs):
    total = collect(dst_ref[:, :1], 0, EARLY, refs[:NY])
    refs[NY][...] = base_ref[...] + (adapter_scale * inv_ref[:, :1]) * total


def finish_late_kernel(sum_ref, inv_ref, dst_ref, *refs):
    total = collect(dst_ref[:, :1], EARLY, LATE, refs[:NY])
    refs[NY][...] = (sum_ref[...] + (adapter_scale * inv_ref[:, :1]) * total).astype(BF16)


def finish(kernel, start, inv, dst, back, kind):
    return pl.pallas_call(
        kernel,
        in_specs=[whole()] * (3 + NY),
        out_specs=whole(),
        out_shape=jax.ShapeDtypeStruct((TOK, 256), kind),
        compiler_params=params(),
        cost_estimate=pl.CostEstimate(
            flops=2 * TOK * 1024 * 256, bytes_accessed=1_500_000, transcendentals=0
        ),
    )(start, inv, dst, *back)


def shift(x, axis, size, by):
    return lax.ppermute(x, axis, [(i, (i + by) % size) for i in range(size)])


def pair_sum(x, axis, size, flip):
    other = lax.ppermute(x, axis, [(i, i ^ flip) for i in range(size)])
    return (x.astype(F32) + other.astype(F32)).astype(BF16)


def sum_over_tp(x):
    x = pair_sum(x, "core", 2, 1)
    x = pair_sum(x, "x", 4, 1)
    return pair_sum(x, "x", 4, 3)


def on_device(hidden, gain, kv_weight, down_weight, up_weight, pair_index, row_index):
    tp = lax.axis_index("x") * 2 + lax.axis_index("core")
    places = [tp, lax.axis_index("y"), lax.axis_index("z")]
    place = jnp.stack(places).astype(jnp.int32)

    own = pack(down_weight, up_weight.reshape(2, RANK2, 128))
    chunks = {0: own}
    plus = minus = own
    for k in range(1, 4):
        plus = [shift(plus[a], "z", NZ, 1) for a in range(2)]
        minus = [shift(minus[a], "z", NZ, -1) for a in range(2)]
        chunks[NZ - k] = plus
        chunks[k] = minus
    last = [shift(plus[0], "z", NZ, 1), shift(minus[1], "z", NZ, -1)]
    early = [a for dz in ORDER[:EARLY] for a in chunks[dz]]
    late = [a for dz in ORDER[EARLY:-1] for a in chunks[dz]] + last

    gains = gain.reshape(DIM // 128, 128)
    send, dst, hot = dispatch(
        place, hidden, gains, pair_index.reshape(1, TOK), row_index.reshape(1, -1)
    )
    dst = columns(dst)
    received = [send[0]] + [shift(send[dy], "y", NY, dy) for dy in range(1, NY)]

    mixed = kv_weight.reshape(2 * DIM, 128)
    base, inv = base_projection(0, hidden, gains, mixed)
    base, inv = base_projection(1, hidden, gains, mixed, base, inv)

    low, more = down_early(hot, received, early)
    low = sum_over_tp(low)
    delta = up_early(low, received, early)
    back = [delta[0]] + [shift(delta[dy], "y", NY, -dy) for dy in range(1, NY)]
    summed = finish(finish_early_kernel, base, inv, dst, back, F32)

    low = down_late(hot, received, late, more)
    matrix, mask = up_prepare(hot, received, early + late[:-2])
    low = sum_over_tp(low)
    delta = up_late(hot, low, matrix, mask, last)
    back = [delta[0]] + [shift(delta[dy], "y", NY, -dy) for dy in range(1, NY)]
    out = finish(finish_late_kernel, summed, inv, dst, back, BF16)
    return out.reshape(TOK, 2, 128)


def solution(mesh):
    split = Mesh(mesh.devices.reshape(4, 2, NY, NZ), ("x", "core", "y", "z"))
    tp = ("x", "core")
    ad = ("y", "z")
    return jax.shard_map(
        on_device,
        mesh=split,
        in_specs=(
            P(ad, None),
            P(),
            P(None, None, tp),
            P(ad, tp, None),
            P(ad, None, None, tp),
            P(ad),
            P(),
        ),
        out_specs=P(ad, None, tp),
        check_vma=False,
    )
```

```python
import functools

import jax
import jax.numpy as jnp
from jax import lax
from jax.experimental import pallas as pl
from jax.experimental.pallas import tpu as pltpu
from jax.sharding import Mesh, PartitionSpec as P


epsilon = 1e-05
adapter_scale = 0.5
F32 = jnp.float32
BF16 = jnp.bfloat16

TOK = 448
DIM = 8192
COLS = 1024
CAP = 28
BLOCK = 32
NZ = 8
NY = 4
BUCKETS = NZ + 1
SLOTS = BUCKETS * BLOCK
EARLY = 5
LATE = BUCKETS - EARLY
ORDER = (0, 7, 1, 6, 2, 5, 3, 4)
RANK2 = 128
CHUNK = COLS + RANK2
VMEM_LIMIT = 20 * 1024 * 1024
WIDE_LIMIT = 58 * 1024 * 1024
PACK_LIMIT = 66_200_000


def iota(shape, axis):
    return lax.broadcasted_iota(jnp.int32, shape, axis).astype(F32)


def to_column(row, count):
    same = iota((count, count), 0) == iota((count, count), 1)
    return jnp.sum(jnp.where(same, row, 0.0), axis=1, keepdims=True)


def params():
    return pltpu.CompilerParams(vmem_limit_bytes=VMEM_LIMIT)


def whole():
    return pl.BlockSpec(memory_space=pltpu.VMEM)


def scalars():
    return pl.BlockSpec(memory_space=pltpu.SMEM)


def in_hbm():
    return pl.BlockSpec(memory_space=pltpu.HBM)


def pack_kernel(down_ref, up_ref, zero_ref, one_ref, sems):
    copies = []
    for a, out_ref in enumerate((zero_ref, one_ref)):
        for src, dst in (
            (down_ref.at[a], out_ref.at[pl.ds(0, COLS)]),
            (up_ref.at[a], out_ref.at[pl.ds(COLS, RANK2)]),
        ):
            copies.append(pltpu.make_async_copy(src, dst, sems.at[len(copies)]))
    for copy in copies:
        copy.start()
    for copy in copies:
        copy.wait()


def pack(down_weight, up_planes):
    return pl.pallas_call(
        pack_kernel,
        in_specs=[in_hbm()] * 2,
        out_specs=[whole()] * 2,
        out_shape=[jax.ShapeDtypeStruct((CHUNK, 128), BF16)] * 2,
        scratch_shapes=[pltpu.SemaphoreType.DMA((4,))],
        compiler_params=pltpu.CompilerParams(vmem_limit_bytes=PACK_LIMIT),
        cost_estimate=pl.CostEstimate(flops=0, bytes_accessed=1_200_000, transcendentals=0),
    )(down_weight, up_planes)


def gain_row(gain):
    wide = gain.astype(F32)
    return jnp.concatenate([wide[i : i + 1] for i in range(8)], axis=1)


def dispatch_kernel(place_ref, hidden_ref, gain_ref, pair_ref, table_ref, *outs):
    sends = outs[:NY]
    dst_ref, hot_ref = outs[NY:]
    own = (hidden_ref[...].astype(F32) * gain_row(gain_ref[...])).astype(BF16)
    y_me = place_ref[1].astype(F32)
    z_me = place_ref[2].astype(F32)
    count = table_ref.shape[1]
    pair = pair_ref[...].astype(F32)
    table = to_column(table_ref[...].astype(F32), count)
    slot = jnp.sum(jnp.where(iota((count, TOK), 0) == pair, table, 0.0), axis=0, keepdims=True)
    owner = jnp.floor(slot * 0.5)
    local = slot - 2.0 * owner
    same = to_column(owner, TOK) == owner
    before = iota((TOK, TOK), 0) < iota((TOK, TOK), 1)
    pos = jnp.sum(jnp.where(same & before, 1.0, 0.0), axis=0, keepdims=True)
    y_to = jnp.floor(owner * (1.0 / NZ))
    dy = y_to - y_me
    dy = jnp.where(dy < 0, dy + NY, dy)
    dz = owner - NZ * y_to - z_me
    dz = jnp.where(dz < 0, dz + NZ, dz)
    rank = jnp.where(dz == 4, 7.0, jnp.where(dz < 4, 2.0 * dz, 15.0 - 2.0 * dz))
    over = pos >= CAP
    bucket = dy * BUCKETS + jnp.where(over, float(NZ), rank)
    place = jnp.where(over, pos - CAP, pos)
    dst = bucket * BLOCK + place
    dst_ref[...] = dst
    hot_ref[0] = jnp.max(jnp.where(over, rank, -1.0)).astype(jnp.int32)
    spot = jnp.where(iota((TOK, 128), 1) == to_column(place, TOK), 1.0, 0.0).astype(BF16)
    for part in range(NY):
        pick = jnp.where(iota((SLOTS, TOK), 0) + part * SLOTS == dst, 1.0, 0.0).astype(BF16)
        rows = jnp.dot(pick, own, preferred_element_type=F32).astype(BF16)
        sends[part][...] = rows.reshape(BUCKETS, BLOCK, COLS)
        marks = jnp.where(iota((16, TOK), 0) + part * BUCKETS == bucket, local, 0.0).astype(BF16)
        ids = jnp.dot(marks, spot, preferred_element_type=F32)
        for b in range(BUCKETS):
            head = rows[b * BLOCK : (b + 1) * BLOCK, :128].astype(F32)
            head = jnp.where(iota((BLOCK, 128), 0) == CAP, ids[b : b + 1], head)
            sends[part][b, :, pl.ds(0, 128)] = head.astype(BF16)


def dispatch(place, hidden, gain, pair, table):
    message = jax.ShapeDtypeStruct((BUCKETS, BLOCK, COLS), BF16)
    out = pl.pallas_call(
        dispatch_kernel,
        grid_spec=pltpu.PrefetchScalarGridSpec(
            num_scalar_prefetch=1,
            grid=(1,),
            in_specs=[
                pl.BlockSpec((TOK, COLS), lambda i, p: (0, p[0])),
                pl.BlockSpec((8, 128), lambda i, p: (p[0], 0)),
                pl.BlockSpec((1, TOK), lambda i, p: (0, 0)),
                pl.BlockSpec((1, table.shape[1]), lambda i, p: (0, 0)),
            ],
            out_specs=[pl.BlockSpec((BUCKETS, BLOCK, COLS), lambda i, p: (0, 0, 0))] * NY
            + [pl.BlockSpec((1, TOK), lambda i, p: (0, 0)), scalars()],
        ),
        out_shape=[message] * NY
        + [jax.ShapeDtypeStruct((1, TOK), F32), jax.ShapeDtypeStruct((1,), jnp.int32)],
        compiler_params=pltpu.CompilerParams(vmem_limit_bytes=WIDE_LIMIT),
        cost_estimate=pl.CostEstimate(
            flops=2 * NY * SLOTS * TOK * COLS, bytes_accessed=4_000_000, transcendentals=0
        ),
    )(place, hidden, gain, pair, table)
    return out[:NY], out[NY], out[NY + 1]


def columns_kernel(row_ref, column_ref):
    column_ref[...] = jnp.broadcast_to(to_column(row_ref[...], TOK), (TOK, 128))


def columns(row):
    return pl.pallas_call(
        columns_kernel,
        in_specs=[whole()],
        out_specs=whole(),
        out_shape=jax.ShapeDtypeStruct((TOK, 128), F32),
        compiler_params=params(),
        cost_estimate=pl.CostEstimate(flops=1_000_000, bytes_accessed=300_000, transcendentals=0),
    )(row)


def base_kernel(part, hidden_ref, gain_ref, mixed_ref, *refs):
    out_ref, square_ref, scaled_ref, weight_ref = refs[-4:]
    rows, tile = 64, hidden_ref.shape[1]
    step = pl.program_id(0)

    @pl.when(step == 0)
    def _():
        out_ref[...] = refs[0][...] if part else jnp.zeros_like(out_ref)
        square_ref[...] = refs[1][...] if part else jnp.zeros_like(square_ref)

    gain = gain_row(gain_ref[...]).astype(BF16)
    for r in range(0, TOK, rows):
        square = square_ref[r : r + rows, :]
        for c in range(0, tile, 128):
            block = hidden_ref[r : r + rows, c : c + 128]
            scaled_ref[r : r + rows, c : c + 128] = block * gain[:, c : c + 128]
            wide = block.astype(F32)
            square = square + wide * wide
        square_ref[r : r + rows, :] = square
    row = lax.broadcasted_iota(jnp.int32, (256, 256), 0)
    source = 2 * (row % 128) + row // 128
    part_rows = jnp.where(
        lax.broadcasted_iota(jnp.int32, (256, 256), 1) == source, 1.0, 0.0
    ).astype(BF16)
    first = (part * pl.num_programs(0) + step) * (2 * tile)
    for b in range(0, 2 * tile, 512):
        at = pl.multiple_of(first + b, 512)
        pair = jnp.concatenate(
            [mixed_ref[pl.ds(at, 256), :], mixed_ref[pl.ds(at + 256, 256), :]], axis=1
        )
        parted = jnp.dot(part_rows, pair, preferred_element_type=F32).astype(BF16)
        d = b // 2
        weight_ref[d : d + 128, :128] = parted[:128, :128]
        weight_ref[d : d + 128, 128:] = parted[128:, :128]
        weight_ref[d + 128 : d + 256, :128] = parted[:128, 128:]
        weight_ref[d + 128 : d + 256, 128:] = parted[128:, 128:]
    out_ref[...] += jnp.dot(scaled_ref[...], weight_ref[...], preferred_element_type=F32)

    if part:

        @pl.when(step == pl.num_programs(0) - 1)
        def _():
            mean = jnp.sum(square_ref[...], axis=1, keepdims=True) * (1.0 / DIM)
            inv = lax.rsqrt(mean + epsilon)
            out_ref[...] = out_ref[...] * inv
            square_ref[...] = jnp.broadcast_to(inv, (TOK, 128))


def base_projection(part, hidden, gain, weight, *begun):
    tile = 1024
    steps = DIM // tile // 2
    first = part * steps
    return pl.pallas_call(
        functools.partial(base_kernel, part),
        grid=(steps,),
        in_specs=[
            pl.BlockSpec((TOK, tile), lambda k: (0, first + k)),
            pl.BlockSpec((8, 128), lambda k: (first + k, 0)),
            whole(),
        ]
        + [whole()] * len(begun),
        out_specs=[whole()] * 2,
        out_shape=[
            jax.ShapeDtypeStruct((TOK, 256), F32),
            jax.ShapeDtypeStruct((TOK, 128), F32),
        ],
        scratch_shapes=[pltpu.VMEM((TOK, tile), BF16), pltpu.VMEM((tile, 256), BF16)],
        compiler_params=pltpu.CompilerParams(vmem_limit_bytes=WIDE_LIMIT),
        cost_estimate=pl.CostEstimate(
            flops=TOK * DIM * 256, bytes_accessed=6_000_000, transcendentals=0
        ),
    )(hidden, gain, weight, *begun)


def local_column(head):
    row = head[CAP : CAP + 1, :].astype(F32)
    same = iota((BLOCK, 128), 0) == iota((BLOCK, 128), 1)
    return jnp.sum(jnp.where(same, row, 0.0), axis=1, keepdims=True)


def bucket_rows(received, b):
    rows = jnp.concatenate([r[b] for r in received], axis=0)
    local = jnp.concatenate([local_column(r[b, :, :128]) for r in received], axis=0)
    return rows, local


def project(rows, local, weight):
    both = jnp.dot(rows, weight, preferred_element_type=F32)
    return jnp.where(local < 0.5, both[:, :RANK2], both[:, RANK2:])


def down_early_kernel(hot_ref, *refs):
    received = refs[:NY]
    chunks = refs[NY:-2]
    low_ref, more_ref = refs[-2:]
    more_ref[...] = jnp.zeros_like(more_ref)
    for k in range(EARLY):
        weight = jnp.concatenate([chunks[2 * k][:COLS], chunks[2 * k + 1][:COLS]], axis=1)
        rows, local = bucket_rows(received, k)
        low_ref[k] = project(rows, local, weight).astype(BF16)

        @pl.when(hot_ref[0] == k)
        def _():
            rows, local = bucket_rows(received, NZ)
            more_ref[...] = project(rows, local, weight).astype(BF16)


def down_early(hot, received, chunks):
    return pl.pallas_call(
        down_early_kernel,
        in_specs=[scalars()] + [whole()] * (NY + len(chunks)),
        out_specs=[whole()] * 2,
        out_shape=[
            jax.ShapeDtypeStruct((EARLY, NY * BLOCK, RANK2), BF16),
            jax.ShapeDtypeStruct((NY * BLOCK, RANK2), BF16),
        ],
        compiler_params=params(),
        cost_estimate=pl.CostEstimate(
            flops=2 * EARLY * 128 * 1024 * 256, bytes_accessed=6_000_000, transcendentals=0
        ),
    )(hot, *received, *chunks)


def down_late_kernel(hot_ref, *refs):
    received = refs[:NY]
    chunks = refs[NY:-2]
    more_ref, low_ref = refs[-2:]
    low_ref[LATE - 1] = more_ref[...]
    for at in range(LATE - 1):
        weight = jnp.concatenate([chunks[2 * at][:COLS], chunks[2 * at + 1][:COLS]], axis=1)
        rows, local = bucket_rows(received, EARLY + at)
        low_ref[at] = project(rows, local, weight).astype(BF16)

        @pl.when(hot_ref[0] == EARLY + at)
        def _():
            rows, local = bucket_rows(received, NZ)
            low_ref[LATE - 1] = project(rows, local, weight).astype(BF16)


def down_late(hot, received, chunks, more):
    return pl.pallas_call(
        down_late_kernel,
        in_specs=[scalars()] + [whole()] * (NY + len(chunks) + 1),
        out_specs=whole(),
        out_shape=jax.ShapeDtypeStruct((LATE, NY * BLOCK, RANK2), BF16),
        compiler_params=params(),
        cost_estimate=pl.CostEstimate(
            flops=2 * 512 * 1024 * 256, bytes_accessed=2_000_000, transcendentals=0
        ),
    )(hot, *received, *chunks, more)


def spread(low, local):
    zero = jnp.zeros_like(low)
    return jnp.concatenate(
        [jnp.where(local < 0.5, low, zero), jnp.where(local < 0.5, zero, low)], axis=1
    ).astype(BF16)


def up_matrix(up):
    key_row = (lax.broadcasted_iota(jnp.int32, (2 * RANK2, 128), 0) % RANK2) < RANK2 // 2
    up = up.astype(F32)
    return jnp.concatenate(
        [jnp.where(key_row, up, 0.0), jnp.where(key_row, 0.0, up)], axis=1
    ).astype(BF16)


def up_rows(zero, one):
    return jnp.concatenate([zero[COLS:], one[COLS:]], axis=0)


def up_early_kernel(low_ref, *refs):
    received = refs[:NY]
    chunks = refs[NY:-NY]
    outs = refs[-NY:]
    for k in range(EARLY):
        local = jnp.concatenate([local_column(r[k, :, :128]) for r in received], axis=0)
        low = low_ref[k].astype(F32)
        delta = jnp.dot(
            spread(low, local), up_matrix(up_rows(chunks[2 * k], chunks[2 * k + 1])), preferred_element_type=F32
        ).astype(BF16)
        for s in range(NY):
            outs[s][k] = delta[s * BLOCK : (s + 1) * BLOCK]


def up_early(low, received, chunks):
    return pl.pallas_call(
        up_early_kernel,
        in_specs=[whole()] * (1 + NY + len(chunks)),
        out_specs=[whole()] * NY,
        out_shape=[jax.ShapeDtypeStruct((EARLY, BLOCK, 256), BF16)] * NY,
        compiler_params=params(),
        cost_estimate=pl.CostEstimate(
            flops=2 * EARLY * 128 * 256 * 256, bytes_accessed=1_500_000, transcendentals=0
        ),
    )(low, *received, *chunks)


def up_prepare_kernel(hot_ref, *refs):
    received = refs[:NY]
    chunks = refs[NY:-2]
    matrix_ref, mask_ref = refs[-2:]
    ups = [up_rows(chunks[2 * k], chunks[2 * k + 1]) for k in range(NZ - 1)]
    hot_up = ups[0].astype(F32)
    for k in range(1, NZ - 1):
        hot_up = jnp.where(hot_ref[0] == k, ups[k].astype(F32), hot_up)
    ones = jnp.ones((NY * BLOCK, RANK2), F32)
    for at in range(LATE - 2):
        matrix_ref[at] = up_matrix(ups[EARLY + at])
    matrix_ref[LATE - 2] = up_matrix(hot_up)
    for at in range(LATE):
        local = jnp.concatenate([local_column(r[EARLY + at, :, :128]) for r in received], axis=0)
        mask_ref[at] = spread(ones, local)


def up_prepare(hot, received, chunks):
    return pl.pallas_call(
        up_prepare_kernel,
        in_specs=[scalars()] + [whole()] * (NY + len(chunks)),
        out_specs=[whole()] * 2,
        out_shape=[
            jax.ShapeDtypeStruct((LATE - 1, 256, 256), BF16),
            jax.ShapeDtypeStruct((LATE, NY * BLOCK, 256), BF16),
        ],
        compiler_params=params(),
        cost_estimate=pl.CostEstimate(
            flops=4_000_000, bytes_accessed=1_500_000, transcendentals=0
        ),
    )(hot, *received, *chunks)


def up_late_kernel(hot_ref, low_ref, matrix_ref, mask_ref, zero_ref, one_ref, *outs):
    last = up_matrix(up_rows(zero_ref, one_ref))
    hot = jnp.where(
        hot_ref[0] == NZ - 1, last.astype(F32), matrix_ref[LATE - 2].astype(F32)
    ).astype(BF16)
    for at in range(LATE):
        low = low_ref[at]
        both = jnp.concatenate([low, low], axis=1) * mask_ref[at]
        matrix = matrix_ref[at] if at < LATE - 2 else (last if at == LATE - 2 else hot)
        delta = jnp.dot(both, matrix, preferred_element_type=F32).astype(BF16)
        for s in range(NY):
            outs[s][at] = delta[s * BLOCK : (s + 1) * BLOCK]


def up_late(hot, low, matrix, mask, last):
    return pl.pallas_call(
        up_late_kernel,
        in_specs=[scalars()] + [whole()] * 5,
        out_specs=[whole()] * NY,
        out_shape=[jax.ShapeDtypeStruct((LATE, BLOCK, 256), BF16)] * NY,
        compiler_params=params(),
        cost_estimate=pl.CostEstimate(
            flops=2 * 512 * 256 * 256, bytes_accessed=1_000_000, transcendentals=0
        ),
    )(hot, low, matrix, mask, *last)


def collect(dst, first, count, back):
    total = jnp.zeros((TOK, 256), F32)
    for part in range(NY):
        size = count * BLOCK
        at = iota((TOK, size), 1) + (part * SLOTS + first * BLOCK)
        pick = jnp.where(at == dst, 1.0, 0.0).astype(BF16)
        total = total + jnp.dot(
            pick, back[part][...].reshape(size, 256), preferred_element_type=F32
        )
    return total


def finish_early_kernel(base_ref, inv_ref, dst_ref, *refs):
    total = collect(dst_ref[:, :1], 0, EARLY, refs[:NY])
    refs[NY][...] = base_ref[...] + (adapter_scale * inv_ref[:, :1]) * total


def finish_late_kernel(sum_ref, inv_ref, dst_ref, *refs):
    total = collect(dst_ref[:, :1], EARLY, LATE, refs[:NY])
    refs[NY][...] = (sum_ref[...] + (adapter_scale * inv_ref[:, :1]) * total).astype(BF16)


def finish(kernel, start, inv, dst, back, kind):
    return pl.pallas_call(
        kernel,
        in_specs=[whole()] * (3 + NY),
        out_specs=whole(),
        out_shape=jax.ShapeDtypeStruct((TOK, 256), kind),
        compiler_params=params(),
        cost_estimate=pl.CostEstimate(
            flops=2 * TOK * 1024 * 256, bytes_accessed=1_500_000, transcendentals=0
        ),
    )(start, inv, dst, *back)


def shift(x, axis, size, by):
    return lax.ppermute(x, axis, [(i, (i + by) % size) for i in range(size)])


def pair_sum(x, axis, size, flip):
    other = lax.ppermute(x, axis, [(i, i ^ flip) for i in range(size)])
    return (x.astype(F32) + other.astype(F32)).astype(BF16)


def sum_over_tp(x):
    x = pair_sum(x, "core", 2, 1)
    x = pair_sum(x, "x", 4, 1)
    return pair_sum(x, "x", 4, 3)


def on_device(hidden, gain, kv_weight, down_weight, up_weight, pair_index, row_index):
    tp = lax.axis_index("x") * 2 + lax.axis_index("core")
    places = [tp, lax.axis_index("y"), lax.axis_index("z")]
    place = jnp.stack(places).astype(jnp.int32)

    own = pack(down_weight, up_weight.reshape(2, RANK2, 128))
    chunks = {0: own}
    plus = minus = own
    for k in range(1, 4):
        plus = [shift(plus[a], "z", NZ, 1) for a in range(2)]
        minus = [shift(minus[a], "z", NZ, -1) for a in range(2)]
        chunks[NZ - k] = plus
        chunks[k] = minus
    last = [shift(plus[0], "z", NZ, 1), shift(minus[1], "z", NZ, -1)]
    early = [a for dz in ORDER[:EARLY] for a in chunks[dz]]
    late = [a for dz in ORDER[EARLY:-1] for a in chunks[dz]] + last

    gains = gain.reshape(DIM // 128, 128)
    send, dst, hot = dispatch(
        place, hidden, gains, pair_index.reshape(1, TOK), row_index.reshape(1, -1)
    )
    dst = columns(dst)
    received = [send[0]] + [shift(send[dy], "y", NY, dy) for dy in range(1, NY)]

    mixed = kv_weight.reshape(2 * DIM, 128)
    base, inv = base_projection(0, hidden, gains, mixed)
    base, inv = base_projection(1, hidden, gains, mixed, base, inv)

    low, more = down_early(hot, received, early)
    low = sum_over_tp(low)
    delta = up_early(low, received, early)
    back = [delta[0]] + [shift(delta[dy], "y", NY, -dy) for dy in range(1, NY)]
    summed = finish(finish_early_kernel, base, inv, dst, back, F32)

    low = down_late(hot, received, late, more)
    matrix, mask = up_prepare(hot, received, early + late[:-2])
    low = sum_over_tp(low)
    delta = up_late(hot, low, matrix, mask, last)
    back = [delta[0]] + [shift(delta[dy], "y", NY, -dy) for dy in range(1, NY)]
    out = finish(finish_late_kernel, summed, inv, dst, back, BF16)
    return out.reshape(TOK, 2, 128)


def solution(mesh):
    split = Mesh(mesh.devices.reshape(4, 2, NY, NZ), ("x", "core", "y", "z"))
    tp = ("x", "core")
    ad = ("y", "z")
    return jax.shard_map(
        on_device,
        mesh=split,
        in_specs=(
            P(ad, None),
            P(),
            P(None, None, tp),
            P(ad, tp, None),
            P(ad, None, None, tp),
            P(ad),
            P(),
        ),
        out_specs=P(ad, None, tp),
        check_vma=False,
    )
```

```python
import functools

import jax
import jax.numpy as jnp
from jax import lax
from jax.experimental import pallas as pl
from jax.experimental.pallas import tpu as pltpu
from jax.sharding import Mesh, PartitionSpec as P


epsilon = 1e-05
adapter_scale = 0.5
F32 = jnp.float32
BF16 = jnp.bfloat16

TOK = 448
DIM = 8192
COLS = 1024
CAP = 28
BLOCK = 32
NZ = 8
NY = 4
BUCKETS = NZ + 1
SLOTS = BUCKETS * BLOCK
EARLY = 5
LATE = BUCKETS - EARLY
ORDER = (0, 7, 1, 6, 2, 5, 3, 4)
RANK2 = 128
CHUNK = COLS + RANK2
VMEM_LIMIT = 20 * 1024 * 1024
PACK_LIMIT = 66_200_000


def iota(shape, axis):
    return lax.broadcasted_iota(jnp.int32, shape, axis).astype(F32)


def to_column(row, count):
    same = iota((count, count), 0) == iota((count, count), 1)
    return jnp.sum(jnp.where(same, row, 0.0), axis=1, keepdims=True)


def params():
    return pltpu.CompilerParams(vmem_limit_bytes=VMEM_LIMIT)


def whole():
    return pl.BlockSpec(memory_space=pltpu.VMEM)


def scalars():
    return pl.BlockSpec(memory_space=pltpu.SMEM)


def in_hbm():
    return pl.BlockSpec(memory_space=pltpu.HBM)


def pack_kernel(down_ref, up_ref, zero_ref, one_ref, sems):
    copies = []
    for a, out_ref in enumerate((zero_ref, one_ref)):
        for src, dst in (
            (down_ref.at[a], out_ref.at[pl.ds(0, COLS)]),
            (up_ref.at[a], out_ref.at[pl.ds(COLS, RANK2)]),
        ):
            copies.append(pltpu.make_async_copy(src, dst, sems.at[len(copies)]))
    for copy in copies:
        copy.start()
    for copy in copies:
        copy.wait()


def pack(down_weight, up_planes):
    return pl.pallas_call(
        pack_kernel,
        in_specs=[in_hbm()] * 2,
        out_specs=[whole()] * 2,
        out_shape=[jax.ShapeDtypeStruct((CHUNK, 128), BF16)] * 2,
        scratch_shapes=[pltpu.SemaphoreType.DMA((4,))],
        compiler_params=pltpu.CompilerParams(vmem_limit_bytes=PACK_LIMIT),
        cost_estimate=pl.CostEstimate(flops=0, bytes_accessed=1_200_000, transcendentals=0),
    )(down_weight, up_planes)


def gain_row(gain):
    wide = gain.astype(F32)
    return jnp.concatenate([wide[i : i + 1] for i in range(gain.shape[0])], axis=1)


def dispatch_kernel(place_ref, hidden_ref, gain_ref, pair_ref, table_ref, *outs):
    sends = outs[:NY]
    dst_ref, hot_ref, stage_ref, sems = outs[NY:]
    own = (hidden_ref[...].astype(F32) * gain_row(gain_ref[...])).astype(BF16)
    y_me = place_ref[1].astype(F32)
    z_me = place_ref[2].astype(F32)
    count = table_ref.shape[1]
    pair = pair_ref[...].astype(F32)
    table = to_column(table_ref[...].astype(F32), count)
    slot = jnp.sum(jnp.where(iota((count, TOK), 0) == pair, table, 0.0), axis=0, keepdims=True)
    owner = jnp.floor(slot * 0.5)
    local = slot - 2.0 * owner
    same = to_column(owner, TOK) == owner
    before = iota((TOK, TOK), 0) < iota((TOK, TOK), 1)
    pos = jnp.sum(jnp.where(same & before, 1.0, 0.0), axis=0, keepdims=True)
    y_to = jnp.floor(owner * (1.0 / NZ))
    dy = y_to - y_me
    dy = jnp.where(dy < 0, dy + NY, dy)
    dz = owner - NZ * y_to - z_me
    dz = jnp.where(dz < 0, dz + NZ, dz)
    rank = jnp.where(dz == 4, 7.0, jnp.where(dz < 4, 2.0 * dz, 15.0 - 2.0 * dz))
    over = pos >= CAP
    bucket = dy * BUCKETS + jnp.where(over, float(NZ), rank)
    place = jnp.where(over, pos - CAP, pos)
    dst = bucket * BLOCK + place
    dst_ref[...] = dst
    hot_ref[0] = jnp.max(jnp.where(over, rank, -1.0)).astype(jnp.int32)
    spot = jnp.where(iota((TOK, 128), 1) == to_column(place, TOK), 1.0, 0.0).astype(BF16)
    copies = []
    for part in (2, 1, 3, 0):
        pick = jnp.where(iota((SLOTS, TOK), 0) + part * SLOTS == dst, 1.0, 0.0).astype(BF16)
        rows = jnp.dot(pick, own, preferred_element_type=F32).astype(BF16)
        stage_ref[part] = rows.reshape(BUCKETS, BLOCK, COLS)
        marks = jnp.where(iota((16, TOK), 0) + part * BUCKETS == bucket, local, 0.0).astype(BF16)
        ids = jnp.dot(marks, spot, preferred_element_type=F32)
        for b in range(BUCKETS):
            head = rows[b * BLOCK : (b + 1) * BLOCK, :128].astype(F32)
            head = jnp.where(iota((BLOCK, 128), 0) == CAP, ids[b : b + 1], head)
            stage_ref[part, b, :, pl.ds(0, 128)] = head.astype(BF16)
        copy = pltpu.make_async_copy(stage_ref.at[part], sends[part], sems.at[part])
        copy.start()
        copies.append(copy)
    for copy in copies:
        copy.wait()


def dispatch(place, hidden, gain, pair, table):
    message = jax.ShapeDtypeStruct((BUCKETS, BLOCK, COLS), BF16)
    out = pl.pallas_call(
        dispatch_kernel,
        grid_spec=pltpu.PrefetchScalarGridSpec(
            num_scalar_prefetch=1,
            grid=(1,),
            in_specs=[
                pl.BlockSpec((TOK, COLS), lambda i, p: (0, p[0])),
                pl.BlockSpec((8, 128), lambda i, p: (p[0], 0)),
                pl.BlockSpec((1, TOK), lambda i, p: (0, 0)),
                pl.BlockSpec((1, table.shape[1]), lambda i, p: (0, 0)),
            ],
            out_specs=[pl.BlockSpec(memory_space=pl.ANY)] * NY
            + [pl.BlockSpec((1, TOK), lambda i, p: (0, 0)), scalars()],
            scratch_shapes=[
                pltpu.VMEM((NY, BUCKETS, BLOCK, COLS), BF16),
                pltpu.SemaphoreType.DMA((NY,)),
            ],
        ),
        out_shape=[message] * NY
        + [jax.ShapeDtypeStruct((1, TOK), F32), jax.ShapeDtypeStruct((1,), jnp.int32)],
        cost_estimate=pl.CostEstimate(
            flops=2 * NY * SLOTS * TOK * COLS, bytes_accessed=4_000_000, transcendentals=0
        ),
    )(place, hidden, gain, pair, table)
    return out[:NY], out[NY], out[NY + 1]


def columns_kernel(row_ref, column_ref):
    column_ref[...] = jnp.broadcast_to(to_column(row_ref[...], TOK), (TOK, 128))


def columns(row):
    return pl.pallas_call(
        columns_kernel,
        in_specs=[whole()],
        out_specs=whole(),
        out_shape=jax.ShapeDtypeStruct((TOK, 128), F32),
        compiler_params=params(),
        cost_estimate=pl.CostEstimate(flops=1_000_000, bytes_accessed=300_000, transcendentals=0),
    )(row)


def base_kernel(part, hidden_ref, gain_ref, mixed_ref, *refs):
    out_ref, square_ref, scaled_ref, weight_ref = refs[-4:]
    rows, tile = 64, hidden_ref.shape[1]
    step = pl.program_id(0)

    @pl.when(step == 0)
    def _():
        out_ref[...] = refs[0][...] if part else jnp.zeros_like(out_ref)
        square_ref[...] = refs[1][...] if part else jnp.zeros_like(square_ref)

    gain = gain_row(gain_ref[...]).astype(BF16)
    for r in range(0, TOK, rows):
        square = square_ref[r : r + rows, :]
        for c in range(0, tile, 128):
            block = hidden_ref[r : r + rows, c : c + 128]
            scaled_ref[r : r + rows, c : c + 128] = block * gain[:, c : c + 128]
            wide = block.astype(F32)
            square = square + wide * wide
        square_ref[r : r + rows, :] = square
    row = lax.broadcasted_iota(jnp.int32, (256, 256), 0)
    source = 2 * (row % 128) + row // 128
    part_rows = jnp.where(
        lax.broadcasted_iota(jnp.int32, (256, 256), 1) == source, 1.0, 0.0
    ).astype(BF16)
    for b in range(0, 2 * tile, 512):
        pair = jnp.concatenate(
            [mixed_ref[b : b + 256], mixed_ref[b + 256 : b + 512]], axis=1
        )
        parted = jnp.dot(part_rows, pair, preferred_element_type=F32).astype(BF16)
        d = b // 2
        weight_ref[d : d + 128, :128] = parted[:128, :128]
        weight_ref[d : d + 128, 128:] = parted[128:, :128]
        weight_ref[d + 128 : d + 256, :128] = parted[:128, 128:]
        weight_ref[d + 128 : d + 256, 128:] = parted[128:, 128:]
    out_ref[...] += jnp.dot(scaled_ref[...], weight_ref[...], preferred_element_type=F32)

    if part:

        @pl.when(step == pl.num_programs(0) - 1)
        def _():
            mean = jnp.sum(square_ref[...], axis=1, keepdims=True) * (1.0 / DIM)
            inv = lax.rsqrt(mean + epsilon)
            out_ref[...] = out_ref[...] * inv
            square_ref[...] = jnp.broadcast_to(inv, (TOK, 128))


def base_projection(part, hidden, gain, weight, *begun):
    tile = 2048
    steps = DIM // tile // 2
    first = part * steps
    sums = [pl.BlockSpec((TOK, 256), lambda k: (0, 0)), pl.BlockSpec((TOK, 128), lambda k: (0, 0))]
    return pl.pallas_call(
        functools.partial(base_kernel, part),
        grid=(steps,),
        in_specs=[
            pl.BlockSpec((TOK, tile), lambda k: (0, first + k)),
            pl.BlockSpec((tile // 128, 128), lambda k: (first + k, 0)),
            pl.BlockSpec((2 * tile, 128), lambda k: (first + k, 0)),
        ]
        + sums[: len(begun)],
        out_specs=sums,
        out_shape=[
            jax.ShapeDtypeStruct((TOK, 256), F32),
            jax.ShapeDtypeStruct((TOK, 128), F32),
        ],
        scratch_shapes=[pltpu.VMEM((TOK, tile), BF16), pltpu.VMEM((tile, 256), BF16)],
        cost_estimate=pl.CostEstimate(
            flops=TOK * DIM * 256, bytes_accessed=6_000_000, transcendentals=0
        ),
    )(hidden, gain, weight, *begun)


def local_column(head):
    row = head[CAP : CAP + 1, :].astype(F32)
    same = iota((BLOCK, 128), 0) == iota((BLOCK, 128), 1)
    return jnp.sum(jnp.where(same, row, 0.0), axis=1, keepdims=True)


def bucket_rows(received, b):
    rows = jnp.concatenate([r[b] for r in received], axis=0)
    local = jnp.concatenate([local_column(r[b, :, :128]) for r in received], axis=0)
    return rows, local


def project(rows, local, weight):
    both = jnp.dot(rows, weight, preferred_element_type=F32)
    return jnp.where(local < 0.5, both[:, :RANK2], both[:, RANK2:])


def down_early_kernel(hot_ref, *refs):
    received = refs[:NY]
    chunks = refs[NY:-2]
    low_ref, more_ref = refs[-2:]
    more_ref[...] = jnp.zeros_like(more_ref)
    for k in range(EARLY):
        weight = jnp.concatenate([chunks[2 * k][:COLS], chunks[2 * k + 1][:COLS]], axis=1)
        rows, local = bucket_rows(received, k)
        low_ref[k] = project(rows, local, weight).astype(BF16)

        @pl.when(hot_ref[0] == k)
        def _():
            rows, local = bucket_rows(received, NZ)
            more_ref[...] = project(rows, local, weight).astype(BF16)


def down_early(hot, received, chunks):
    return pl.pallas_call(
        down_early_kernel,
        in_specs=[scalars()] + [whole()] * (NY + len(chunks)),
        out_specs=[whole()] * 2,
        out_shape=[
            jax.ShapeDtypeStruct((EARLY, NY * BLOCK, RANK2), BF16),
            jax.ShapeDtypeStruct((NY * BLOCK, RANK2), BF16),
        ],
        compiler_params=params(),
        cost_estimate=pl.CostEstimate(
            flops=2 * EARLY * 128 * 1024 * 256, bytes_accessed=6_000_000, transcendentals=0
        ),
    )(hot, *received, *chunks)


def down_late_kernel(hot_ref, *refs):
    received = refs[:NY]
    chunks = refs[NY:-2]
    more_ref, low_ref = refs[-2:]
    low_ref[LATE - 1] = more_ref[...]
    for at in range(LATE - 1):
        weight = jnp.concatenate([chunks[2 * at][:COLS], chunks[2 * at + 1][:COLS]], axis=1)
        rows, local = bucket_rows(received, EARLY + at)
        low_ref[at] = project(rows, local, weight).astype(BF16)

        @pl.when(hot_ref[0] == EARLY + at)
        def _():
            rows, local = bucket_rows(received, NZ)
            low_ref[LATE - 1] = project(rows, local, weight).astype(BF16)


def down_late(hot, received, chunks, more):
    return pl.pallas_call(
        down_late_kernel,
        in_specs=[scalars()] + [whole()] * (NY + len(chunks) + 1),
        out_specs=whole(),
        out_shape=jax.ShapeDtypeStruct((LATE, NY * BLOCK, RANK2), BF16),
        compiler_params=params(),
        cost_estimate=pl.CostEstimate(
            flops=2 * 512 * 1024 * 256, bytes_accessed=2_000_000, transcendentals=0
        ),
    )(hot, *received, *chunks, more)


def spread(low, local):
    zero = jnp.zeros_like(low)
    return jnp.concatenate(
        [jnp.where(local < 0.5, low, zero), jnp.where(local < 0.5, zero, low)], axis=1
    ).astype(BF16)


def up_matrix(up):
    key_row = (lax.broadcasted_iota(jnp.int32, (2 * RANK2, 128), 0) % RANK2) < RANK2 // 2
    up = up.astype(F32)
    return jnp.concatenate(
        [jnp.where(key_row, up, 0.0), jnp.where(key_row, 0.0, up)], axis=1
    ).astype(BF16)


def up_rows(zero, one):
    return jnp.concatenate([zero[COLS:], one[COLS:]], axis=0)


def up_early_kernel(low_ref, *refs):
    received = refs[:NY]
    chunks = refs[NY:-NY]
    outs = refs[-NY:]
    for k in range(EARLY):
        local = jnp.concatenate([local_column(r[k, :, :128]) for r in received], axis=0)
        low = low_ref[k].astype(F32)
        delta = jnp.dot(
            spread(low, local), up_matrix(up_rows(chunks[2 * k], chunks[2 * k + 1])), preferred_element_type=F32
        ).astype(BF16)
        for s in range(NY):
            outs[s][k] = delta[s * BLOCK : (s + 1) * BLOCK]


def up_early(low, received, chunks):
    return pl.pallas_call(
        up_early_kernel,
        in_specs=[whole()] * (1 + NY + len(chunks)),
        out_specs=[whole()] * NY,
        out_shape=[jax.ShapeDtypeStruct((EARLY, BLOCK, 256), BF16)] * NY,
        compiler_params=params(),
        cost_estimate=pl.CostEstimate(
            flops=2 * EARLY * 128 * 256 * 256, bytes_accessed=1_500_000, transcendentals=0
        ),
    )(low, *received, *chunks)


def up_prepare_kernel(hot_ref, *refs):
    received = refs[:NY]
    chunks = refs[NY:-2]
    matrix_ref, mask_ref = refs[-2:]
    ups = [up_rows(chunks[2 * k], chunks[2 * k + 1]) for k in range(NZ - 1)]
    hot_up = ups[0].astype(F32)
    for k in range(1, NZ - 1):
        hot_up = jnp.where(hot_ref[0] == k, ups[k].astype(F32), hot_up)
    ones = jnp.ones((NY * BLOCK, RANK2), F32)
    for at in range(LATE - 2):
        matrix_ref[at] = up_matrix(ups[EARLY + at])
    matrix_ref[LATE - 2] = up_matrix(hot_up)
    for at in range(LATE):
        local = jnp.concatenate([local_column(r[EARLY + at, :, :128]) for r in received], axis=0)
        mask_ref[at] = spread(ones, local)


def up_prepare(hot, received, chunks):
    return pl.pallas_call(
        up_prepare_kernel,
        in_specs=[scalars()] + [whole()] * (NY + len(chunks)),
        out_specs=[whole()] * 2,
        out_shape=[
            jax.ShapeDtypeStruct((LATE - 1, 256, 256), BF16),
            jax.ShapeDtypeStruct((LATE, NY * BLOCK, 256), BF16),
        ],
        compiler_params=params(),
        cost_estimate=pl.CostEstimate(
            flops=4_000_000, bytes_accessed=1_500_000, transcendentals=0
        ),
    )(hot, *received, *chunks)


def up_late_kernel(hot_ref, low_ref, matrix_ref, mask_ref, zero_ref, one_ref, *outs):
    last = up_matrix(up_rows(zero_ref, one_ref))
    hot = jnp.where(
        hot_ref[0] == NZ - 1, last.astype(F32), matrix_ref[LATE - 2].astype(F32)
    ).astype(BF16)
    for at in range(LATE):
        low = low_ref[at]
        both = jnp.concatenate([low, low], axis=1) * mask_ref[at]
        matrix = matrix_ref[at] if at < LATE - 2 else (last if at == LATE - 2 else hot)
        delta = jnp.dot(both, matrix, preferred_element_type=F32).astype(BF16)
        for s in range(NY):
            outs[s][at] = delta[s * BLOCK : (s + 1) * BLOCK]


def up_late(hot, low, matrix, mask, last):
    return pl.pallas_call(
        up_late_kernel,
        in_specs=[scalars()] + [whole()] * 5,
        out_specs=[whole()] * NY,
        out_shape=[jax.ShapeDtypeStruct((LATE, BLOCK, 256), BF16)] * NY,
        compiler_params=params(),
        cost_estimate=pl.CostEstimate(
            flops=2 * 512 * 256 * 256, bytes_accessed=1_000_000, transcendentals=0
        ),
    )(hot, low, matrix, mask, *last)


def collect(dst, first, count, back):
    total = jnp.zeros((TOK, 256), F32)
    for part in range(NY):
        size = count * BLOCK
        at = iota((TOK, size), 1) + (part * SLOTS + first * BLOCK)
        pick = jnp.where(at == dst, 1.0, 0.0).astype(BF16)
        total = total + jnp.dot(
            pick, back[part][...].reshape(size, 256), preferred_element_type=F32
        )
    return total


def finish_early_kernel(base_ref, inv_ref, dst_ref, *refs):
    total = collect(dst_ref[:, :1], 0, EARLY, refs[:NY])
    refs[NY][...] = base_ref[...] + (adapter_scale * inv_ref[:, :1]) * total


def finish_late_kernel(sum_ref, inv_ref, dst_ref, *refs):
    total = collect(dst_ref[:, :1], EARLY, LATE, refs[:NY])
    refs[NY][...] = (sum_ref[...] + (adapter_scale * inv_ref[:, :1]) * total).astype(BF16)


def finish(kernel, start, inv, dst, back, kind):
    return pl.pallas_call(
        kernel,
        in_specs=[whole()] * (3 + NY),
        out_specs=whole(),
        out_shape=jax.ShapeDtypeStruct((TOK, 256), kind),
        compiler_params=params(),
        cost_estimate=pl.CostEstimate(
            flops=2 * TOK * 1024 * 256, bytes_accessed=1_500_000, transcendentals=0
        ),
    )(start, inv, dst, *back)


def shift(x, axis, size, by):
    return lax.ppermute(x, axis, [(i, (i + by) % size) for i in range(size)])


def pair_sum(x, axis, size, flip):
    other = lax.ppermute(x, axis, [(i, i ^ flip) for i in range(size)])
    return (x.astype(F32) + other.astype(F32)).astype(BF16)


def sum_over_tp(x):
    x = pair_sum(x, "core", 2, 1)
    x = pair_sum(x, "x", 4, 1)
    return pair_sum(x, "x", 4, 3)


def on_device(hidden, gain, kv_weight, down_weight, up_weight, pair_index, row_index):
    tp = lax.axis_index("x") * 2 + lax.axis_index("core")
    places = [tp, lax.axis_index("y"), lax.axis_index("z")]
    place = jnp.stack(places).astype(jnp.int32)

    own = pack(down_weight, up_weight.reshape(2, RANK2, 128))
    chunks = {0: own}
    plus = minus = own
    for k in range(1, 4):
        plus = [shift(plus[a], "z", NZ, 1) for a in range(2)]
        minus = [shift(minus[a], "z", NZ, -1) for a in range(2)]
        chunks[NZ - k] = plus
        chunks[k] = minus
    last = [shift(plus[0], "z", NZ, 1), shift(minus[1], "z", NZ, -1)]
    early = [a for dz in ORDER[:EARLY] for a in chunks[dz]]
    late = [a for dz in ORDER[EARLY:-1] for a in chunks[dz]] + last

    gains = gain.reshape(DIM // 128, 128)
    send, dst, hot = dispatch(
        place, hidden, gains, pair_index.reshape(1, TOK), row_index.reshape(1, -1)
    )
    dst = columns(dst)
    received = [send[0]] + [shift(send[dy], "y", NY, dy) for dy in range(1, NY)]

    mixed = kv_weight.reshape(2 * DIM, 128)
    base, inv = base_projection(0, hidden, gains, mixed)
    base, inv = base_projection(1, hidden, gains, mixed, base, inv)

    low, more = down_early(hot, received, early)
    low = sum_over_tp(low)
    delta = up_early(low, received, early)
    back = [delta[0]] + [shift(delta[dy], "y", NY, -dy) for dy in range(1, NY)]
    summed = finish(finish_early_kernel, base, inv, dst, back, F32)

    low = down_late(hot, received, late, more)
    matrix, mask = up_prepare(hot, received, early + late[:-2])
    low = sum_over_tp(low)
    delta = up_late(hot, low, matrix, mask, last)
    back = [delta[0]] + [shift(delta[dy], "y", NY, -dy) for dy in range(1, NY)]
    out = finish(finish_late_kernel, summed, inv, dst, back, BF16)
    return out.reshape(TOK, 2, 128)


def solution(mesh):
    split = Mesh(mesh.devices.reshape(4, 2, NY, NZ), ("x", "core", "y", "z"))
    tp = ("x", "core")
    ad = ("y", "z")
    return jax.shard_map(
        on_device,
        mesh=split,
        in_specs=(
            P(ad, None),
            P(),
            P(None, None, tp),
            P(ad, tp, None),
            P(ad, None, None, tp),
            P(ad),
            P(),
        ),
        out_specs=P(ad, None, tp),
        check_vma=False,
    )
```

```python
import functools

import jax
import jax.numpy as jnp
from jax import lax
from jax.experimental import pallas as pl
from jax.experimental.pallas import tpu as pltpu
from jax.sharding import Mesh, PartitionSpec as P


epsilon = 1e-05
adapter_scale = 0.5
F32 = jnp.float32
BF16 = jnp.bfloat16

TOK = 448
DIM = 8192
COLS = 1024
CAP = 28
BLOCK = 32
NZ = 8
NY = 4
BUCKETS = NZ + 1
SLOTS = BUCKETS * BLOCK
EARLY = 5
LATE = BUCKETS - EARLY
ORDER = (0, 7, 1, 6, 2, 5, 3, 4)
RANK2 = 128
CHUNK = COLS + RANK2
VMEM_LIMIT = 20 * 1024 * 1024
WIDE_LIMIT = 58 * 1024 * 1024
PACK_LIMIT = 66_200_000


def iota(shape, axis):
    return lax.broadcasted_iota(jnp.int32, shape, axis).astype(F32)


def to_column(row, count):
    same = iota((count, count), 0) == iota((count, count), 1)
    return jnp.sum(jnp.where(same, row, 0.0), axis=1, keepdims=True)


def params():
    return pltpu.CompilerParams(vmem_limit_bytes=VMEM_LIMIT)


def whole():
    return pl.BlockSpec(memory_space=pltpu.VMEM)


def scalars():
    return pl.BlockSpec(memory_space=pltpu.SMEM)


def in_hbm():
    return pl.BlockSpec(memory_space=pltpu.HBM)


def pack_kernel(down_ref, up_ref, zero_ref, one_ref, sems):
    copies = []
    for a, out_ref in enumerate((zero_ref, one_ref)):
        for src, dst in (
            (down_ref.at[a], out_ref.at[pl.ds(0, COLS)]),
            (up_ref.at[a], out_ref.at[pl.ds(COLS, RANK2)]),
        ):
            copies.append(pltpu.make_async_copy(src, dst, sems.at[len(copies)]))
    for copy in copies:
        copy.start()
    for copy in copies:
        copy.wait()


def pack(down_weight, up_planes):
    return pl.pallas_call(
        pack_kernel,
        in_specs=[in_hbm()] * 2,
        out_specs=[whole()] * 2,
        out_shape=[jax.ShapeDtypeStruct((CHUNK, 128), BF16)] * 2,
        scratch_shapes=[pltpu.SemaphoreType.DMA((4,))],
        compiler_params=pltpu.CompilerParams(vmem_limit_bytes=PACK_LIMIT),
        cost_estimate=pl.CostEstimate(flops=0, bytes_accessed=1_200_000, transcendentals=0),
    )(down_weight, up_planes)


def gain_row(gain):
    wide = gain.astype(F32)
    return jnp.concatenate([wide[i : i + 1] for i in range(gain.shape[0])], axis=1)


def dispatch_kernel(place_ref, hidden_ref, gain_ref, pair_ref, table_ref, *outs):
    sends = outs[:NY]
    dst_ref, hot_ref = outs[NY:]
    own = (hidden_ref[...].astype(F32) * gain_row(gain_ref[...])).astype(BF16)
    y_me = place_ref[1].astype(F32)
    z_me = place_ref[2].astype(F32)
    count = table_ref.shape[1]
    pair = pair_ref[...].astype(F32)
    table = to_column(table_ref[...].astype(F32), count)
    slot = jnp.sum(jnp.where(iota((count, TOK), 0) == pair, table, 0.0), axis=0, keepdims=True)
    owner = jnp.floor(slot * 0.5)
    local = slot - 2.0 * owner
    same = to_column(owner, TOK) == owner
    before = iota((TOK, TOK), 0) < iota((TOK, TOK), 1)
    pos = jnp.sum(jnp.where(same & before, 1.0, 0.0), axis=0, keepdims=True)
    y_to = jnp.floor(owner * (1.0 / NZ))
    dy = y_to - y_me
    dy = jnp.where(dy < 0, dy + NY, dy)
    dz = owner - NZ * y_to - z_me
    dz = jnp.where(dz < 0, dz + NZ, dz)
    rank = jnp.where(dz == 4, 7.0, jnp.where(dz < 4, 2.0 * dz, 15.0 - 2.0 * dz))
    over = pos >= CAP
    bucket = dy * BUCKETS + jnp.where(over, float(NZ), rank)
    place = jnp.where(over, pos - CAP, pos)
    dst = bucket * BLOCK + place
    dst_ref[...] = dst
    hot_ref[0] = jnp.max(jnp.where(over, rank, -1.0)).astype(jnp.int32)
    spot = jnp.where(iota((TOK, 128), 1) == to_column(place, TOK), 1.0, 0.0).astype(BF16)
    for part in range(NY):
        pick = jnp.where(iota((SLOTS, TOK), 0) + part * SLOTS == dst, 1.0, 0.0).astype(BF16)
        rows = jnp.dot(pick, own, preferred_element_type=F32).astype(BF16)
        sends[part][...] = rows.reshape(BUCKETS, BLOCK, COLS)
        marks = jnp.where(iota((16, TOK), 0) + part * BUCKETS == bucket, local, 0.0).astype(BF16)
        ids = jnp.dot(marks, spot, preferred_element_type=F32)
        for b in range(BUCKETS):
            head = rows[b * BLOCK : (b + 1) * BLOCK, :128].astype(F32)
            head = jnp.where(iota((BLOCK, 128), 0) == CAP, ids[b : b + 1], head)
            sends[part][b, :, pl.ds(0, 128)] = head.astype(BF16)


def dispatch(place, hidden, gain, pair, table):
    message = jax.ShapeDtypeStruct((BUCKETS, BLOCK, COLS), BF16)
    out = pl.pallas_call(
        dispatch_kernel,
        grid_spec=pltpu.PrefetchScalarGridSpec(
            num_scalar_prefetch=1,
            grid=(1,),
            in_specs=[
                pl.BlockSpec((TOK, COLS), lambda i, p: (0, p[0])),
                pl.BlockSpec((8, 128), lambda i, p: (p[0], 0)),
                pl.BlockSpec((1, TOK), lambda i, p: (0, 0)),
                pl.BlockSpec((1, table.shape[1]), lambda i, p: (0, 0)),
            ],
            out_specs=[pl.BlockSpec((BUCKETS, BLOCK, COLS), lambda i, p: (0, 0, 0))] * NY
            + [pl.BlockSpec((1, TOK), lambda i, p: (0, 0)), scalars()],
        ),
        out_shape=[message] * NY
        + [jax.ShapeDtypeStruct((1, TOK), F32), jax.ShapeDtypeStruct((1,), jnp.int32)],
        cost_estimate=pl.CostEstimate(
            flops=2 * NY * SLOTS * TOK * COLS, bytes_accessed=4_000_000, transcendentals=0
        ),
    )(place, hidden, gain, pair, table)
    return out[:NY], out[NY], out[NY + 1]


def columns_kernel(row_ref, column_ref):
    column_ref[...] = jnp.broadcast_to(to_column(row_ref[...], TOK), (TOK, 128))


def columns(row):
    return pl.pallas_call(
        columns_kernel,
        in_specs=[whole()],
        out_specs=whole(),
        out_shape=jax.ShapeDtypeStruct((TOK, 128), F32),
        compiler_params=params(),
        cost_estimate=pl.CostEstimate(flops=1_000_000, bytes_accessed=300_000, transcendentals=0),
    )(row)


def base_kernel(part, hidden_ref, gain_ref, mixed_ref, *refs):
    out_ref, square_ref, scaled_ref, weight_ref = refs[-4:]
    rows, tile = 64, hidden_ref.shape[1]
    step = pl.program_id(0)

    @pl.when(step == 0)
    def _():
        out_ref[...] = refs[0][...] if part else jnp.zeros_like(out_ref)
        square_ref[...] = refs[1][...] if part else jnp.zeros_like(square_ref)

    gain = gain_row(gain_ref[...]).astype(BF16)
    for r in range(0, TOK, rows):
        square = square_ref[r : r + rows, :]
        for c in range(0, tile, 128):
            block = hidden_ref[r : r + rows, c : c + 128]
            scaled_ref[r : r + rows, c : c + 128] = block * gain[:, c : c + 128]
            wide = block.astype(F32)
            square = square + wide * wide
        square_ref[r : r + rows, :] = square
    row = lax.broadcasted_iota(jnp.int32, (256, 256), 0)
    source = 2 * (row % 128) + row // 128
    part_rows = jnp.where(
        lax.broadcasted_iota(jnp.int32, (256, 256), 1) == source, 1.0, 0.0
    ).astype(BF16)
    for b in range(0, 2 * tile, 512):
        pair = jnp.concatenate(
            [mixed_ref[b : b + 256], mixed_ref[b + 256 : b + 512]], axis=1
        )
        parted = jnp.dot(part_rows, pair, preferred_element_type=F32).astype(BF16)
        d = b // 2
        weight_ref[d : d + 128, :128] = parted[:128, :128]
        weight_ref[d : d + 128, 128:] = parted[128:, :128]
        weight_ref[d + 128 : d + 256, :128] = parted[:128, 128:]
        weight_ref[d + 128 : d + 256, 128:] = parted[128:, 128:]
    out_ref[...] += jnp.dot(scaled_ref[...], weight_ref[...], preferred_element_type=F32)

    if part:

        @pl.when(step == pl.num_programs(0) - 1)
        def _():
            mean = jnp.sum(square_ref[...], axis=1, keepdims=True) * (1.0 / DIM)
            inv = lax.rsqrt(mean + epsilon)
            out_ref[...] = out_ref[...] * inv
            square_ref[...] = jnp.broadcast_to(inv, (TOK, 128))


def base_projection(part, hidden, gain, weight, *begun):
    tile = 2048
    steps = DIM // tile // 2
    first = part * steps
    sums = [pl.BlockSpec((TOK, 256), lambda k: (0, 0)), pl.BlockSpec((TOK, 128), lambda k: (0, 0))]
    return pl.pallas_call(
        functools.partial(base_kernel, part),
        grid=(steps,),
        in_specs=[
            pl.BlockSpec((TOK, tile), lambda k: (0, first + k)),
            pl.BlockSpec((tile // 128, 128), lambda k: (first + k, 0)),
            pl.BlockSpec((2 * tile, 128), lambda k: (first + k, 0)),
        ]
        + sums[: len(begun)],
        out_specs=sums,
        out_shape=[
            jax.ShapeDtypeStruct((TOK, 256), F32),
            jax.ShapeDtypeStruct((TOK, 128), F32),
        ],
        scratch_shapes=[pltpu.VMEM((TOK, tile), BF16), pltpu.VMEM((tile, 256), BF16)],
        compiler_params=pltpu.CompilerParams(vmem_limit_bytes=WIDE_LIMIT),
        cost_estimate=pl.CostEstimate(
            flops=TOK * DIM * 256, bytes_accessed=6_000_000, transcendentals=0
        ),
    )(hidden, gain, weight, *begun)


def local_column(head):
    row = head[CAP : CAP + 1, :].astype(F32)
    same = iota((BLOCK, 128), 0) == iota((BLOCK, 128), 1)
    return jnp.sum(jnp.where(same, row, 0.0), axis=1, keepdims=True)


def bucket_rows(received, b):
    rows = jnp.concatenate([r[b] for r in received], axis=0)
    local = jnp.concatenate([local_column(r[b, :, :128]) for r in received], axis=0)
    return rows, local


def project(rows, local, weight):
    both = jnp.dot(rows, weight, preferred_element_type=F32)
    return jnp.where(local < 0.5, both[:, :RANK2], both[:, RANK2:])


def down_early_kernel(hot_ref, *refs):
    received = refs[:NY]
    chunks = refs[NY:-2]
    low_ref, more_ref = refs[-2:]
    more_ref[...] = jnp.zeros_like(more_ref)
    for k in range(EARLY):
        weight = jnp.concatenate([chunks[2 * k][:COLS], chunks[2 * k + 1][:COLS]], axis=1)
        rows, local = bucket_rows(received, k)
        low_ref[k] = project(rows, local, weight).astype(BF16)

        @pl.when(hot_ref[0] == k)
        def _():
            rows, local = bucket_rows(received, NZ)
            more_ref[...] = project(rows, local, weight).astype(BF16)


def down_early(hot, received, chunks):
    return pl.pallas_call(
        down_early_kernel,
        in_specs=[scalars()] + [whole()] * (NY + len(chunks)),
        out_specs=[whole()] * 2,
        out_shape=[
            jax.ShapeDtypeStruct((EARLY, NY * BLOCK, RANK2), BF16),
            jax.ShapeDtypeStruct((NY * BLOCK, RANK2), BF16),
        ],
        compiler_params=params(),
        cost_estimate=pl.CostEstimate(
            flops=2 * EARLY * 128 * 1024 * 256, bytes_accessed=6_000_000, transcendentals=0
        ),
    )(hot, *received, *chunks)


def down_late_kernel(hot_ref, *refs):
    received = refs[:NY]
    chunks = refs[NY:-2]
    more_ref, low_ref = refs[-2:]
    low_ref[LATE - 1] = more_ref[...]
    for at in range(LATE - 1):
        weight = jnp.concatenate([chunks[2 * at][:COLS], chunks[2 * at + 1][:COLS]], axis=1)
        rows, local = bucket_rows(received, EARLY + at)
        low_ref[at] = project(rows, local, weight).astype(BF16)

        @pl.when(hot_ref[0] == EARLY + at)
        def _():
            rows, local = bucket_rows(received, NZ)
            low_ref[LATE - 1] = project(rows, local, weight).astype(BF16)


def down_late(hot, received, chunks, more):
    return pl.pallas_call(
        down_late_kernel,
        in_specs=[scalars()] + [whole()] * (NY + len(chunks) + 1),
        out_specs=whole(),
        out_shape=jax.ShapeDtypeStruct((LATE, NY * BLOCK, RANK2), BF16),
        compiler_params=params(),
        cost_estimate=pl.CostEstimate(
            flops=2 * 512 * 1024 * 256, bytes_accessed=2_000_000, transcendentals=0
        ),
    )(hot, *received, *chunks, more)


def spread(low, local):
    zero = jnp.zeros_like(low)
    return jnp.concatenate(
        [jnp.where(local < 0.5, low, zero), jnp.where(local < 0.5, zero, low)], axis=1
    ).astype(BF16)


def up_matrix(up):
    key_row = (lax.broadcasted_iota(jnp.int32, (2 * RANK2, 128), 0) % RANK2) < RANK2 // 2
    up = up.astype(F32)
    return jnp.concatenate(
        [jnp.where(key_row, up, 0.0), jnp.where(key_row, 0.0, up)], axis=1
    ).astype(BF16)


def up_rows(zero, one):
    return jnp.concatenate([zero[COLS:], one[COLS:]], axis=0)


def up_early_kernel(low_ref, *refs):
    received = refs[:NY]
    chunks = refs[NY:-NY]
    outs = refs[-NY:]
    for k in range(EARLY):
        local = jnp.concatenate([local_column(r[k, :, :128]) for r in received], axis=0)
        low = low_ref[k].astype(F32)
        delta = jnp.dot(
            spread(low, local), up_matrix(up_rows(chunks[2 * k], chunks[2 * k + 1])), preferred_element_type=F32
        ).astype(BF16)
        for s in range(NY):
            outs[s][k] = delta[s * BLOCK : (s + 1) * BLOCK]


def up_early(low, received, chunks):
    return pl.pallas_call(
        up_early_kernel,
        in_specs=[whole()] * (1 + NY + len(chunks)),
        out_specs=[whole()] * NY,
        out_shape=[jax.ShapeDtypeStruct((EARLY, BLOCK, 256), BF16)] * NY,
        compiler_params=params(),
        cost_estimate=pl.CostEstimate(
            flops=2 * EARLY * 128 * 256 * 256, bytes_accessed=1_500_000, transcendentals=0
        ),
    )(low, *received, *chunks)


def up_prepare_kernel(hot_ref, *refs):
    received = refs[:NY]
    chunks = refs[NY:-2]
    matrix_ref, mask_ref = refs[-2:]
    ups = [up_rows(chunks[2 * k], chunks[2 * k + 1]) for k in range(NZ - 1)]
    hot_up = ups[0].astype(F32)
    for k in range(1, NZ - 1):
        hot_up = jnp.where(hot_ref[0] == k, ups[k].astype(F32), hot_up)
    ones = jnp.ones((NY * BLOCK, RANK2), F32)
    for at in range(LATE - 2):
        matrix_ref[at] = up_matrix(ups[EARLY + at])
    matrix_ref[LATE - 2] = up_matrix(hot_up)
    for at in range(LATE):
        local = jnp.concatenate([local_column(r[EARLY + at, :, :128]) for r in received], axis=0)
        mask_ref[at] = spread(ones, local)


def up_prepare(hot, received, chunks):
    return pl.pallas_call(
        up_prepare_kernel,
        in_specs=[scalars()] + [whole()] * (NY + len(chunks)),
        out_specs=[whole()] * 2,
        out_shape=[
            jax.ShapeDtypeStruct((LATE - 1, 256, 256), BF16),
            jax.ShapeDtypeStruct((LATE, NY * BLOCK, 256), BF16),
        ],
        compiler_params=params(),
        cost_estimate=pl.CostEstimate(
            flops=4_000_000, bytes_accessed=1_500_000, transcendentals=0
        ),
    )(hot, *received, *chunks)


def up_late_kernel(hot_ref, low_ref, matrix_ref, mask_ref, zero_ref, one_ref, *outs):
    last = up_matrix(up_rows(zero_ref, one_ref))
    hot = jnp.where(
        hot_ref[0] == NZ - 1, last.astype(F32), matrix_ref[LATE - 2].astype(F32)
    ).astype(BF16)
    for at in range(LATE):
        low = low_ref[at]
        both = jnp.concatenate([low, low], axis=1) * mask_ref[at]
        matrix = matrix_ref[at] if at < LATE - 2 else (last if at == LATE - 2 else hot)
        delta = jnp.dot(both, matrix, preferred_element_type=F32).astype(BF16)
        for s in range(NY):
            outs[s][at] = delta[s * BLOCK : (s + 1) * BLOCK]


def up_late(hot, low, matrix, mask, last):
    return pl.pallas_call(
        up_late_kernel,
        in_specs=[scalars()] + [whole()] * 5,
        out_specs=[whole()] * NY,
        out_shape=[jax.ShapeDtypeStruct((LATE, BLOCK, 256), BF16)] * NY,
        compiler_params=params(),
        cost_estimate=pl.CostEstimate(
            flops=2 * 512 * 256 * 256, bytes_accessed=1_000_000, transcendentals=0
        ),
    )(hot, low, matrix, mask, *last)


def collect(dst, first, count, back):
    total = jnp.zeros((TOK, 256), F32)
    for part in range(NY):
        size = count * BLOCK
        at = iota((TOK, size), 1) + (part * SLOTS + first * BLOCK)
        pick = jnp.where(at == dst, 1.0, 0.0).astype(BF16)
        total = total + jnp.dot(
            pick, back[part][...].reshape(size, 256), preferred_element_type=F32
        )
    return total


def finish_early_kernel(base_ref, inv_ref, dst_ref, *refs):
    total = collect(dst_ref[:, :1], 0, EARLY, refs[:NY])
    refs[NY][...] = base_ref[...] + (adapter_scale * inv_ref[:, :1]) * total


def finish_late_kernel(sum_ref, inv_ref, dst_ref, *refs):
    total = collect(dst_ref[:, :1], EARLY, LATE, refs[:NY])
    refs[NY][...] = (sum_ref[...] + (adapter_scale * inv_ref[:, :1]) * total).astype(BF16)


def finish(kernel, start, inv, dst, back, kind):
    return pl.pallas_call(
        kernel,
        in_specs=[whole()] * (3 + NY),
        out_specs=whole(),
        out_shape=jax.ShapeDtypeStruct((TOK, 256), kind),
        compiler_params=params(),
        cost_estimate=pl.CostEstimate(
            flops=2 * TOK * 1024 * 256, bytes_accessed=1_500_000, transcendentals=0
        ),
    )(start, inv, dst, *back)


def shift(x, axis, size, by):
    return lax.ppermute(x, axis, [(i, (i + by) % size) for i in range(size)])


def pair_sum(x, axis, size, flip):
    other = lax.ppermute(x, axis, [(i, i ^ flip) for i in range(size)])
    return (x.astype(F32) + other.astype(F32)).astype(BF16)


def sum_over_tp(x):
    x = pair_sum(x, "core", 2, 1)
    x = pair_sum(x, "x", 4, 1)
    return pair_sum(x, "x", 4, 3)


def on_device(hidden, gain, kv_weight, down_weight, up_weight, pair_index, row_index):
    tp = lax.axis_index("x") * 2 + lax.axis_index("core")
    places = [tp, lax.axis_index("y"), lax.axis_index("z")]
    place = jnp.stack(places).astype(jnp.int32)

    own = pack(down_weight, up_weight.reshape(2, RANK2, 128))
    chunks = {0: own}
    plus = minus = own
    for k in range(1, 4):
        plus = [shift(plus[a], "z", NZ, 1) for a in range(2)]
        minus = [shift(minus[a], "z", NZ, -1) for a in range(2)]
        chunks[NZ - k] = plus
        chunks[k] = minus
    last = [shift(plus[0], "z", NZ, 1), shift(minus[1], "z", NZ, -1)]
    early = [a for dz in ORDER[:EARLY] for a in chunks[dz]]
    late = [a for dz in ORDER[EARLY:-1] for a in chunks[dz]] + last

    gains = gain.reshape(DIM // 128, 128)
    send, dst, hot = dispatch(
        place, hidden, gains, pair_index.reshape(1, TOK), row_index.reshape(1, -1)
    )
    dst = columns(dst)
    received = [send[0]] + [shift(send[dy], "y", NY, dy) for dy in range(1, NY)]

    mixed = kv_weight.reshape(2 * DIM, 128)
    base, inv = base_projection(0, hidden, gains, mixed)
    base, inv = base_projection(1, hidden, gains, mixed, base, inv)

    low, more = down_early(hot, received, early)
    low = sum_over_tp(low)
    delta = up_early(low, received, early)
    back = [delta[0]] + [shift(delta[dy], "y", NY, -dy) for dy in range(1, NY)]
    summed = finish(finish_early_kernel, base, inv, dst, back, F32)

    low = down_late(hot, received, late, more)
    matrix, mask = up_prepare(hot, received, early + late[:-2])
    low = sum_over_tp(low)
    delta = up_late(hot, low, matrix, mask, last)
    back = [delta[0]] + [shift(delta[dy], "y", NY, -dy) for dy in range(1, NY)]
    out = finish(finish_late_kernel, summed, inv, dst, back, BF16)
    return out.reshape(TOK, 2, 128)


def solution(mesh):
    split = Mesh(mesh.devices.reshape(4, 2, NY, NZ), ("x", "core", "y", "z"))
    tp = ("x", "core")
    ad = ("y", "z")
    return jax.shard_map(
        on_device,
        mesh=split,
        in_specs=(
            P(ad, None),
            P(),
            P(None, None, tp),
            P(ad, tp, None),
            P(ad, None, None, tp),
            P(ad),
            P(),
        ),
        out_specs=P(ad, None, tp),
        check_vma=False,
    )
```

```python
import functools

import jax
import jax.numpy as jnp
from jax import lax
from jax.experimental import pallas as pl
from jax.experimental.pallas import tpu as pltpu
from jax.sharding import Mesh, PartitionSpec as P


epsilon = 1e-05
adapter_scale = 0.5
F32 = jnp.float32
BF16 = jnp.bfloat16

TOK = 448
DIM = 8192
COLS = 1024
CAP = 28
BLOCK = 32
NZ = 8
NY = 4
BUCKETS = NZ + 1
SLOTS = BUCKETS * BLOCK
EARLY = 5
LATE = BUCKETS - EARLY
ORDER = (0, 7, 1, 6, 2, 5, 3, 4)
RANK2 = 128
CHUNK = COLS + RANK2
VMEM_LIMIT = 20 * 1024 * 1024
WIDE_LIMIT = 56 * 1024 * 1024
PACK_LIMIT = 66_200_000


def iota(shape, axis):
    return lax.broadcasted_iota(jnp.int32, shape, axis).astype(F32)


def to_column(row, count):
    same = iota((count, count), 0) == iota((count, count), 1)
    return jnp.sum(jnp.where(same, row, 0.0), axis=1, keepdims=True)


def params():
    return pltpu.CompilerParams(vmem_limit_bytes=VMEM_LIMIT)


def whole():
    return pl.BlockSpec(memory_space=pltpu.VMEM)


def scalars():
    return pl.BlockSpec(memory_space=pltpu.SMEM)


def in_hbm():
    return pl.BlockSpec(memory_space=pltpu.HBM)


def pack_kernel(down_ref, up_ref, zero_ref, one_ref, stage_ref, sems):
    moves = []
    half = COLS // 2
    for a, out_ref in enumerate((zero_ref, one_ref)):
        for src, first, size in (
            (down_ref.at[a, pl.ds(0, half)], 0, half),
            (down_ref.at[a, pl.ds(half, half)], half, half),
            (up_ref.at[a], COLS, RANK2),
        ):
            n = len(moves)
            stage = stage_ref.at[a, pl.ds(first, size)]
            moves.append(
                (
                    pltpu.make_async_copy(src, stage, sems.at[0, n]),
                    pltpu.make_async_copy(stage, out_ref.at[pl.ds(first, size)], sems.at[1, n]),
                )
            )
    for fetch, _ in moves:
        fetch.start()
    for fetch, store in moves:
        fetch.wait()
        store.start()
    for _, store in moves:
        store.wait()


def pack(down_weight, up_planes):
    return pl.pallas_call(
        pack_kernel,
        in_specs=[in_hbm()] * 2,
        out_specs=[in_hbm()] * 2,
        out_shape=[jax.ShapeDtypeStruct((CHUNK, 128), BF16)] * 2,
        scratch_shapes=[pltpu.VMEM((2, CHUNK, 128), BF16), pltpu.SemaphoreType.DMA((2, 6))],
        compiler_params=pltpu.CompilerParams(vmem_limit_bytes=PACK_LIMIT),
        cost_estimate=pl.CostEstimate(flops=0, bytes_accessed=1_200_000, transcendentals=0),
    )(down_weight, up_planes)


def gain_row(gain):
    wide = gain.astype(F32)
    return jnp.concatenate([wide[i : i + 1] for i in range(gain.shape[0])], axis=1)


def dispatch_kernel(place_ref, hidden_ref, gain_ref, pair_ref, table_ref, *outs):
    sends = outs[:NY]
    dst_ref, hot_ref = outs[NY:]
    own = (hidden_ref[...].astype(F32) * gain_row(gain_ref[...])).astype(BF16)
    y_me = place_ref[1].astype(F32)
    z_me = place_ref[2].astype(F32)
    count = table_ref.shape[1]
    pair = pair_ref[...].astype(F32)
    table = to_column(table_ref[...].astype(F32), count)
    slot = jnp.sum(jnp.where(iota((count, TOK), 0) == pair, table, 0.0), axis=0, keepdims=True)
    owner = jnp.floor(slot * 0.5)
    local = slot - 2.0 * owner
    same = to_column(owner, TOK) == owner
    before = iota((TOK, TOK), 0) < iota((TOK, TOK), 1)
    pos = jnp.sum(jnp.where(same & before, 1.0, 0.0), axis=0, keepdims=True)
    y_to = jnp.floor(owner * (1.0 / NZ))
    dy = y_to - y_me
    dy = jnp.where(dy < 0, dy + NY, dy)
    dz = owner - NZ * y_to - z_me
    dz = jnp.where(dz < 0, dz + NZ, dz)
    rank = jnp.where(dz == 4, 7.0, jnp.where(dz < 4, 2.0 * dz, 15.0 - 2.0 * dz))
    over = pos >= CAP
    bucket = dy * BUCKETS + jnp.where(over, float(NZ), rank)
    place = jnp.where(over, pos - CAP, pos)
    dst = bucket * BLOCK + place
    dst_ref[...] = dst
    hot_ref[0] = jnp.max(jnp.where(over, rank, -1.0)).astype(jnp.int32)
    spot = jnp.where(iota((TOK, 128), 1) == to_column(place, TOK), 1.0, 0.0).astype(BF16)
    for part in range(NY):
        pick = jnp.where(iota((SLOTS, TOK), 0) + part * SLOTS == dst, 1.0, 0.0).astype(BF16)
        rows = jnp.dot(pick, own, preferred_element_type=F32).astype(BF16)
        sends[part][...] = rows.reshape(BUCKETS, BLOCK, COLS)
        marks = jnp.where(iota((16, TOK), 0) + part * BUCKETS == bucket, local, 0.0).astype(BF16)
        ids = jnp.dot(marks, spot, preferred_element_type=F32)
        for b in range(BUCKETS):
            head = rows[b * BLOCK : (b + 1) * BLOCK, :128].astype(F32)
            head = jnp.where(iota((BLOCK, 128), 0) == CAP, ids[b : b + 1], head)
            sends[part][b, :, pl.ds(0, 128)] = head.astype(BF16)


def dispatch(place, hidden, gain, pair, table):
    message = jax.ShapeDtypeStruct((BUCKETS, BLOCK, COLS), BF16)
    out = pl.pallas_call(
        dispatch_kernel,
        grid_spec=pltpu.PrefetchScalarGridSpec(
            num_scalar_prefetch=1,
            grid=(1,),
            in_specs=[
                pl.BlockSpec((TOK, COLS), lambda i, p: (0, p[0])),
                pl.BlockSpec((8, 128), lambda i, p: (p[0], 0)),
                pl.BlockSpec((1, TOK), lambda i, p: (0, 0)),
                pl.BlockSpec((1, table.shape[1]), lambda i, p: (0, 0)),
            ],
            out_specs=[pl.BlockSpec((BUCKETS, BLOCK, COLS), lambda i, p: (0, 0, 0))] * NY
            + [pl.BlockSpec((1, TOK), lambda i, p: (0, 0)), scalars()],
        ),
        out_shape=[message] * NY
        + [jax.ShapeDtypeStruct((1, TOK), F32), jax.ShapeDtypeStruct((1,), jnp.int32)],
        cost_estimate=pl.CostEstimate(
            flops=2 * NY * SLOTS * TOK * COLS, bytes_accessed=4_000_000, transcendentals=0
        ),
    )(place, hidden, gain, pair, table)
    return out[:NY], out[NY], out[NY + 1]


def columns_kernel(row_ref, column_ref):
    column_ref[...] = jnp.broadcast_to(to_column(row_ref[...], TOK), (TOK, 128))


def columns(row):
    return pl.pallas_call(
        columns_kernel,
        in_specs=[whole()],
        out_specs=whole(),
        out_shape=jax.ShapeDtypeStruct((TOK, 128), F32),
        compiler_params=params(),
        cost_estimate=pl.CostEstimate(flops=1_000_000, bytes_accessed=300_000, transcendentals=0),
    )(row)


def base_kernel(part, hidden_ref, gain_ref, mixed_ref, *refs):
    out_ref, square_ref, scaled_ref, weight_ref = refs[-4:]
    rows, tile = 64, hidden_ref.shape[1]
    step = pl.program_id(0)

    @pl.when(step == 0)
    def _():
        out_ref[...] = refs[0][...] if part else jnp.zeros_like(out_ref)
        square_ref[...] = refs[1][...] if part else jnp.zeros_like(square_ref)

    gain = gain_row(gain_ref[...]).astype(BF16)
    for r in range(0, TOK, rows):
        square = square_ref[r : r + rows, :]
        for c in range(0, tile, 128):
            block = hidden_ref[r : r + rows, c : c + 128]
            scaled_ref[r : r + rows, c : c + 128] = block * gain[:, c : c + 128]
            wide = block.astype(F32)
            square = square + wide * wide
        square_ref[r : r + rows, :] = square
    row = lax.broadcasted_iota(jnp.int32, (256, 256), 0)
    source = 2 * (row % 128) + row // 128
    part_rows = jnp.where(
        lax.broadcasted_iota(jnp.int32, (256, 256), 1) == source, 1.0, 0.0
    ).astype(BF16)
    for b in range(0, 2 * tile, 512):
        pair = jnp.concatenate(
            [mixed_ref[b : b + 256], mixed_ref[b + 256 : b + 512]], axis=1
        )
        parted = jnp.dot(part_rows, pair, preferred_element_type=F32).astype(BF16)
        d = b // 2
        weight_ref[d : d + 128, :128] = parted[:128, :128]
        weight_ref[d : d + 128, 128:] = parted[128:, :128]
        weight_ref[d + 128 : d + 256, :128] = parted[:128, 128:]
        weight_ref[d + 128 : d + 256, 128:] = parted[128:, 128:]
    out_ref[...] += jnp.dot(scaled_ref[...], weight_ref[...], preferred_element_type=F32)

    if part:

        @pl.when(step == pl.num_programs(0) - 1)
        def _():
            mean = jnp.sum(square_ref[...], axis=1, keepdims=True) * (1.0 / DIM)
            inv = lax.rsqrt(mean + epsilon)
            out_ref[...] = out_ref[...] * inv
            square_ref[...] = jnp.broadcast_to(inv, (TOK, 128))


def base_projection(part, hidden, gain, weight, *begun):
    tile = 2048
    steps = DIM // tile // 2
    first = part * steps
    sums = [pl.BlockSpec((TOK, 256), lambda k: (0, 0)), pl.BlockSpec((TOK, 128), lambda k: (0, 0))]
    return pl.pallas_call(
        functools.partial(base_kernel, part),
        grid=(steps,),
        in_specs=[
            pl.BlockSpec((TOK, tile), lambda k: (0, first + k)),
            pl.BlockSpec((tile // 128, 128), lambda k: (first + k, 0)),
            pl.BlockSpec((2 * tile, 128), lambda k: (first + k, 0)),
        ]
        + sums[: len(begun)],
        out_specs=sums,
        out_shape=[
            jax.ShapeDtypeStruct((TOK, 256), F32),
            jax.ShapeDtypeStruct((TOK, 128), F32),
        ],
        scratch_shapes=[pltpu.VMEM((TOK, tile), BF16), pltpu.VMEM((tile, 256), BF16)],
        compiler_params=pltpu.CompilerParams(vmem_limit_bytes=WIDE_LIMIT),
        cost_estimate=pl.CostEstimate(
            flops=TOK * DIM * 256, bytes_accessed=6_000_000, transcendentals=0
        ),
    )(hidden, gain, weight, *begun)


def local_column(head):
    row = head[CAP : CAP + 1, :].astype(F32)
    same = iota((BLOCK, 128), 0) == iota((BLOCK, 128), 1)
    return jnp.sum(jnp.where(same, row, 0.0), axis=1, keepdims=True)


def bucket_rows(received, b):
    rows = jnp.concatenate([r[b] for r in received], axis=0)
    local = jnp.concatenate([local_column(r[b, :, :128]) for r in received], axis=0)
    return rows, local


def project(rows, local, weight):
    both = jnp.dot(rows, weight, preferred_element_type=F32)
    return jnp.where(local < 0.5, both[:, :RANK2], both[:, RANK2:])


def down_kernel(first, count, hot_ref, *refs):
    received = refs[:NY]
    chunks = refs[NY : NY + 2 * count]
    begun = refs[NY + 2 * count : -2]
    low_ref, more_ref = refs[-2:]
    more_ref[...] = begun[0][...] if begun else jnp.zeros_like(more_ref)
    for k in range(count):
        weight = jnp.concatenate([chunks[2 * k][:COLS], chunks[2 * k + 1][:COLS]], axis=1)
        rows, local = bucket_rows(received, first + k)
        low_ref[k] = project(rows, local, weight).astype(BF16)

        @pl.when(hot_ref[0] == first + k)
        def _():
            rows, local = bucket_rows(received, NZ)
            more_ref[...] = project(rows, local, weight).astype(BF16)


def down(first, hot, received, chunks, *begun):
    count = len(chunks) // 2
    return pl.pallas_call(
        functools.partial(down_kernel, first, count),
        in_specs=[scalars()] + [whole()] * (NY + len(chunks) + len(begun)),
        out_specs=[whole()] * 2,
        out_shape=[
            jax.ShapeDtypeStruct((count, NY * BLOCK, RANK2), BF16),
            jax.ShapeDtypeStruct((NY * BLOCK, RANK2), BF16),
        ],
        compiler_params=params(),
        cost_estimate=pl.CostEstimate(
            flops=2 * count * 128 * 1024 * 256, bytes_accessed=count * 1_000_000, transcendentals=0
        ),
    )(hot, *received, *chunks, *begun)


def down_last_kernel(hot_ref, *refs):
    received = refs[:NY]
    zero_ref, one_ref, before_ref, more_ref, low_ref = refs[NY:]
    low_ref[: LATE - 2] = before_ref[...]
    low_ref[LATE - 1] = more_ref[...]
    weight = jnp.concatenate([zero_ref[:COLS], one_ref[:COLS]], axis=1)
    rows, local = bucket_rows(received, NZ - 1)
    low_ref[LATE - 2] = project(rows, local, weight).astype(BF16)

    @pl.when(hot_ref[0] == NZ - 1)
    def _():
        rows, local = bucket_rows(received, NZ)
        low_ref[LATE - 1] = project(rows, local, weight).astype(BF16)


def down_last(hot, received, chunks, before, more):
    return pl.pallas_call(
        down_last_kernel,
        in_specs=[scalars()] + [whole()] * (NY + 4),
        out_specs=whole(),
        out_shape=jax.ShapeDtypeStruct((LATE, NY * BLOCK, RANK2), BF16),
        compiler_params=params(),
        cost_estimate=pl.CostEstimate(
            flops=2 * 256 * 1024 * 256, bytes_accessed=1_000_000, transcendentals=0
        ),
    )(hot, *received, *chunks, before, more)


def spread(low, local):
    zero = jnp.zeros_like(low)
    return jnp.concatenate(
        [jnp.where(local < 0.5, low, zero), jnp.where(local < 0.5, zero, low)], axis=1
    ).astype(BF16)


def up_matrix(up):
    key_row = (lax.broadcasted_iota(jnp.int32, (2 * RANK2, 128), 0) % RANK2) < RANK2 // 2
    up = up.astype(F32)
    return jnp.concatenate(
        [jnp.where(key_row, up, 0.0), jnp.where(key_row, 0.0, up)], axis=1
    ).astype(BF16)


def up_rows(zero, one):
    return jnp.concatenate([zero[COLS:], one[COLS:]], axis=0)


def up_early_kernel(low_ref, *refs):
    received = refs[:NY]
    chunks = refs[NY:-NY]
    outs = refs[-NY:]
    for k in range(EARLY):
        local = jnp.concatenate([local_column(r[k, :, :128]) for r in received], axis=0)
        low = low_ref[k].astype(F32)
        delta = jnp.dot(
            spread(low, local), up_matrix(up_rows(chunks[2 * k], chunks[2 * k + 1])), preferred_element_type=F32
        ).astype(BF16)
        for s in range(NY):
            outs[s][k] = delta[s * BLOCK : (s + 1) * BLOCK]


def up_early(low, received, chunks):
    return pl.pallas_call(
        up_early_kernel,
        in_specs=[whole()] * (1 + NY + len(chunks)),
        out_specs=[whole()] * NY,
        out_shape=[jax.ShapeDtypeStruct((EARLY, BLOCK, 256), BF16)] * NY,
        compiler_params=params(),
        cost_estimate=pl.CostEstimate(
            flops=2 * EARLY * 128 * 256 * 256, bytes_accessed=1_500_000, transcendentals=0
        ),
    )(low, *received, *chunks)


def up_prepare_kernel(hot_ref, *refs):
    received = refs[:NY]
    chunks = refs[NY:-2]
    matrix_ref, mask_ref = refs[-2:]
    ups = [up_rows(chunks[2 * k], chunks[2 * k + 1]) for k in range(NZ - 1)]
    hot_up = ups[0].astype(F32)
    for k in range(1, NZ - 1):
        hot_up = jnp.where(hot_ref[0] == k, ups[k].astype(F32), hot_up)
    ones = jnp.ones((NY * BLOCK, RANK2), F32)
    for at in range(LATE - 2):
        matrix_ref[at] = up_matrix(ups[EARLY + at])
    matrix_ref[LATE - 2] = up_matrix(hot_up)
    for at in range(LATE):
        local = jnp.concatenate([local_column(r[EARLY + at, :, :128]) for r in received], axis=0)
        mask_ref[at] = spread(ones, local)


def up_prepare(hot, received, chunks):
    return pl.pallas_call(
        up_prepare_kernel,
        in_specs=[scalars()] + [whole()] * (NY + len(chunks)),
        out_specs=[whole()] * 2,
        out_shape=[
            jax.ShapeDtypeStruct((LATE - 1, 256, 256), BF16),
            jax.ShapeDtypeStruct((LATE, NY * BLOCK, 256), BF16),
        ],
        compiler_params=params(),
        cost_estimate=pl.CostEstimate(
            flops=4_000_000, bytes_accessed=1_500_000, transcendentals=0
        ),
    )(hot, *received, *chunks)


def up_late_kernel(hot_ref, low_ref, matrix_ref, mask_ref, zero_ref, one_ref, *outs):
    last = up_matrix(up_rows(zero_ref, one_ref))
    hot = jnp.where(
        hot_ref[0] == NZ - 1, last.astype(F32), matrix_ref[LATE - 2].astype(F32)
    ).astype(BF16)
    for at in range(LATE):
        low = low_ref[at]
        both = jnp.concatenate([low, low], axis=1) * mask_ref[at]
        matrix = matrix_ref[at] if at < LATE - 2 else (last if at == LATE - 2 else hot)
        delta = jnp.dot(both, matrix, preferred_element_type=F32).astype(BF16)
        for s in range(NY):
            outs[s][at] = delta[s * BLOCK : (s + 1) * BLOCK]


def up_late(hot, low, matrix, mask, last):
    return pl.pallas_call(
        up_late_kernel,
        in_specs=[scalars()] + [whole()] * 5,
        out_specs=[whole()] * NY,
        out_shape=[jax.ShapeDtypeStruct((LATE, BLOCK, 256), BF16)] * NY,
        compiler_params=params(),
        cost_estimate=pl.CostEstimate(
            flops=2 * 512 * 256 * 256, bytes_accessed=1_000_000, transcendentals=0
        ),
    )(hot, low, matrix, mask, *last)


def collect(dst, first, count, back):
    total = jnp.zeros((TOK, 256), F32)
    for part in range(NY):
        size = count * BLOCK
        at = iota((TOK, size), 1) + (part * SLOTS + first * BLOCK)
        pick = jnp.where(at == dst, 1.0, 0.0).astype(BF16)
        total = total + jnp.dot(
            pick, back[part][...].reshape(size, 256), preferred_element_type=F32
        )
    return total


def finish_early_kernel(base_ref, inv_ref, dst_ref, *refs):
    total = collect(dst_ref[:, :1], 0, EARLY, refs[:NY])
    refs[NY][...] = base_ref[...] + (adapter_scale * inv_ref[:, :1]) * total


def finish_late_kernel(sum_ref, inv_ref, dst_ref, *refs):
    total = collect(dst_ref[:, :1], EARLY, LATE, refs[:NY])
    refs[NY][...] = (sum_ref[...] + (adapter_scale * inv_ref[:, :1]) * total).astype(BF16)


def finish(kernel, start, inv, dst, back, kind):
    return pl.pallas_call(
        kernel,
        in_specs=[whole()] * (3 + NY),
        out_specs=whole(),
        out_shape=jax.ShapeDtypeStruct((TOK, 256), kind),
        compiler_params=params(),
        cost_estimate=pl.CostEstimate(
            flops=2 * TOK * 1024 * 256, bytes_accessed=1_500_000, transcendentals=0
        ),
    )(start, inv, dst, *back)


def shift(x, axis, size, by):
    return lax.ppermute(x, axis, [(i, (i + by) % size) for i in range(size)])


def pair_sum(x, axis, size, flip):
    other = lax.ppermute(x, axis, [(i, i ^ flip) for i in range(size)])
    return (x.astype(F32) + other.astype(F32)).astype(BF16)


def sum_over_tp(x):
    x = pair_sum(x, "core", 2, 1)
    x = pair_sum(x, "x", 4, 1)
    return pair_sum(x, "x", 4, 3)


def on_device(hidden, gain, kv_weight, down_weight, up_weight, pair_index, row_index):
    tp = lax.axis_index("x") * 2 + lax.axis_index("core")
    places = [tp, lax.axis_index("y"), lax.axis_index("z")]
    place = jnp.stack(places).astype(jnp.int32)

    own = pack(down_weight, up_weight.reshape(2, RANK2, 128))
    chunks = {0: own}
    plus = minus = own
    for k in range(1, 4):
        plus = [shift(plus[a], "z", NZ, 1) for a in range(2)]
        minus = [shift(minus[a], "z", NZ, -1) for a in range(2)]
        chunks[NZ - k] = plus
        chunks[k] = minus
    last = [shift(plus[0], "z", NZ, 1), shift(minus[1], "z", NZ, -1)]
    early = [a for dz in ORDER[:EARLY] for a in chunks[dz]]
    late = [a for dz in ORDER[EARLY:-1] for a in chunks[dz]] + last

    gains = gain.reshape(DIM // 128, 128)
    send, dst, hot = dispatch(
        place, hidden, gains, pair_index.reshape(1, TOK), row_index.reshape(1, -1)
    )
    dst = columns(dst)
    received = [send[0]] + [shift(send[dy], "y", NY, dy) for dy in range(1, NY)]

    mixed = kv_weight.reshape(2 * DIM, 128)
    base, inv = base_projection(0, hidden, gains, mixed)
    base, inv = base_projection(1, hidden, gains, mixed, base, inv)

    low, more = down(0, hot, received, early)
    low = sum_over_tp(low)
    delta = up_early(low, received, early)
    back = [delta[0]] + [shift(delta[dy], "y", NY, -dy) for dy in range(1, NY)]
    summed = finish(finish_early_kernel, base, inv, dst, back, F32)

    before, more = down(EARLY, hot, received, late[:-2], more)
    low = down_last(hot, received, last, before, more)
    matrix, mask = up_prepare(hot, received, early + late[:-2])
    low = sum_over_tp(low)
    delta = up_late(hot, low, matrix, mask, last)
    back = [delta[0]] + [shift(delta[dy], "y", NY, -dy) for dy in range(1, NY)]
    out = finish(finish_late_kernel, summed, inv, dst, back, BF16)
    return out.reshape(TOK, 2, 128)


def solution(mesh):
    split = Mesh(mesh.devices.reshape(4, 2, NY, NZ), ("x", "core", "y", "z"))
    tp = ("x", "core")
    ad = ("y", "z")
    return jax.shard_map(
        on_device,
        mesh=split,
        in_specs=(
            P(ad, None),
            P(),
            P(None, None, tp),
            P(ad, tp, None),
            P(ad, None, None, tp),
            P(ad),
            P(),
        ),
        out_specs=P(ad, None, tp),
        check_vma=False,
    )
```
